32 devices in a mesh: wide: 8 (over y, x, core), narrow: 4 (over z).
Axes of the slice: x: 2, y: 2, z: 4, core: 2. Of those that a mesh axis runs over, the one named last changes fastest.
Arguments:
- long_tokens: bfloat16 [32, 512, 768], P(('wide', 'narrow')), may hold values from -6 to 6
- long_lengths: int32 [32], P(('wide', 'narrow')), may hold values from 129 to 512, as said below
- short_tokens: bfloat16 [64, 128, 768], P(('wide', 'narrow')), may hold values from -6 to 6
- short_lengths: int32 [64], P(('wide', 'narrow')), may hold values from 33 to 128, as said below
- w_qkv: bfloat16 [768, 1152], P('narrow'), may hold values from -0.21875 to 0.21875
- w_depth: bfloat16 [9, 768], P(None, 'narrow'), may hold values from -2 to 2
- w_point: bfloat16 [768, 384], P('narrow'), may hold values from -0.21875 to 0.21875
- w_kernel: bfloat16 [384, 54], P('narrow'), may hold values from -0.3125 to 0.3125
- w_convout: bfloat16 [768, 384], P('narrow'), may hold values from -0.21875 to 0.21875
- w_out: bfloat16 [768, 768], P('narrow'), may hold values from -0.875 to 0.875
- norm1_gain: bfloat16 [768], P('narrow'), may hold values from 0.5 to 1.5
- norm1_bias: bfloat16 [768], P('narrow'), may hold values from -1.796875 to 1.796875
- w_inner: bfloat16 [2, 384, 1536], P(None, 'narrow'), may hold values from -0.3125 to 0.3125
- w_outer: bfloat16 [2, 1536, 384], P(None, 'narrow'), may hold values from -0.15625 to 0.15625
- norm2_gain: bfloat16 [768], P('narrow'), may hold values from 0.5 to 1.5
- norm2_bias: bfloat16 [768], P('narrow'), may hold values from -1.796875 to 1.796875
- long_cotangent: bfloat16 [32, 512, 768], P(('wide', 'narrow')), may hold values from -6 to 6
- short_cotangent: bfloat16 [64, 128, 768], P(('wide', 'narrow')), may hold values from -6 to 6
Outputs:
- long_output: bfloat16 [32, 512, 768], P(('wide', 'narrow'))
- short_output: bfloat16 [64, 128, 768], P(('wide', 'narrow'))
- long_input_grad: bfloat16 [32, 512, 768], P(('wide', 'narrow'))
- short_input_grad: bfloat16 [64, 128, 768], P(('wide', 'narrow'))
- grad_qkv: float32 [768, 1152], P('narrow')
- grad_depth: float32 [9, 768], P(None, 'narrow')
- grad_point: float32 [768, 384], P('narrow')
- grad_kernel: float32 [384, 54], P('narrow')
- grad_convout: float32 [768, 384], P('narrow')
- grad_out: float32 [768, 768], P('narrow')
- grad_norm1_gain: float32 [768], P('narrow')
- grad_norm1_bias: float32 [768], P('narrow')
- grad_inner: float32 [2, 384, 1536], P(None, 'narrow')
- grad_outer: float32 [2, 1536, 384], P(None, 'narrow')
- grad_norm2_gain: float32 [768], P('narrow')
- grad_norm2_bias: float32 [768], P('narrow')
The draws below stay inside these ranges and needn't reach their ends.
Inputs may be any that keep to these rules, and one draw needn't show every extreme that they name: `long_lengths`: each long row holds this many live tokens from its start, the rest is padding; some row is full and some row has the fewest allowed. `short_lengths`: each short row holds this many live tokens from its start, the rest is padding; some row is full and some row has the fewest allowed.
All inputs are finite; a program needn't handle non-finite values.
Results may differ from the reference program's by a relative error of at most 0.017.
Values may be sent and summed in bfloat16 or wider, within the bound.
No kernel may reach another device: no remote copies, remote signals or barrier semaphores. Data moves between devices by JAX's collectives and lax.ppermute only.
A program may use at most 192 MiB of HBM per device.

```python
import math
import jax
import jax.numpy as jnp
from jax import lax

D = 768
HEADS = 6
HEAD = 64
KERNEL = 9
FF = 3072
GROUPS = 2
LONG_LEN = 512
SHORT_LEN = 128
AH = 384
NLONG = 32
NSHORT = 64


def bounded_lengths(key, amount, low_end, high_end):
    draw_key, spot_key = jax.random.split(key)
    values = jax.random.randint(draw_key, (amount,), low_end, high_end + 1)
    where_top = jax.random.randint(spot_key, (), 0, amount)
    places = jnp.arange(amount)
    values = jnp.where(places == where_top, high_end, values)
    values = jnp.where(places == (where_top + 1) % amount, low_end, values)
    return values.astype(jnp.int32)


def draw_long_lengths(key, part):
    return bounded_lengths(jax.random.fold_in(key, 11), NLONG, SHORT_LEN + 1, LONG_LEN)


def draw_short_lengths(key, part):
    return bounded_lengths(jax.random.fold_in(key, 23), NSHORT, SHORT_LEN // 4 + 1, SHORT_LEN)


def block_scale(rng, shape, pieces, low, high):
    def one(position, parts):
        heights = jax.random.uniform(jax.random.fold_in(jax.random.fold_in(rng, 6), position), (parts,), jnp.float32, low / len(pieces), high / len(pieces))
        return jnp.repeat(jnp.exp(heights), shape[position] // parts).reshape((-1,) + (1,) * (len(shape) - position - 1))

    loudness = one(*pieces[0])
    for cut in pieces[1:]:
        loudness = loudness * one(*cut)
    return loudness


def scatter_about(key, shape, scale, reach, shards=(), dtype=jnp.bfloat16):
    loudness = block_scale(key, shape, shards, -0.22, 0.18) if shards else 1.0
    array = jax.random.normal(key, shape, jnp.float32) * scale * loudness
    return jnp.minimum(jnp.maximum(array, -reach), reach).astype(dtype)


def setup_inputs(seed: int = 0) -> dict:
    streams_of = jax.random.split(jax.random.key(seed), 19)
    return {
        "long_tokens": scatter_about(streams_of[0], (NLONG, LONG_LEN, D), 1.0, 6.0, ((0, 32),)),
        "long_lengths": draw_long_lengths(jax.random.fold_in(streams_of[18], 71), 0),
        "short_tokens": scatter_about(streams_of[2], (NSHORT, SHORT_LEN, D), 1.0, 6.0, ((0, 32),)),
        "short_lengths": draw_short_lengths(jax.random.fold_in(streams_of[18], 71), 0),
        "w_qkv": scatter_about(streams_of[4], (D, 3 * AH), D ** -0.5, 0.21875, ((0, 4),)),
        "w_depth": scatter_about(streams_of[5], (KERNEL, D), KERNEL ** -0.5, 2.0, ((1, 4),)),
        "w_point": scatter_about(streams_of[6], (D, AH), D ** -0.5, 0.21875, ((0, 4),)),
        "w_kernel": scatter_about(streams_of[7], (AH, HEADS * KERNEL), AH ** -0.5, 0.3125, ((0, 4),)),
        "w_convout": scatter_about(streams_of[8], (D, AH), D ** -0.5, 0.21875, ((0, 4),)),
        "w_out": scatter_about(streams_of[9], (D, D), (D // 16) ** -0.5, 0.875, ((0, 4),)),
        "norm1_gain": jnp.clip(1.0 + 0.1 * jax.random.normal(streams_of[10], (D,), jnp.float32), 0.5, 1.5).astype(jnp.bfloat16),
        "norm1_bias": scatter_about(streams_of[11], (D,), 0.3, 1.796875, ((0, 4),)),
        "w_inner": scatter_about(streams_of[12], (GROUPS, D // GROUPS, FF // GROUPS), (D // GROUPS) ** -0.5, 0.3125, ((1, 4),)),
        "w_outer": scatter_about(streams_of[13], (GROUPS, FF // GROUPS, D // GROUPS), (FF // GROUPS) ** -0.5, 0.15625, ((1, 4),)),
        "norm2_gain": jnp.clip(1.0 + 0.1 * jax.random.normal(streams_of[14], (D,), jnp.float32), 0.5, 1.5).astype(jnp.bfloat16),
        "norm2_bias": scatter_about(streams_of[15], (D,), 0.3, 1.796875, ((0, 4),)),
        "long_cotangent": scatter_about(streams_of[16], (NLONG, LONG_LEN, D), 1.0, 6.0, ((0, 32),)),
        "short_cotangent": scatter_about(streams_of[17], (NSHORT, SHORT_LEN, D), 1.0, 6.0, ((0, 32),)),
    }


@jax.custom_vjp
def low(v):
    return lax.optimization_barrier(v.astype(jnp.bfloat16)).astype(jnp.float32)

@jax.custom_vjp
def low_back(v):
    return v

def low_keep(v):
    return (low(v), None)

def low_pass(kept, grad):
    return (grad,)

def back_keep(v):
    return (v, None)

def back_low(kept, grad):
    return (low(grad),)
low.defvjp(low_keep, low_pass)
low_back.defvjp(back_keep, back_low)
norm_eps = 1e-12

def rounded_both(value):
    return low_back(low(value))

def matmul(left_side, right_side):
    return jnp.matmul(left_side, right_side, precision=lax.Precision.HIGHEST)

def layer_norm(values, norm_gain, norm_bias):
    center = values - lax.optimization_barrier(jnp.mean(values, -1, keepdims=True))
    spread = lax.optimization_barrier(jnp.mean(center * center, -1, keepdims=True))
    return center * lax.rsqrt(spread + norm_eps) * norm_gain + norm_bias

def depth_conv(values, taps_weight):
    kernel_taps = taps_weight.shape[0]
    half_taps = kernel_taps // 2
    length = values.shape[1]
    padded = jnp.pad(values, ((0, 0), (half_taps, half_taps), (0, 0)))
    result = jnp.zeros(values.shape, jnp.float32)
    for offset in range(kernel_taps):
        result = result + taps_weight[offset] * padded[:, offset:offset + length, :]
    return result

def dynamic_conv(logits, values):
    kernel_probs = jax.nn.softmax(logits, axis=-1)
    batches, length, head_count, kernel_taps = logits.shape
    half_taps = kernel_taps // 2
    padded = jnp.pad(values, ((0, 0), (half_taps, half_taps), (0, 0)))
    result = jnp.zeros((batches, length, head_count, values.shape[2] // head_count), jnp.float32)
    for offset in range(kernel_taps):
        window_piece = padded[:, offset:offset + length, :].reshape(batches, length, head_count, -1)
        result = result + kernel_probs[:, :, :, offset][..., None] * window_piece
    return result.reshape(batches, length, -1)

def layer_block(params, tokens, lengths):
    w_qkv, w_depth, w_point, w_kernel, w_convout, w_out, gain_one, bias_one, w_inner, w_outer, gain_two, bias_two = params
    batches, length, model_width = tokens.shape
    inner_width = HEADS * HEAD
    valid_rows = (jnp.arange(length)[None, :] < lengths[:, None]).astype(jnp.float32)
    masked = tokens * valid_rows[:, :, None]
    packed = rounded_both(matmul(masked, w_qkv))
    queries = packed[:, :, :inner_width]
    query_heads = queries.reshape(batches, length, HEADS, HEAD)
    key_heads = packed[:, :, inner_width:2 * inner_width].reshape(batches, length, HEADS, HEAD)
    value_heads = packed[:, :, 2 * inner_width:].reshape(batches, length, HEADS, HEAD)
    scores = low_back(jnp.einsum('blhe,bmhe->bhlm', query_heads, key_heads, precision=lax.Precision.HIGHEST) * HEAD ** (-0.5))
    scores = jnp.where(valid_rows[:, None, None, :] > 0, scores, -1000000000.0)
    attn_probs = low(jax.nn.softmax(scores, axis=-1))
    attended = jnp.einsum('bhlm,bmhe->blhe', attn_probs, value_heads, precision=lax.Precision.HIGHEST).reshape(batches, length, inner_width)
    depthwise = rounded_both(depth_conv(masked, w_depth))
    key_conv = low_back(matmul(depthwise, w_point))
    conv_query = low(key_conv * queries)
    kernel_logits = low_back(matmul(conv_query, w_kernel)).reshape(batches, length, HEADS, KERNEL)
    conv_values = low_back(matmul(masked, w_convout))
    convolved = dynamic_conv(kernel_logits, conv_values)
    context = rounded_both(jnp.concatenate([attended, convolved], axis=-1))
    projected = low_back(matmul(context, w_out))
    first_norm = layer_norm(projected + masked, gain_one, bias_one)
    grouped = low(first_norm).reshape(batches, length, GROUPS, model_width // GROUPS)
    hidden = low_back(jnp.einsum('blgd,gdf->blgf', grouped, w_inner, precision=lax.Precision.HIGHEST))
    active = low(jax.nn.gelu(hidden, approximate=False))
    ffn_out = low_back(jnp.einsum('blgf,gfd->blgd', active, w_outer, precision=lax.Precision.HIGHEST)).reshape(batches, length, model_width)
    return layer_norm(ffn_out + first_norm, gain_two, bias_two)

def run_bucket(params, tokens, lengths):
    amount, length, model_width = tokens.shape
    group_size = math.gcd(amount, max(1, 4096 // length))
    shaped = tokens.reshape(amount // group_size, group_size, length, model_width)
    group_lengths = lengths.reshape(amount // group_size, group_size)

    def one_group(operands):
        return layer_block(params, operands[0], operands[1])
    result = lax.map(jax.checkpoint(one_group), (shaped, group_lengths))
    return result.reshape(amount, length, model_width)

def reference(long_tokens, long_lengths, short_tokens, short_lengths, w_qkv, w_depth, w_point, w_kernel, w_convout, w_out, norm1_gain, norm1_bias, w_inner, w_outer, norm2_gain, norm2_bias, long_cotangent, short_cotangent):
    params = tuple((weight.astype(jnp.float32) for weight in (w_qkv, w_depth, w_point, w_kernel, w_convout, w_out, norm1_gain, norm1_bias, w_inner, w_outer, norm2_gain, norm2_bias)))

    def forward(weights, long_input, short_input):
        return (run_bucket(weights, long_input, long_lengths), run_bucket(weights, short_input, short_lengths))
    (long_out, short_out), pullback = jax.vjp(forward, params, long_tokens.astype(jnp.float32), short_tokens.astype(jnp.float32))
    long_valid = (jnp.arange(LONG_LEN)[None, :] < long_lengths[:, None]).astype(jnp.float32)
    short_valid = (jnp.arange(SHORT_LEN)[None, :] < short_lengths[:, None]).astype(jnp.float32)
    long_upstream = long_cotangent.astype(jnp.float32) * long_valid[:, :, None]
    short_upstream = short_cotangent.astype(jnp.float32) * short_valid[:, :, None]
    grads, long_grad, short_grad = pullback((long_upstream, short_upstream))
    return (long_out.astype(jnp.bfloat16), short_out.astype(jnp.bfloat16), long_grad.astype(jnp.bfloat16), short_grad.astype(jnp.bfloat16), grads[0], grads[1], grads[2], grads[3], grads[4], grads[5], grads[6], grads[7], grads[8], grads[9], grads[10], grads[11])
```

```python
import jax
import jax.numpy as jnp
from jax import lax
from jax.experimental import pallas as pl
from jax.experimental.pallas import tpu as pltpu
from jax.sharding import Mesh
from jax.sharding import PartitionSpec as P

BF = jnp.bfloat16
F32 = jnp.float32
EPS = 1e-12
D = 768
AH = 384
HEADS = 6
TAPS = 9
LONG = 512
SHORT = 128
ROWS = 768
PAD = 800
SLOTS = 8
NEG = -1000000000.0
PSTART = tuple(8 + 128 * i + 8 * max(i - 3, 0) for i in range(6))
SEGS = ((0, 512, 8), (512, 128, 528), (640, 128, 664))


def nn(a, b):
    return lax.dot_general(a, b, (((1,), (0,)), ((), ())), preferred_element_type=F32)


def nt(a, b):
    return lax.dot_general(a, b, (((1,), (1,)), ((), ())), preferred_element_type=F32)


def tn(a, b):
    return lax.dot_general(a, b, (((0,), (0,)), ((), ())), preferred_element_type=F32)


def iota(shape, axis):
    return lax.broadcasted_iota(jnp.int32, shape, axis)


def loop(count, body):
    def step(i, carry):
        body(i)
        return carry

    lax.fori_loop(0, count, step, 0)


def at(i, size):
    if isinstance(i, int):
        return pl.ds(i * size, size)
    return pl.ds(pl.multiple_of(i * size, size), size)


def padded_start(i):
    return pl.multiple_of(8 + 128 * i + 8 * jnp.maximum(i - 3, 0), 8)


def zero_gaps(ref):
    for start in (0, 520, 656, 792):
        ref[start : start + 8, :] = jnp.zeros((8, ref.shape[1]), ref.dtype)


def eye(n, dtype):
    return jnp.where(iota((n, n), 0) == iota((n, n), 1), 1.0, 0.0).astype(dtype)


def tap_permutation():
    row, col = iota((128, 128), 0), iota((128, 128), 1)
    head, tap = col & 7, col >> 3
    keep = (head < HEADS) & (tap < TAPS) & (row == 64 + head * TAPS + tap)
    return jnp.where(keep, 1.0, 0.0).astype(BF)


def head_spread():
    row, col = iota((256, AH), 0), iota((256, AH), 1)
    return jnp.where((row & 127) == (col >> 6), 1.0, 0.0).astype(BF)


def head_gather():
    row, col = iota((AH, 128), 0), iota((AH, 128), 1)
    return jnp.where((row >> 6) == col, 1.0, 0.0).astype(BF)


def split_two(values):
    high = values.astype(BF)
    low = (values - high.astype(F32)).astype(BF)
    return jnp.concatenate([high, low], axis=1)


def tap_kernel(wm):
    stored = jnp.concatenate([wm[7, 192 * n : 192 * n + 96, 128:256] for n in range(4)], axis=0)
    return nn(stored, tap_permutation()).astype(BF)


def mixer_forward(
    lens, xl, xs, wm, xm, packed, plong, pshort, dw, kc, cq, kp, cv, ctx, vec, xpad, spread, wk
):
    zero_gaps(xpad)
    zero_gaps(cv)
    zero_gaps(kp)
    for i in range(6):
        seg = max(i - 3, 0)
        base = 128 * i if i < 4 else 0
        tokens = xl[128 * i : 128 * i + 128, :] if i < 4 else xs[128 * (i - 4) : 128 * (i - 3), :]
        live = base + iota((128, D), 0) < lens[seg]
        values = jnp.where(live, tokens.astype(F32), 0.0)
        xpad[PSTART[i] : PSTART[i] + 128, :] = values
        xm[128 * i : 128 * i + 128, :] = values.astype(BF)
    vec[...] = nt(eye(128, BF), wm[7, :, 128:256])[0:24, :]
    spread[...] = head_spread()
    wk[...] = tap_kernel(wm)

    def project(b):
        packed[:, at(b, 256)] = nn(xm[...], wm[b]).astype(BF)

    loop(4, project)
    part = nn(xm[...], wm[4])
    packed[:, 1024:1152] = part[:, 0:128].astype(BF)
    for start, rows, pstart in SEGS:
        cv[pstart : pstart + rows, 0:128] = part[start : start + rows, 128:256]
    part = nn(xm[...], wm[5])
    for start, rows, pstart in SEGS:
        cv[pstart : pstart + rows, 128:384] = part[start : start + rows, :]

    def depth(i):
        ps = padded_start(i)
        for c in range(3):
            lanes = slice(256 * c, 256 * c + 256)
            window = xpad[pl.ds(pl.multiple_of(ps - 8, 8), 144), lanes]
            total = jnp.zeros((128, 256), F32)
            for j in range(TAPS):
                total = total + vec[j : j + 1, lanes] * window[4 + j : 132 + j, :]
            dw[at(i, 128), lanes] = total.astype(BF)

    loop(6, depth)
    kc[:, 0:256] = nn(dw[...], wm[6])
    kc[:, 256:384] = nn(dw[...], wm[7, :, 0:128])

    def dynamic(i):
        rows = at(i, 128)
        ps = padded_start(i)
        query = (kc[rows, :] * packed[rows, 0:AH].astype(F32)).astype(BF)
        cq[rows, :] = query
        logits = nn(query, wk[...])
        lane = iota((128, 128), 1)
        real = lane < 8 * TAPS
        top = jnp.where(real, logits, NEG * 1e20)
        for shift in (64, 32, 16, 8):
            top = jnp.maximum(top, pltpu.roll(top, shift, 1))
        ex = jnp.where(real, jnp.exp(logits - top), 0.0)
        total = ex
        for shift in (64, 32, 16, 8):
            total = total + pltpu.roll(total, shift, 1)
        probs = ex / total
        kp[pl.ds(ps, 128), :] = probs
        window = cv[pl.ds(pl.multiple_of(ps - 8, 8), 144), :]
        out = jnp.zeros((128, AH), F32)
        for j in range(TAPS):
            moved = probs if j == 0 else pltpu.roll(probs, 128 - 8 * j, 1)
            out = out + nn(split_two(moved), spread[...]) * window[4 + j : 132 + j, :]
        ctx[rows, AH:D] = out.astype(BF)

    loop(6, dynamic)

    def attend(row0, nq, key0, nk, limit, pair, store):
        queries = packed[pl.ds(row0, nq), at(pair, 128)].astype(F32)
        keys = packed[pl.ds(key0, nk), pl.ds(pl.multiple_of(AH + pair * 128, 128), 128)]
        vals = packed[pl.ds(key0, nk), pl.ds(pl.multiple_of(2 * AH + pair * 128, 128), 128)]
        lane = iota((nq, 128), 1)
        outs = []
        for hh in range(2):
            mine = (lane >> 6) == hh
            scores = nt(jnp.where(mine, queries, 0.0).astype(BF), keys) * 0.125
            scores = jnp.where(iota((nq, nk), 1) < limit, scores, NEG)
            ex = jnp.exp(scores - jnp.max(scores, axis=1, keepdims=True))
            probs = (ex / jnp.sum(ex, axis=1, keepdims=True)).astype(BF)
            store(hh, probs)
            outs.append(nn(probs, vals))
        both = jnp.where(lane < 64, outs[0], outs[1])
        ctx[pl.ds(row0, nq), at(pair, 128)] = both.astype(BF)

    def long_attend(i):
        pair, block = i >> 1, i & 1
        row0 = pl.multiple_of(block * 256, 256)

        def store(hh, probs):
            plong[2 * pair + hh, pl.ds(row0, 256), :] = probs

        attend(row0, 256, 0, LONG, lens[0], pair, store)

    loop(6, long_attend)

    def short_attend(i):
        seg = jnp.where(i >= 3, 1, 0)
        pair = i - 3 * seg
        row0 = pl.multiple_of(LONG + 128 * seg, 128)

        def store(hh, probs):
            pshort[seg, 2 * pair + hh, :, :] = probs

        attend(row0, 128, row0, SHORT, lens[1 + seg], pair, store)

    loop(6, short_attend)


ERFC = (
    -1.26551223, 1.00002368, 0.37409196, 0.09678418, -0.18628806,
    0.27886807, -1.13520398, 1.48851587, -0.82215223, 0.17087277,
)


def gelu_parts(hidden):
    z = jnp.abs(hidden) * 0.7071067811865476
    t = 1.0 / (1.0 + 0.5 * z)
    series = jnp.full_like(z, ERFC[-1])
    for coefficient in ERFC[-2::-1]:
        series = series * t + coefficient
    square = z * z
    tail = 0.5 * t * jnp.exp(series - square)
    cdf = jnp.where(hidden < 0.0, tail, 1.0 - tail)
    return cdf, jnp.exp(-square) * 0.3989422804014327


def ffn_both(
    lens, xm, ctx, vec, wf, cl, cs,
    ol, os, ga, gone, gctx, gvec,
    wo, wi, wu, res, xhat, grouped, gffn, active, slope, ffn, rstd, acc, ghid, gproj,
):
    for n in range(4):
        for w in range(8):
            wi[w, 96 * n : 96 * n + 96, :] = wf[w, n, 0:96, :]
            wu[4 * (w // 4) + n, 96 * (w % 4) : 96 * (w % 4) + 96, :] = wf[w, n, 96:192, :]
            row = 192 * n + 48 * (w % 4)
            lanes = slice(AH * (w // 4), AH * (w // 4) + AH)
            wo[row : row + 48, lanes] = wf[w, n, 192:240, :]
    gain_one, bias_one = vec[16:17, :], vec[17:18, :]
    gain_two, bias_two = vec[18:19, :], vec[19:20, :]
    gvec[...] = jnp.zeros((8, D), F32)

    def mix(i):
        rows = at(i, 256)
        res[rows, :] = nn(ctx[rows, :], wo[...]) + xm[rows, :].astype(F32)

    loop(3, mix)

    def norm_one(i):
        rows = at(i, 64)
        values = res[rows, :]
        center = values - jnp.mean(values, axis=1, keepdims=True)
        scale = lax.rsqrt(jnp.mean(center * center, axis=1, keepdims=True) + EPS)
        hat = center * scale
        first = hat * gain_one + bias_one
        xhat[rows, :] = hat
        rstd[rows, :] = jnp.broadcast_to(scale, (64, 128))
        res[rows, :] = first
        short = first.astype(BF)
        grouped[0, rows, :] = short[:, 0:AH]
        grouped[1, rows, :] = short[:, AH:D]

    loop(12, norm_one)
    ffn[...] = jnp.zeros((2, ROWS, AH), F32)

    def expand(b):
        acc[...] = nn(grouped[b >> 2], wi[b])

        def act(i):
            rows = at(i, 64)
            hidden = acc[rows, :]
            cdf, density = gelu_parts(hidden)
            active[b, rows, :] = (hidden * cdf).astype(BF)
            slope[b, rows, :] = cdf + hidden * density

        loop(12, act)
        ffn[b >> 2] += nn(active[b], wu[b])

    loop(8, expand)

    def norm_two(cot, out, offset):
        def run(i):
            rows = at(i, 64)
            whole = pl.ds(pl.multiple_of(offset + i * 64, 64), 64)
            values = jnp.concatenate([ffn[0, whole, :], ffn[1, whole, :]], axis=1) + res[whole, :]
            center = values - jnp.mean(values, axis=1, keepdims=True)
            scale = lax.rsqrt(jnp.mean(center * center, axis=1, keepdims=True) + EPS)
            hat = center * scale
            out[rows, :] = (hat * gain_two + bias_two).astype(BF)
            if offset:
                seg, base = 1 + (i >> 1), (i & 1) * 64
            else:
                seg, base = 0, i * 64
            live = base + iota((64, D), 0) < lens[seg]
            up = jnp.where(live, cot[rows, :].astype(F32), 0.0)
            gvec[2:3, :] += jnp.sum(up * hat, axis=0, keepdims=True)
            gvec[3:4, :] += jnp.sum(up, axis=0, keepdims=True)
            up = up * gain_two
            grad = scale * (
                up
                - jnp.mean(up, axis=1, keepdims=True)
                - hat * jnp.mean(up * hat, axis=1, keepdims=True)
            )
            res[whole, :] = grad
            short = grad.astype(BF)
            gffn[0, whole, :] = short[:, 0:AH]
            gffn[1, whole, :] = short[:, AH:D]

        return run

    loop(8, norm_two(cl, ol, 0))
    loop(4, norm_two(cs, os, LONG))
    ffn[...] = jnp.zeros((2, ROWS, AH), F32)

    def contract(b):
        g, n = b >> 2, b & 3
        acc[...] = nt(gffn[g], wu[b])

        def act(i):
            rows = at(i, 64)
            ghid[rows, :] = (acc[rows, :] * slope[b, rows, :]).astype(BF)

        loop(12, act)
        part = tn(active[b], gffn[g]).astype(BF)
        for w in range(4):
            ga[4 * g + w, n, 96:192, :] = part[96 * w : 96 * w + 96, :]
        part = tn(grouped[g], ghid[...]).astype(BF)
        for m in range(4):
            ga[b, m, 0:96, :] = part[96 * m : 96 * m + 96, :]
        ffn[g] += nt(ghid[...], wi[b])

    loop(8, contract)

    def norm_one_back(i):
        rows = at(i, 64)
        up = res[rows, :] + jnp.concatenate([ffn[0, rows, :], ffn[1, rows, :]], axis=1)
        hat = xhat[rows, :]
        gvec[0:1, :] += jnp.sum(up * hat, axis=0, keepdims=True)
        gvec[1:2, :] += jnp.sum(up, axis=0, keepdims=True)
        up = up * gain_one
        grad = rstd[rows, 0:1] * (
            up
            - jnp.mean(up, axis=1, keepdims=True)
            - hat * jnp.mean(up * hat, axis=1, keepdims=True)
        )
        gone[rows, :] = grad
        gproj[rows, :] = grad.astype(BF)

    loop(12, norm_one_back)
    for c in range(2):
        part = tn(ctx[...], gproj[:, AH * c : AH * c + AH]).astype(BF)
        for n in range(4):
            for r in range(4):
                row = 192 * n + 48 * r
                ga[4 * c + r, n, 192:240, :] = part[row : row + 48, :]

    def unmix(i):
        rows = at(i, 256)
        gctx[rows, :] = nt(gproj[rows, :], wo[...]).astype(BF)

    loop(3, unmix)


def mixer_backward(
    lens, xm, packed, plong, pshort, dw, kc, cq, kp, cv, vec, gone, gctx, gvec, wm,
    il, is_, gb,
    xpad, gcp, gdp, grads, gqc, dkv, gkc, glog, gdep, spread, gather, wk,
):
    zero_gaps(xpad)
    zero_gaps(gcp)
    zero_gaps(gdp)
    for start, rows, pstart in SEGS:
        xpad[pstart : pstart + rows, :] = xm[start : start + rows, :].astype(F32)
        gcp[pstart : pstart + rows, :] = gctx[start : start + rows, AH:D].astype(F32)
    spread[...] = head_spread()
    gather[...] = head_gather()
    wk[...] = tap_kernel(wm)
    gdep[...] = jnp.zeros((8 * TAPS, D), F32)

    def dynamic(i):
        rows = at(i, 128)
        ps = padded_start(i)
        wide = pl.ds(pl.multiple_of(ps - 8, 8), 144)
        taps = kp[wide, :]
        grad_wide = gcp[wide, :]
        values = cv[wide, :]
        grad = gcp[pl.ds(ps, 128), :]
        total = jnp.zeros((128, AH), F32)
        gprob = jnp.zeros((128, 128), F32)
        for j in range(TAPS):
            moved = taps if j == 0 else pltpu.roll(taps, 128 - 8 * j, 1)
            part = nn(split_two(moved), spread[...]) * grad_wide
            total = total + part[12 - j : 140 - j, :]
            part = nn((grad * values[4 + j : 132 + j, :]).astype(BF), gather[...])
            gprob = gprob + (part if j == 0 else pltpu.roll(part, 8 * j, 1))
        grads[rows, 3 * AH : 4 * AH] = total.astype(BF)
        probs = kp[pl.ds(ps, 128), :]
        inner = probs * gprob
        for shift in (64, 32, 16, 8):
            inner = inner + pltpu.roll(inner, shift, 1)
        glogits = (probs * (gprob - inner)).astype(BF)
        glog[rows, :] = glogits
        gquery = nt(glogits, wk[...])
        gkc[rows, :] = (gquery * packed[rows, 0:AH].astype(F32)).astype(BF)
        gqc[rows, :] = gquery * kc[rows, :]

    loop(6, dynamic)

    def point_back(c):
        part = nt(gkc[:, 0:256], wm[6, at(c, 256), :])
        part = part + nt(gkc[:, 256:384], wm[7, at(c, 256), 0:128])
        part = part.astype(BF).astype(F32)
        for start, rows, pstart in SEGS:
            gdp[pstart : pstart + rows, at(c, 256)] = part[start : start + rows, :]

    loop(3, point_back)

    def depth(i):
        ps = padded_start(i)
        wide = pl.ds(pl.multiple_of(ps - 8, 8), 144)
        for c in range(3):
            lanes = slice(256 * c, 256 * c + 256)
            tokens = xpad[wide, lanes]
            grad_wide = gdp[wide, lanes]
            grad = gdp[pl.ds(ps, 128), lanes]
            total = gone[at(i, 128), lanes]
            for j in range(TAPS):
                total = total + vec[j : j + 1, lanes] * grad_wide[12 - j : 140 - j, :]
                part = tokens[4 + j : 132 + j, :] * grad
                gdep[8 * j : 8 * j + 8, lanes] += jnp.sum(part.reshape(16, 8, 256), axis=0)
            gone[at(i, 128), lanes] = total

    loop(6, depth)

    def attend(row0, nq, key0, nk, pair, load, first):
        queries = packed[pl.ds(row0, nq), at(pair, 128)].astype(F32)
        keys = packed[pl.ds(key0, nk), pl.ds(pl.multiple_of(AH + pair * 128, 128), 128)]
        vals = packed[pl.ds(key0, nk), pl.ds(pl.multiple_of(2 * AH + pair * 128, 128), 128)]
        up = gctx[pl.ds(row0, nq), at(pair, 128)].astype(F32)
        lane = iota((nq, 128), 1)
        outs = []
        gkeys = jnp.zeros((nk, 128), F32)
        gvals = jnp.zeros((nk, 128), F32)
        for hh in range(2):
            mine = (lane >> 6) == hh
            query = jnp.where(mine, queries, 0.0).astype(BF)
            upper = jnp.where(mine, up, 0.0).astype(BF)
            probs_low = load(hh)
            probs = probs_low.astype(F32)
            gprobs = nt(upper, vals)
            inner = jnp.sum(probs * gprobs, axis=1, keepdims=True)
            gscores = (probs * (gprobs - inner)).astype(BF)
            outs.append(nn(gscores, keys))
            gkeys = gkeys + tn(gscores, query)
            gvals = gvals + tn(probs_low, upper)
        both = jnp.where(lane < 64, outs[0], outs[1]) * 0.125
        both = both + gqc[pl.ds(row0, nq), at(pair, 128)]
        grads[pl.ds(row0, nq), at(pair, 128)] = both.astype(BF)
        span = pl.ds(key0, nk)
        if first:
            dkv[0, span, at(pair, 128)] = gkeys
            dkv[1, span, at(pair, 128)] = gvals
        else:
            dkv[0, span, at(pair, 128)] += gkeys
            dkv[1, span, at(pair, 128)] += gvals

    def long_attend(pair):
        for block in range(2):
            attend(
                256 * block, 256, 0, LONG, pair,
                lambda hh: plong[2 * pair + hh, 256 * block : 256 * block + 256, :],
                block == 0,
            )

    loop(3, long_attend)

    def short_attend(i):
        seg = jnp.where(i >= 3, 1, 0)
        pair = i - 3 * seg
        row0 = pl.multiple_of(LONG + 128 * seg, 128)
        attend(row0, 128, row0, SHORT, pair, lambda hh: pshort[seg, 2 * pair + hh, :, :], True)

    loop(6, short_attend)

    def pack(i):
        rows = at(i, 128)
        grads[rows, AH : 2 * AH] = (dkv[0, rows, :] * 0.125).astype(BF)
        grads[rows, 2 * AH : 3 * AH] = dkv[1, rows, :].astype(BF)

    loop(6, pack)

    def weights(b):
        gb[b] = tn(xm[...], grads[:, at(b, 256)]).astype(BF)

    loop(6, weights)
    gb[6] = tn(dw[...], gkc[:, 0:256]).astype(BF)
    gb[7, :, 0:128] = tn(dw[...], gkc[:, 256:384]).astype(BF)
    taps = [jnp.sum(gdep[8 * j : 8 * j + 8, :], axis=0, keepdims=True) for j in range(TAPS)]
    table = jnp.concatenate(
        taps + [jnp.zeros((7, D), F32), gvec[...], jnp.zeros((104, D), F32)], axis=0
    ).astype(BF)
    misc = tn(table, eye(128, BF))
    gkernel = nt(tn(cq[...], glog[...]).astype(BF), tap_permutation())
    for n in range(4):
        row = 192 * n
        gb[7, row : row + 96, 128:256] = (
            misc[row : row + 96, :] + gkernel[96 * n : 96 * n + 96, :]
        ).astype(BF)
        gb[7, row + 96 : row + 192, 128:256] = misc[row + 96 : row + 192, :].astype(BF)

    def inputs(i):
        rows = at(i, 256)
        total = gone[rows, :]
        for b in range(6):
            total = total + nt(grads[rows, 256 * b : 256 * b + 256], wm[b])
        return total

    def inputs_long(i):
        live = i * 256 + iota((256, D), 0) < lens[0]
        il[at(i, 256), :] = jnp.where(live, inputs(i), 0.0).astype(BF)

    loop(2, inputs_long)
    total = inputs(2)
    row = iota((128, D), 0)
    for seg in range(2):
        part = total[128 * seg : 128 * seg + 128, :]
        is_[128 * seg : 128 * seg + 128, :] = jnp.where(row < lens[1 + seg], part, 0.0).astype(BF)


def call(kernel, n_in, outs, scratch, *args):
    return pl.pallas_call(
        kernel,
        out_shape=[jax.ShapeDtypeStruct(s, d) for s, d in outs],
        in_specs=[pl.BlockSpec(memory_space=pltpu.SMEM)]
        + [pl.BlockSpec(memory_space=pltpu.VMEM)] * (n_in - 1),
        out_specs=[pl.BlockSpec(memory_space=pltpu.VMEM)] * len(outs),
        scratch_shapes=[pltpu.VMEM(s, d) for s, d in scratch],
        compiler_params=pltpu.CompilerParams(vmem_limit_bytes=60 << 20),
        name=kernel.__name__,
    )(*args)


def forward_mixer(lens, xl, xs, wm):
    outs = [
        ((ROWS, D), BF), ((ROWS, 3 * AH), BF),
        ((HEADS, LONG, LONG), BF), ((2, HEADS, SHORT, SHORT), BF),
        ((ROWS, D), BF), ((ROWS, AH), F32), ((ROWS, AH), BF), ((PAD, 128), F32),
        ((PAD, AH), F32), ((ROWS, D), BF), ((24, D), F32),
    ]
    scratch = [((PAD, D), F32), ((256, AH), BF), ((AH, 128), BF)]
    return call(mixer_forward, 4, outs, scratch, lens, xl, xs, wm)


def feed_forward(lens, xm, ctx, vec, wf, cl, cs):
    outs = [
        ((LONG, D), BF), ((2 * SHORT, D), BF), ((SLOTS, 4, 240, AH), BF),
        ((ROWS, D), F32), ((ROWS, D), BF), ((8, D), F32),
    ]
    scratch = [
        ((D, D), BF), ((8, AH, AH), BF), ((8, AH, AH), BF), ((ROWS, D), F32), ((ROWS, D), F32),
        ((2, ROWS, AH), BF), ((2, ROWS, AH), BF), ((8, ROWS, AH), BF), ((8, ROWS, AH), F32),
        ((2, ROWS, AH), F32), ((ROWS, 128), F32), ((ROWS, AH), F32), ((ROWS, AH), BF),
        ((ROWS, D), BF),
    ]
    return call(ffn_both, 7, outs, scratch, lens, xm, ctx, vec, wf, cl, cs)


def backward_mixer(*args):
    outs = [((LONG, D), BF), ((2 * SHORT, D), BF), ((SLOTS, D, 256), BF)]
    scratch = [
        ((PAD, D), F32), ((PAD, AH), F32), ((PAD, D), F32), ((ROWS, 4 * AH), BF),
        ((ROWS, AH), F32), ((2, ROWS, AH), F32), ((ROWS, AH), BF), ((ROWS, 128), BF),
        ((8 * TAPS, D), F32), ((256, AH), BF), ((AH, 128), BF), ((AH, 128), BF),
    ]
    return call(mixer_backward, 15, outs, scratch, *args)


def layer(lens, xl, xs, cl, cs, wm, wf):
    xm, packed, plong, pshort, dw, kc, cq, kp, cv, ctx, vec = forward_mixer(lens, xl, xs, wm)
    ol, os, ga, gone, gctx, gvec = feed_forward(lens, xm, ctx, vec, wf, cl, cs)
    il, is_, gb = backward_mixer(
        lens, xm, packed, plong, pshort, dw, kc, cq, kp, cv, vec, gone, gctx, gvec, wm
    )
    return ol, os, il, is_, ga, gb


def pack_mixer(w_qkv, w_depth, w_point, w_kernel, w_convout, g1, b1, g2, b2):
    rows = w_qkv.shape[0]
    norms = jnp.stack([g1, b1, g2, b2], axis=1)
    left = jnp.concatenate(
        [
            jnp.pad(w_depth.T, ((0, 0), (0, 16 - TAPS))),
            jnp.pad(norms, ((0, 0), (0, 44))),
        ],
        axis=1,
    )
    right = jnp.pad(w_kernel, ((0, rows - w_kernel.shape[0]), (0, 64 - w_kernel.shape[1])))
    return jnp.concatenate([w_qkv, w_convout, w_point, left, right], axis=1)


def pack_ffn(w_out, w_inner, w_outer, slot):
    g, c = slot // 4, slot % 4
    inner = lax.dynamic_slice(w_inner, (g, 0, c * AH), (1, 96, AH))[0]
    outer = lax.dynamic_slice(w_outer, (g, c * 96, 0), (1, 96, AH))[0]
    out = lax.dynamic_slice(w_out, (c * 48, g * AH), (48, AH))
    return jnp.concatenate([inner, outer, out], axis=0)


def body(
    long_tokens, long_lengths, short_tokens, short_lengths,
    w_qkv, w_depth, w_point, w_kernel, w_convout, w_out, norm1_gain, norm1_bias,
    w_inner, w_outer, norm2_gain, norm2_bias, long_cotangent, short_cotangent,
):
    slot = lax.axis_index("wide")
    mixer = pack_mixer(
        w_qkv, w_depth, w_point, w_kernel, w_convout, norm1_gain, norm1_bias, norm2_gain, norm2_bias
    )
    mixer = lax.dynamic_slice(mixer, (0, slot * 256), (192, 256))
    wm = lax.all_gather(mixer, ("wide", "narrow"), axis=0, tiled=False).reshape(SLOTS, D, 256)
    wf = lax.all_gather(pack_ffn(w_out, w_inner, w_outer, slot), ("wide", "narrow"), axis=0)
    wf = wf.reshape(SLOTS, 4, 240, AH)
    lens = jnp.concatenate([long_lengths, short_lengths])
    ol, os, il, is_, ga, gb = layer(
        lens,
        long_tokens.reshape(LONG, D), short_tokens.reshape(2 * SHORT, D),
        long_cotangent.reshape(LONG, D), short_cotangent.reshape(2 * SHORT, D),
        wm, wf,
    )

    def reduce(parts):
        parts = lax.psum_scatter(parts, "wide", scatter_dimension=0, tiled=False)
        parts = lax.psum_scatter(parts, "narrow", scatter_dimension=0, tiled=False)
        parts = lax.psum(parts, "hi")
        return lax.all_gather(parts, "wide", axis=0, tiled=False).astype(F32)

    ga = reduce(ga)
    gb = reduce(gb.reshape(SLOTS, 4, 192, 256))
    inner = ga[:, 0:96].reshape(2, 4, 96, AH).transpose(0, 2, 1, 3).reshape(2, 96, 4 * AH)
    outer = ga[:, 96:192].reshape(2, AH, AH)
    out = ga[:, 192:240].reshape(2, 4, 48, AH).transpose(1, 2, 0, 3).reshape(192, D)
    gb = gb.transpose(1, 0, 2).reshape(192, 2048)
    misc = gb[:, 1920:2048]
    return (
        ol.reshape(long_tokens.shape), os.reshape(short_tokens.shape),
        il.reshape(long_tokens.shape), is_.reshape(short_tokens.shape),
        gb[:, 0:1152], misc[:, 0:TAPS].T, gb[:, 1536:1920], misc[0:96, 64:118], gb[:, 1152:1536],
        out, misc[:, 16], misc[:, 17], inner, outer, misc[:, 18], misc[:, 19],
    )


def solution(mesh):
    wide, narrow = mesh.shape["wide"], mesh.shape["narrow"]
    inner_mesh = Mesh(mesh.devices.reshape(wide // SLOTS, SLOTS, narrow), ("hi", "wide", "narrow"))
    every = ("hi", "wide", "narrow")
    rows = P(every, None, None)
    weights = (
        P("narrow", None), P(None, "narrow"), P("narrow", None), P("narrow", None),
        P("narrow", None), P("narrow", None), P("narrow"), P("narrow"),
        P(None, "narrow", None), P(None, "narrow", None), P("narrow"), P("narrow"),
    )
    return jax.shard_map(
        body,
        mesh=inner_mesh,
        in_specs=(rows, P(every), rows, P(every)) + weights + (rows, rows),
        out_specs=(rows, rows, rows, rows) + weights,
        check_vma=False,
    )
```

```python
import jax
import jax.numpy as jnp
from jax import lax
from jax.experimental import pallas as pl
from jax.experimental.pallas import tpu as pltpu
from jax.sharding import Mesh
from jax.sharding import PartitionSpec as P

BF = jnp.bfloat16
F32 = jnp.float32
EPS = 1e-12
D = 768
AH = 384
HEADS = 6
TAPS = 9
LONG = 512
SHORT = 128
ROWS = 768
PAD = 800
SLOTS = 8
NEG = -1000000000.0
PSTART = tuple(8 + 128 * i + 8 * max(i - 3, 0) for i in range(6))
SEGS = ((0, 512, 8), (512, 128, 528), (640, 128, 664))


def nn(a, b):
    return lax.dot_general(a, b, (((1,), (0,)), ((), ())), preferred_element_type=F32)


def nt(a, b):
    return lax.dot_general(a, b, (((1,), (1,)), ((), ())), preferred_element_type=F32)


def tn(a, b):
    return lax.dot_general(a, b, (((0,), (0,)), ((), ())), preferred_element_type=F32)


def iota(shape, axis):
    return lax.broadcasted_iota(jnp.int32, shape, axis)


def loop(count, body):
    def step(i, carry):
        body(i)
        return carry

    lax.fori_loop(0, count, step, 0)


def at(i, size):
    if isinstance(i, int):
        return pl.ds(i * size, size)
    return pl.ds(pl.multiple_of(i * size, size), size)


def padded_start(i):
    return pl.multiple_of(8 + 128 * i + 8 * jnp.maximum(i - 3, 0), 8)


def zero_gaps(ref):
    for start in (0, 520, 656, 792):
        ref[start : start + 8, :] = jnp.zeros((8, ref.shape[1]), ref.dtype)


def eye(n, dtype):
    return jnp.where(iota((n, n), 0) == iota((n, n), 1), 1.0, 0.0).astype(dtype)


def tap_permutation():
    row, col = iota((128, 128), 0), iota((128, 128), 1)
    head, tap = col & 7, col >> 3
    keep = (head < HEADS) & (tap < TAPS) & (row == 64 + head * TAPS + tap)
    return jnp.where(keep, 1.0, 0.0).astype(BF)


def head_spread():
    row, col = iota((256, AH), 0), iota((256, AH), 1)
    return jnp.where((row & 127) == (col >> 6), 1.0, 0.0).astype(BF)


def head_gather():
    row, col = iota((AH, 128), 0), iota((AH, 128), 1)
    return jnp.where((row >> 6) == col, 1.0, 0.0).astype(BF)


def split_two(values):
    high = values.astype(BF)
    low = (values - high.astype(F32)).astype(BF)
    return jnp.concatenate([high, low], axis=1)


def tap_kernel(wm):
    stored = jnp.concatenate([wm[7, 192 * n : 192 * n + 96, 128:256] for n in range(4)], axis=0)
    return nn(stored, tap_permutation()).astype(BF)


def slot_of(where, core, chip):
    return 2 * ((where >> 1) ^ chip) + ((where & 1) ^ core)


def mixer_forward(
    place, llen, slen, xl, xs, p0, p1, p2, p3, p4, p5, p6, p7,
    xm, packed, plong, pshort, dw, kc, cq, kp, cv, ctx, vec, wm, xpad, spread, wk, sem
):
    for core, pieces in enumerate(((p0, p1, p2, p3), (p4, p5, p6, p7))):
        for chip, piece in enumerate(pieces):
            slot = slot_of(place[0], core, chip)

            def fetch(k):
                rows = pl.ds(pl.multiple_of((place[1] ^ k) * 192, 192), 192)
                pltpu.make_async_copy(piece.at[k], wm.at[slot, rows, :], sem).start()

            loop(4, fetch)
    lens = (llen[0], slen[0], slen[1])
    zero_gaps(xpad)
    zero_gaps(cv)
    zero_gaps(kp)
    for i in range(6):
        seg = max(i - 3, 0)
        base = 128 * i if i < 4 else 0
        tokens = xl[128 * i : 128 * i + 128, :] if i < 4 else xs[128 * (i - 4) : 128 * (i - 3), :]
        live = base + iota((128, D), 0) < lens[seg]
        values = jnp.where(live, tokens.astype(F32), 0.0)
        xpad[PSTART[i] : PSTART[i] + 128, :] = values
        xm[128 * i : 128 * i + 128, :] = values.astype(BF)
    spread[...] = head_spread()
    pltpu.make_async_copy(wm, wm, sem).wait()
    vec[...] = nt(eye(128, BF), wm[7, :, 128:256])[0:24, :]
    wk[...] = tap_kernel(wm)

    def project(b):
        packed[:, at(b, 256)] = nn(xm[...], wm[b]).astype(BF)

    loop(4, project)
    part = nn(xm[...], wm[4])
    packed[:, 1024:1152] = part[:, 0:128].astype(BF)
    for start, rows, pstart in SEGS:
        cv[pstart : pstart + rows, 0:128] = part[start : start + rows, 128:256]
    part = nn(xm[...], wm[5])
    for start, rows, pstart in SEGS:
        cv[pstart : pstart + rows, 128:384] = part[start : start + rows, :]

    def depth(i):
        ps = padded_start(i)
        for c in range(3):
            lanes = slice(256 * c, 256 * c + 256)
            window = xpad[pl.ds(pl.multiple_of(ps - 8, 8), 144), lanes]
            total = jnp.zeros((128, 256), F32)
            for j in range(TAPS):
                total = total + vec[j : j + 1, lanes] * window[4 + j : 132 + j, :]
            dw[at(i, 128), lanes] = total.astype(BF)

    loop(6, depth)
    kc[:, 0:256] = nn(dw[...], wm[6])
    kc[:, 256:384] = nn(dw[...], wm[7, :, 0:128])

    def dynamic(i):
        rows = at(i, 128)
        ps = padded_start(i)
        query = (kc[rows, :] * packed[rows, 0:AH].astype(F32)).astype(BF)
        cq[rows, :] = query
        logits = nn(query, wk[...])
        lane = iota((128, 128), 1)
        real = lane < 8 * TAPS
        top = jnp.where(real, logits, NEG * 1e20)
        for shift in (64, 32, 16, 8):
            top = jnp.maximum(top, pltpu.roll(top, shift, 1))
        ex = jnp.where(real, jnp.exp(logits - top), 0.0)
        total = ex
        for shift in (64, 32, 16, 8):
            total = total + pltpu.roll(total, shift, 1)
        probs = ex / total
        kp[pl.ds(ps, 128), :] = probs
        window = cv[pl.ds(pl.multiple_of(ps - 8, 8), 144), :]
        out = jnp.zeros((128, AH), F32)
        for j in range(TAPS):
            moved = probs if j == 0 else pltpu.roll(probs, 128 - 8 * j, 1)
            out = out + nn(split_two(moved), spread[...]) * window[4 + j : 132 + j, :]
        ctx[rows, AH:D] = out.astype(BF)

    loop(6, dynamic)

    def attend(row0, nq, key0, nk, limit, pair, store):
        queries = packed[pl.ds(row0, nq), at(pair, 128)].astype(F32)
        keys = packed[pl.ds(key0, nk), pl.ds(pl.multiple_of(AH + pair * 128, 128), 128)]
        vals = packed[pl.ds(key0, nk), pl.ds(pl.multiple_of(2 * AH + pair * 128, 128), 128)]
        lane = iota((nq, 128), 1)
        outs = []
        for hh in range(2):
            mine = (lane >> 6) == hh
            scores = nt(jnp.where(mine, queries, 0.0).astype(BF), keys) * 0.125
            scores = jnp.where(iota((nq, nk), 1) < limit, scores, NEG)
            ex = jnp.exp(scores - jnp.max(scores, axis=1, keepdims=True))
            probs = (ex / jnp.sum(ex, axis=1, keepdims=True)).astype(BF)
            store(hh, probs)
            outs.append(nn(probs, vals))
        both = jnp.where(lane < 64, outs[0], outs[1])
        ctx[pl.ds(row0, nq), at(pair, 128)] = both.astype(BF)

    def long_attend(i):
        pair, block = i >> 1, i & 1
        row0 = pl.multiple_of(block * 256, 256)

        def store(hh, probs):
            plong[2 * pair + hh, pl.ds(row0, 256), :] = probs

        attend(row0, 256, 0, LONG, lens[0], pair, store)

    loop(6, long_attend)

    def short_attend(i):
        seg = jnp.where(i >= 3, 1, 0)
        pair = i - 3 * seg
        row0 = pl.multiple_of(LONG + 128 * seg, 128)

        def store(hh, probs):
            pshort[seg, 2 * pair + hh, :, :] = probs

        attend(row0, 128, row0, SHORT, slen[seg], pair, store)

    loop(6, short_attend)


ERFC = (
    -1.26551223, 1.00002368, 0.37409196, 0.09678418, -0.18628806,
    0.27886807, -1.13520398, 1.48851587, -0.82215223, 0.17087277,
)


def gelu_parts(hidden):
    z = jnp.abs(hidden) * 0.7071067811865476
    t = 1.0 / (1.0 + 0.5 * z)
    series = jnp.full_like(z, ERFC[-1])
    for coefficient in ERFC[-2::-1]:
        series = series * t + coefficient
    square = z * z
    tail = 0.5 * t * jnp.exp(series - square)
    cdf = jnp.where(hidden < 0.0, tail, 1.0 - tail)
    return cdf, jnp.exp(-square) * 0.3989422804014327


def ffn_both(
    place, llen, slen, xm, ctx, vec, cl, cs, p0, p1, p2, p3, p4, p5, p6, p7,
    ol, os, ga, gone, gctx, gvec,
    wo, wi, wu, res, xhat, grouped, gffn, active, slope, ffn, rstd, acc, ghid, gproj, sems,
):
    def fetch(part):
        for core, pieces in enumerate(((p0, p1, p2, p3), (p4, p5, p6, p7))):
            for chip, piece in enumerate(pieces):
                slot = slot_of(place[0], core, chip)
                g, r = slot >> 2, slot & 3

                def one(k):
                    n = place[1] ^ k
                    if part == 0:
                        rows = pl.ds(pl.multiple_of(192 * n + 48 * r, 48), 48)
                        source, target = pl.ds(192, 48), wo.at[g, rows, :]
                    elif part == 1:
                        source, target = pl.ds(0, 96), wi.at[slot, at(n, 96), :]
                    else:
                        source, target = pl.ds(96, 96), wu.at[4 * g + n, at(r, 96), :]
                    pltpu.make_async_copy(piece.at[k, source, :], target, sems.at[part]).start()

                loop(4, one)

    for part in range(3):
        fetch(part)
    gain_one, bias_one = vec[16:17, :], vec[17:18, :]
    gain_two, bias_two = vec[18:19, :], vec[19:20, :]
    gvec[...] = jnp.zeros((8, D), F32)

    pltpu.make_async_copy(wo, wo, sems.at[0]).wait()

    def mix(i):
        rows = at(i, 256)
        for c in range(2):
            lanes = slice(AH * c, AH * c + AH)
            res[rows, lanes] = nn(ctx[rows, :], wo[c]) + xm[rows, lanes].astype(F32)

    loop(3, mix)

    def norm_one(i):
        rows = at(i, 64)
        values = res[rows, :]
        center = values - jnp.mean(values, axis=1, keepdims=True)
        scale = lax.rsqrt(jnp.mean(center * center, axis=1, keepdims=True) + EPS)
        hat = center * scale
        first = hat * gain_one + bias_one
        xhat[rows, :] = hat
        rstd[rows, :] = jnp.broadcast_to(scale, (64, 128))
        res[rows, :] = first
        short = first.astype(BF)
        grouped[0, rows, :] = short[:, 0:AH]
        grouped[1, rows, :] = short[:, AH:D]

    loop(12, norm_one)
    ffn[...] = jnp.zeros((2, ROWS, AH), F32)
    pltpu.make_async_copy(wi, wi, sems.at[1]).wait()
    pltpu.make_async_copy(wu, wu, sems.at[2]).wait()

    def expand(b):
        acc[...] = nn(grouped[b >> 2], wi[b])

        def act(i):
            rows = at(i, 64)
            hidden = acc[rows, :]
            cdf, density = gelu_parts(hidden)
            active[b, rows, :] = (hidden * cdf).astype(BF)
            slope[b, rows, :] = cdf + hidden * density

        loop(12, act)
        ffn[b >> 2] += nn(active[b], wu[b])

    loop(8, expand)

    def norm_two(cot, out, offset):
        def run(i):
            rows = at(i, 64)
            whole = pl.ds(pl.multiple_of(offset + i * 64, 64), 64)
            values = jnp.concatenate([ffn[0, whole, :], ffn[1, whole, :]], axis=1) + res[whole, :]
            center = values - jnp.mean(values, axis=1, keepdims=True)
            scale = lax.rsqrt(jnp.mean(center * center, axis=1, keepdims=True) + EPS)
            hat = center * scale
            out[rows, :] = (hat * gain_two + bias_two).astype(BF)
            if offset:
                limit, base = slen[i >> 1], (i & 1) * 64
            else:
                limit, base = llen[0], i * 64
            live = base + iota((64, D), 0) < limit
            up = jnp.where(live, cot[rows, :].astype(F32), 0.0)
            gvec[2:3, :] += jnp.sum(up * hat, axis=0, keepdims=True)
            gvec[3:4, :] += jnp.sum(up, axis=0, keepdims=True)
            up = up * gain_two
            grad = scale * (
                up
                - jnp.mean(up, axis=1, keepdims=True)
                - hat * jnp.mean(up * hat, axis=1, keepdims=True)
            )
            res[whole, :] = grad
            short = grad.astype(BF)
            gffn[0, whole, :] = short[:, 0:AH]
            gffn[1, whole, :] = short[:, AH:D]

        return run

    loop(8, norm_two(cl, ol, 0))
    loop(4, norm_two(cs, os, LONG))
    ffn[...] = jnp.zeros((2, ROWS, AH), F32)

    def contract(b):
        g, n = b >> 2, b & 3
        acc[...] = nt(gffn[g], wu[b])

        def act(i):
            rows = at(i, 64)
            ghid[rows, :] = (acc[rows, :] * slope[b, rows, :]).astype(BF)

        loop(12, act)
        part = tn(active[b], gffn[g]).astype(BF)
        for w in range(4):
            ga[(4 * g + w) ^ place[0], n ^ place[1], 96:192, :] = part[96 * w : 96 * w + 96, :]
        part = tn(grouped[g], ghid[...]).astype(BF)
        for m in range(4):
            ga[b ^ place[0], m ^ place[1], 0:96, :] = part[96 * m : 96 * m + 96, :]
        ffn[g] += nt(ghid[...], wi[b])

    loop(8, contract)

    def norm_one_back(i):
        rows = at(i, 64)
        up = res[rows, :] + jnp.concatenate([ffn[0, rows, :], ffn[1, rows, :]], axis=1)
        hat = xhat[rows, :]
        gvec[0:1, :] += jnp.sum(up * hat, axis=0, keepdims=True)
        gvec[1:2, :] += jnp.sum(up, axis=0, keepdims=True)
        up = up * gain_one
        grad = rstd[rows, 0:1] * (
            up
            - jnp.mean(up, axis=1, keepdims=True)
            - hat * jnp.mean(up * hat, axis=1, keepdims=True)
        )
        gone[rows, :] = grad
        gproj[rows, :] = grad.astype(BF)

    loop(12, norm_one_back)
    for c in range(2):
        part = tn(ctx[...], gproj[:, AH * c : AH * c + AH]).astype(BF)
        for n in range(4):
            for r in range(4):
                row = 192 * n + 48 * r
                ga[(4 * c + r) ^ place[0], n ^ place[1], 192:240, :] = part[row : row + 48, :]

    def unmix(i):
        rows = at(i, 256)
        part = nt(gproj[rows, 0:AH], wo[0]) + nt(gproj[rows, AH:D], wo[1])
        gctx[rows, :] = part.astype(BF)

    loop(3, unmix)


def mixer_backward(
    place, llen, slen, xm, packed, plong, pshort, dw, kc, cq, kp, cv, vec, gone, gctx, gvec, wm,
    il, is_, gb,
    xpad, gcp, gdp, grads, gqc, dkv, gkc, glog, gdep, spread, gather, wk,
):
    zero_gaps(xpad)
    zero_gaps(gcp)
    zero_gaps(gdp)
    for start, rows, pstart in SEGS:
        xpad[pstart : pstart + rows, :] = xm[start : start + rows, :].astype(F32)
        gcp[pstart : pstart + rows, :] = gctx[start : start + rows, AH:D].astype(F32)
    spread[...] = head_spread()
    gather[...] = head_gather()
    wk[...] = tap_kernel(wm)
    gdep[...] = jnp.zeros((8 * TAPS, D), F32)

    def dynamic(i):
        rows = at(i, 128)
        ps = padded_start(i)
        wide = pl.ds(pl.multiple_of(ps - 8, 8), 144)
        taps = kp[wide, :]
        grad_wide = gcp[wide, :]
        values = cv[wide, :]
        grad = gcp[pl.ds(ps, 128), :]
        total = jnp.zeros((128, AH), F32)
        gprob = jnp.zeros((128, 128), F32)
        for j in range(TAPS):
            moved = taps if j == 0 else pltpu.roll(taps, 128 - 8 * j, 1)
            part = nn(split_two(moved), spread[...]) * grad_wide
            total = total + part[12 - j : 140 - j, :]
            part = nn((grad * values[4 + j : 132 + j, :]).astype(BF), gather[...])
            gprob = gprob + (part if j == 0 else pltpu.roll(part, 8 * j, 1))
        grads[rows, 3 * AH : 4 * AH] = total.astype(BF)
        probs = kp[pl.ds(ps, 128), :]
        inner = probs * gprob
        for shift in (64, 32, 16, 8):
            inner = inner + pltpu.roll(inner, shift, 1)
        glogits = (probs * (gprob - inner)).astype(BF)
        glog[rows, :] = glogits
        gquery = nt(glogits, wk[...])
        gkc[rows, :] = (gquery * packed[rows, 0:AH].astype(F32)).astype(BF)
        gqc[rows, :] = gquery * kc[rows, :]

    loop(6, dynamic)

    def point_back(c):
        part = nt(gkc[:, 0:256], wm[6, at(c, 256), :])
        part = part + nt(gkc[:, 256:384], wm[7, at(c, 256), 0:128])
        part = part.astype(BF).astype(F32)
        for start, rows, pstart in SEGS:
            gdp[pstart : pstart + rows, at(c, 256)] = part[start : start + rows, :]

    loop(3, point_back)

    def depth(i):
        ps = padded_start(i)
        wide = pl.ds(pl.multiple_of(ps - 8, 8), 144)
        for c in range(3):
            lanes = slice(256 * c, 256 * c + 256)
            tokens = xpad[wide, lanes]
            grad_wide = gdp[wide, lanes]
            grad = gdp[pl.ds(ps, 128), lanes]
            total = gone[at(i, 128), lanes]
            for j in range(TAPS):
                total = total + vec[j : j + 1, lanes] * grad_wide[12 - j : 140 - j, :]
                part = tokens[4 + j : 132 + j, :] * grad
                gdep[8 * j : 8 * j + 8, lanes] += jnp.sum(part.reshape(16, 8, 256), axis=0)
            gone[at(i, 128), lanes] = total

    loop(6, depth)

    def attend(row0, nq, key0, nk, pair, load, first):
        queries = packed[pl.ds(row0, nq), at(pair, 128)].astype(F32)
        keys = packed[pl.ds(key0, nk), pl.ds(pl.multiple_of(AH + pair * 128, 128), 128)]
        vals = packed[pl.ds(key0, nk), pl.ds(pl.multiple_of(2 * AH + pair * 128, 128), 128)]
        up = gctx[pl.ds(row0, nq), at(pair, 128)].astype(F32)
        lane = iota((nq, 128), 1)
        outs = []
        gkeys = jnp.zeros((nk, 128), F32)
        gvals = jnp.zeros((nk, 128), F32)
        for hh in range(2):
            mine = (lane >> 6) == hh
            query = jnp.where(mine, queries, 0.0).astype(BF)
            upper = jnp.where(mine, up, 0.0).astype(BF)
            probs_low = load(hh)
            probs = probs_low.astype(F32)
            gprobs = nt(upper, vals)
            inner = jnp.sum(probs * gprobs, axis=1, keepdims=True)
            gscores = (probs * (gprobs - inner)).astype(BF)
            outs.append(nn(gscores, keys))
            gkeys = gkeys + tn(gscores, query)
            gvals = gvals + tn(probs_low, upper)
        both = jnp.where(lane < 64, outs[0], outs[1]) * 0.125
        both = both + gqc[pl.ds(row0, nq), at(pair, 128)]
        grads[pl.ds(row0, nq), at(pair, 128)] = both.astype(BF)
        span = pl.ds(key0, nk)
        if first:
            dkv[0, span, at(pair, 128)] = gkeys
            dkv[1, span, at(pair, 128)] = gvals
        else:
            dkv[0, span, at(pair, 128)] += gkeys
            dkv[1, span, at(pair, 128)] += gvals

    def long_attend(pair):
        for block in range(2):
            attend(
                256 * block, 256, 0, LONG, pair,
                lambda hh: plong[2 * pair + hh, 256 * block : 256 * block + 256, :],
                block == 0,
            )

    loop(3, long_attend)

    def short_attend(i):
        seg = jnp.where(i >= 3, 1, 0)
        pair = i - 3 * seg
        row0 = pl.multiple_of(LONG + 128 * seg, 128)
        attend(row0, 128, row0, SHORT, pair, lambda hh: pshort[seg, 2 * pair + hh, :, :], True)

    loop(6, short_attend)

    def pack(i):
        rows = at(i, 128)
        grads[rows, AH : 2 * AH] = (dkv[0, rows, :] * 0.125).astype(BF)
        grads[rows, 2 * AH : 3 * AH] = dkv[1, rows, :].astype(BF)

    loop(6, pack)

    def spill(b, values, lanes):
        for n in range(4):
            gb[b ^ place[0], n ^ place[1], :, lanes] = values[192 * n : 192 * n + 192, :]

    def weights(b):
        spill(b, tn(xm[...], grads[:, at(b, 256)]).astype(BF), slice(0, 256))

    loop(6, weights)
    spill(6, tn(dw[...], gkc[:, 0:256]).astype(BF), slice(0, 256))
    spill(7, tn(dw[...], gkc[:, 256:384]).astype(BF), slice(0, 128))
    taps = [jnp.sum(gdep[8 * j : 8 * j + 8, :], axis=0, keepdims=True) for j in range(TAPS)]
    table = jnp.concatenate(
        taps + [jnp.zeros((7, D), F32), gvec[...], jnp.zeros((104, D), F32)], axis=0
    ).astype(BF)
    misc = tn(table, eye(128, BF))
    gkernel = nt(tn(cq[...], glog[...]).astype(BF), tap_permutation())
    parts = []
    for n in range(4):
        row = 192 * n
        parts.append(misc[row : row + 96, :] + gkernel[96 * n : 96 * n + 96, :])
        parts.append(misc[row + 96 : row + 192, :])
    spill(7, jnp.concatenate(parts, axis=0).astype(BF), slice(128, 256))

    def inputs(i):
        rows = at(i, 256)
        total = gone[rows, :]
        for b in range(6):
            total = total + nt(grads[rows, 256 * b : 256 * b + 256], wm[b])
        return total

    def inputs_long(i):
        live = i * 256 + iota((256, D), 0) < llen[0]
        il[at(i, 256), :] = jnp.where(live, inputs(i), 0.0).astype(BF)

    loop(2, inputs_long)
    total = inputs(2)
    row = iota((128, D), 0)
    for seg in range(2):
        part = total[128 * seg : 128 * seg + 128, :]
        is_[128 * seg : 128 * seg + 128, :] = jnp.where(row < slen[seg], part, 0.0).astype(BF)


def pack(
    place, qkv, depth, point, kernel, convout, g1, b1, inner, outer, out, g2, b2, mixer, ffn
):
    for w in range(SLOTS):

        @pl.when(place[0] == w)
        def _():
            g, r = w // 4, w % 4
            ffn[0:96, :] = inner[g, :, AH * r : AH * r + AH]
            ffn[96:192, :] = outer[g, 96 * r : 96 * r + 96, :]
            ffn[192:240, :] = out[48 * r : 48 * r + 48, AH * g : AH * g + AH]
            if w < 4:
                mixer[...] = qkv[:, 256 * w : 256 * w + 256]
            elif w == 4:
                mixer[:, 0:128] = qkv[:, 1024:1152]
                mixer[:, 128:256] = convout[:, 0:128]
            elif w == 5:
                mixer[...] = convout[:, 128:384]
            elif w == 6:
                mixer[...] = point[:, 0:256]
            else:
                mixer[:, 0:128] = point[:, 256:384]
                rows = [v[...].astype(F32).reshape(1, 192) for v in (g1, b1, g2, b2)]
                table = jnp.concatenate(
                    [depth[...].astype(F32), jnp.zeros((7, 192), F32)]
                    + rows
                    + [jnp.zeros((108, 192), F32)],
                    axis=0,
                )
                left = tn(table.astype(BF), eye(128, BF))
                row, col = iota((54, 128), 0), iota((54, 128), 1)
                right = nn(kernel[...], jnp.where(col == row + 64, 1.0, 0.0).astype(BF))
                mixer[0:96, 128:256] = (left[0:96, :] + right).astype(BF)
                mixer[96:192, 128:256] = left[96:192, :].astype(BF)


def unpack_ffn(packed, inner, outer, out):
    for w in range(SLOTS):
        g, r = w // 4, w % 4
        inner[g, :, AH * r : AH * r + AH] = packed[w, 0:96, :].astype(F32)
        outer[g, 96 * r : 96 * r + 96, :] = packed[w, 96:192, :].astype(F32)
        out[48 * r : 48 * r + 48, AH * g : AH * g + AH] = packed[w, 192:240, :].astype(F32)


def unpack_mixer(packed, qkv, depth, point, kernel, convout, g1, b1, g2, b2):
    for w in range(4):
        qkv[:, 256 * w : 256 * w + 256] = packed[w].astype(F32)
    qkv[:, 1024:1152] = packed[4, :, 0:128].astype(F32)
    convout[:, 0:128] = packed[4, :, 128:256].astype(F32)
    convout[:, 128:384] = packed[5].astype(F32)
    point[:, 0:256] = packed[6].astype(F32)
    point[:, 256:384] = packed[7, :, 0:128].astype(F32)
    misc = packed[7, :, 128:256]
    table = nt(eye(128, BF), misc)
    depth[...] = table[0:TAPS, :]
    for k, ref in enumerate((g1, b1, g2, b2)):
        ref[...] = table[16 + k : 17 + k, :].reshape(192)
    row, col = iota((128, 54), 0), iota((128, 54), 1)
    kernel[...] = nn(misc[0:96, :], jnp.where(row == col + 64, 1.0, 0.0).astype(BF))


SMEM = pl.BlockSpec(memory_space=pltpu.SMEM)
VMEM = pl.BlockSpec(memory_space=pltpu.VMEM)
ANY = pl.BlockSpec(memory_space=pl.ANY)


def call(kernel, specs, outs, scratch, flops, *args):
    return pl.pallas_call(
        kernel,
        out_shape=[jax.ShapeDtypeStruct(s, d) for s, d in outs],
        in_specs=specs,
        out_specs=[VMEM] * len(outs),
        scratch_shapes=[pltpu.VMEM(s, d) for s, d in scratch[0]] + list(scratch[1:]),
        compiler_params=pltpu.CompilerParams(vmem_limit_bytes=60 << 20),
        cost_estimate=pl.CostEstimate(flops=flops, bytes_accessed=1 << 20, transcendentals=0),
        name=kernel.__name__,
    )(*args)


def forward_mixer(scalars, xl, xs, pieces):
    outs = [
        ((ROWS, D), BF), ((ROWS, 3 * AH), BF),
        ((HEADS, LONG, LONG), BF), ((2, HEADS, SHORT, SHORT), BF),
        ((ROWS, D), BF), ((ROWS, AH), F32), ((ROWS, AH), BF), ((PAD, 128), F32),
        ((PAD, AH), F32), ((ROWS, D), BF), ((24, D), F32), ((SLOTS, D, 256), BF),
    ]
    scratch = [((PAD, D), F32), ((256, AH), BF), ((AH, 128), BF)]
    return call(
        mixer_forward, [SMEM] * 3 + [VMEM] * 2 + [ANY] * 8, outs,
        (scratch, pltpu.SemaphoreType.DMA), 30 * 10**9, *scalars, xl, xs, *pieces,
    )


def feed_forward(scalars, xm, ctx, vec, cl, cs, pieces):
    outs = [
        ((LONG, D), BF), ((2 * SHORT, D), BF), ((SLOTS, 4, 240, AH), BF),
        ((ROWS, D), F32), ((ROWS, D), BF), ((8, D), F32),
    ]
    scratch = [
        ((2, D, AH), BF), ((8, AH, AH), BF), ((8, AH, AH), BF), ((ROWS, D), F32), ((ROWS, D), F32),
        ((2, ROWS, AH), BF), ((2, ROWS, AH), BF), ((8, ROWS, AH), BF), ((8, ROWS, AH), F32),
        ((2, ROWS, AH), F32), ((ROWS, 128), F32), ((ROWS, AH), F32), ((ROWS, AH), BF),
        ((ROWS, D), BF),
    ]
    return call(
        ffn_both, [SMEM] * 3 + [VMEM] * 5 + [ANY] * 8, outs,
        (scratch, pltpu.SemaphoreType.DMA((3,))), 60 * 10**9,
        *scalars, xm, ctx, vec, cl, cs, *pieces,
    )


def backward_mixer(scalars, *args):
    outs = [((LONG, D), BF), ((2 * SHORT, D), BF), ((SLOTS, 4, 192, 256), BF)]
    scratch = [
        ((PAD, D), F32), ((PAD, AH), F32), ((PAD, D), F32), ((ROWS, 4 * AH), BF),
        ((ROWS, AH), F32), ((2, ROWS, AH), F32), ((ROWS, AH), BF), ((ROWS, 128), BF),
        ((8 * TAPS, D), F32), ((256, AH), BF), ((AH, 128), BF), ((AH, 128), BF),
    ]
    return call(
        mixer_backward, [SMEM] * 3 + [VMEM] * len(args), outs, (scratch,), 40 * 10**9,
        *scalars, *args,
    )


def far(values, bit):
    return lax.ppermute(values, "narrow", [(i, i ^ bit) for i in range(4)])


def near(values, bit):
    return lax.ppermute(values, "wide", [(i, i ^ bit) for i in range(SLOTS)])


def gather_narrow(piece):
    return jnp.stack([piece] + [far(piece, k) for k in (1, 2, 3)])


def gather_chips(block):
    return [block] + [near(block, k) for k in (2, 4, 6)]


def gather_cores(blocks):
    return blocks + [near(block, 1) for block in blocks]


def total(first, others):
    result = first.astype(F32)
    for other in others:
        result = result + other.astype(F32)
    return result.astype(BF)


def reduce_cores(parts):
    parts = parts.reshape((4, 2) + parts.shape[1:])
    return total(parts[:, 0], [near(parts[:, 1], 1)])


def reduce_chips(parts):
    return total(parts[0], [near(parts[k], 2 * k) for k in (1, 2, 3)])


def reduce_narrow(parts):
    parts = total(parts[0], [far(parts[k], k) for k in (1, 2, 3)])
    return lax.psum(parts, "hi")


def gather_wide(parts):
    return lax.all_gather(parts, "wide", axis=0, tiled=False)


def body(
    long_tokens, long_lengths, short_tokens, short_lengths,
    w_qkv, w_depth, w_point, w_kernel, w_convout, w_out, norm1_gain, norm1_bias,
    w_inner, w_outer, norm2_gain, norm2_bias, long_cotangent, short_cotangent,
):
    place = jnp.stack([lax.axis_index("wide"), lax.axis_index("narrow")]).astype(jnp.int32)
    scalars = (place, long_lengths, short_lengths)
    xl, xs = long_tokens.reshape(LONG, D), short_tokens.reshape(2 * SHORT, D)
    cl, cs = long_cotangent.reshape(LONG, D), short_cotangent.reshape(2 * SHORT, D)
    mixer, ffn = call(
        pack, [SMEM] + [VMEM] * 12, [((192, 256), BF), ((240, AH), BF)], ([],), 10**9,
        place, w_qkv, w_depth, w_point, w_kernel, w_convout, norm1_gain, norm1_bias,
        w_inner, w_outer, w_out, norm2_gain, norm2_bias,
    )
    mixer = gather_narrow(mixer)
    mixer, ffn = lax.optimization_barrier((mixer, ffn))
    mixer = gather_chips(mixer)
    ffn = gather_narrow(ffn)
    mixer, ffn = lax.optimization_barrier((mixer, ffn))
    mixer = gather_cores(mixer)
    ffn = gather_chips(ffn)
    xm, packed, plong, pshort, dw, kc, cq, kp, cv, ctx, vec, wm = forward_mixer(
        scalars, xl, xs, mixer
    )
    ffn = gather_cores(ffn)
    ol, os, ga, gone, gctx, gvec = feed_forward(scalars, xm, ctx, vec, cl, cs, ffn)
    ga = reduce_cores(ga)
    il, is_, gb = backward_mixer(
        scalars, xm, packed, plong, pshort, dw, kc, cq, kp, cv, vec, gone, gctx, gvec, wm
    )
    ga = reduce_narrow(reduce_chips(ga))
    gb = reduce_narrow(reduce_chips(reduce_cores(gb)))
    inner, outer, out = call(
        unpack_ffn, [VMEM], [((2, 96, 4 * AH), F32), ((2, AH, AH), F32), ((192, D), F32)],
        ([],), 10**9, gather_wide(ga),
    )
    outs = [
        ((192, 3 * AH), F32), ((TAPS, 192), F32), ((192, AH), F32), ((96, 54), F32), ((192, AH), F32),
    ] + [((192,), F32)] * 4
    qkv, depth, point, kernel, convout, g1, b1, g2, b2 = call(
        unpack_mixer, [VMEM], outs, ([],), 10**9, gather_wide(gb)
    )
    return (
        ol.reshape(long_tokens.shape), os.reshape(short_tokens.shape),
        il.reshape(long_tokens.shape), is_.reshape(short_tokens.shape),
        qkv, depth, point, kernel, convout, out, g1, b1, inner, outer, g2, b2,
    )


def solution(mesh):
    wide, narrow = mesh.shape["wide"], mesh.shape["narrow"]
    inner_mesh = Mesh(mesh.devices.reshape(wide // SLOTS, SLOTS, narrow), ("hi", "wide", "narrow"))
    every = ("hi", "wide", "narrow")
    rows = P(every, None, None)
    weights = (
        P("narrow", None), P(None, "narrow"), P("narrow", None), P("narrow", None),
        P("narrow", None), P("narrow", None), P("narrow"), P("narrow"),
        P(None, "narrow", None), P(None, "narrow", None), P("narrow"), P("narrow"),
    )
    return jax.shard_map(
        body,
        mesh=inner_mesh,
        in_specs=(rows, P(every), rows, P(every)) + weights + (rows, rows),
        out_specs=(rows, rows, rows, rows) + weights,
        check_vma=False,
    )
```

```python
import jax
import jax.numpy as jnp
from jax import lax
from jax.experimental import pallas as pl
from jax.experimental.pallas import tpu as pltpu
from jax.sharding import Mesh
from jax.sharding import PartitionSpec as P

BF = jnp.bfloat16
F32 = jnp.float32
EPS = 1e-12
D = 768
AH = 384
HEADS = 6
TAPS = 9
LONG = 512
SHORT = 128
ROWS = 768
PAD = 800
SLOTS = 8
NEG = -1000000000.0
PSTART = tuple(8 + 128 * i + 8 * max(i - 3, 0) for i in range(6))
SEGS = ((0, 512, 8), (512, 128, 528), (640, 128, 664))


def nn(a, b):
    return lax.dot_general(a, b, (((1,), (0,)), ((), ())), preferred_element_type=F32)


def nt(a, b):
    return lax.dot_general(a, b, (((1,), (1,)), ((), ())), preferred_element_type=F32)


def tn(a, b):
    return lax.dot_general(a, b, (((0,), (0,)), ((), ())), preferred_element_type=F32)


def iota(shape, axis):
    return lax.broadcasted_iota(jnp.int32, shape, axis)


def loop(count, body):
    def step(i, carry):
        body(i)
        return carry

    lax.fori_loop(0, count, step, 0)


def at(i, size):
    if isinstance(i, int):
        return pl.ds(i * size, size)
    return pl.ds(pl.multiple_of(i * size, size), size)


def padded_start(i):
    return pl.multiple_of(8 + 128 * i + 8 * jnp.maximum(i - 3, 0), 8)


def zero_gaps(ref):
    for start in (0, 520, 656, 792):
        ref[start : start + 8, :] = jnp.zeros((8, ref.shape[1]), ref.dtype)


def eye(n, dtype):
    return jnp.where(iota((n, n), 0) == iota((n, n), 1), 1.0, 0.0).astype(dtype)


def tap_permutation():
    row, col = iota((128, 128), 0), iota((128, 128), 1)
    head, tap = col & 7, col >> 3
    keep = (head < HEADS) & (tap < TAPS) & (row == 64 + head * TAPS + tap)
    return jnp.where(keep, 1.0, 0.0).astype(BF)


def head_spread():
    row, col = iota((256, AH), 0), iota((256, AH), 1)
    return jnp.where((row & 127) == (col >> 6), 1.0, 0.0).astype(BF)


def head_gather():
    row, col = iota((AH, 128), 0), iota((AH, 128), 1)
    return jnp.where((row >> 6) == col, 1.0, 0.0).astype(BF)


def split_two(values):
    high = values.astype(BF)
    low = (values - high.astype(F32)).astype(BF)
    return jnp.concatenate([high, low], axis=1)


def tap_kernel(wm):
    stored = jnp.concatenate([wm[7, 192 * n : 192 * n + 96, 128:256] for n in range(4)], axis=0)
    return nn(stored, tap_permutation()).astype(BF)


def slot_of(where, core, chip):
    return 2 * ((where >> 1) ^ chip) + ((where & 1) ^ core)


def store_relative(keep, send, place, slot, shard, rows, lanes, values):
    where = slot ^ place[0]
    chip, far_off = where >> 1, shard ^ place[1]

    @pl.when((where & 1) == 0)
    def _():
        keep[chip, far_off, rows, lanes] = values

    @pl.when((where & 1) == 1)
    def _():
        send[chip, far_off, rows, lanes] = values


def mixer_forward(
    place, llen, slen, xl, xs, p0, p1, p2, p3, p4, p5, p6, p7,
    xm, packed, plong, pshort, dw, kc, cq, kp, cv, ctx, vec, wm, xpad, spread, wk, sem
):
    for core, pieces in enumerate(((p0, p1, p2, p3), (p4, p5, p6, p7))):
        for chip, piece in enumerate(pieces):
            slot = slot_of(place[0], core, chip)

            def fetch(k):
                rows = pl.ds(pl.multiple_of((place[1] ^ k) * 192, 192), 192)
                pltpu.make_async_copy(piece.at[k], wm.at[slot, rows, :], sem).start()

            loop(4, fetch)
    lens = (llen[0], slen[0], slen[1])
    zero_gaps(xpad)
    zero_gaps(cv)
    zero_gaps(kp)
    for i in range(6):
        seg = max(i - 3, 0)
        base = 128 * i if i < 4 else 0
        tokens = xl[128 * i : 128 * i + 128, :] if i < 4 else xs[128 * (i - 4) : 128 * (i - 3), :]
        live = base + iota((128, D), 0) < lens[seg]
        values = jnp.where(live, tokens.astype(F32), 0.0)
        xpad[PSTART[i] : PSTART[i] + 128, :] = values
        xm[128 * i : 128 * i + 128, :] = values.astype(BF)
    spread[...] = head_spread()
    pltpu.make_async_copy(wm, wm, sem).wait()
    vec[...] = nt(eye(128, BF), wm[7, :, 128:256])[0:24, :]
    wk[...] = tap_kernel(wm)

    def project(b):
        packed[:, at(b, 256)] = nn(xm[...], wm[b]).astype(BF)

    loop(4, project)
    part = nn(xm[...], wm[4])
    packed[:, 1024:1152] = part[:, 0:128].astype(BF)
    for start, rows, pstart in SEGS:
        cv[pstart : pstart + rows, 0:128] = part[start : start + rows, 128:256]
    part = nn(xm[...], wm[5])
    for start, rows, pstart in SEGS:
        cv[pstart : pstart + rows, 128:384] = part[start : start + rows, :]

    def depth(i):
        ps = padded_start(i)
        for c in range(3):
            lanes = slice(256 * c, 256 * c + 256)
            window = xpad[pl.ds(pl.multiple_of(ps - 8, 8), 144), lanes]
            total = jnp.zeros((128, 256), F32)
            for j in range(TAPS):
                total = total + vec[j : j + 1, lanes] * window[4 + j : 132 + j, :]
            dw[at(i, 128), lanes] = total.astype(BF)

    loop(6, depth)
    kc[:, 0:256] = nn(dw[...], wm[6])
    kc[:, 256:384] = nn(dw[...], wm[7, :, 0:128])

    def dynamic(i):
        rows = at(i, 128)
        ps = padded_start(i)
        query = (kc[rows, :] * packed[rows, 0:AH].astype(F32)).astype(BF)
        cq[rows, :] = query
        logits = nn(query, wk[...])
        lane = iota((128, 128), 1)
        real = lane < 8 * TAPS
        top = jnp.where(real, logits, NEG * 1e20)
        for shift in (64, 32, 16, 8):
            top = jnp.maximum(top, pltpu.roll(top, shift, 1))
        ex = jnp.where(real, jnp.exp(logits - top), 0.0)
        total = ex
        for shift in (64, 32, 16, 8):
            total = total + pltpu.roll(total, shift, 1)
        probs = ex / total
        kp[pl.ds(ps, 128), :] = probs
        window = cv[pl.ds(pl.multiple_of(ps - 8, 8), 144), :]
        out = jnp.zeros((128, AH), F32)
        for j in range(TAPS):
            moved = probs if j == 0 else pltpu.roll(probs, 128 - 8 * j, 1)
            out = out + nn(split_two(moved), spread[...]) * window[4 + j : 132 + j, :]
        ctx[rows, AH:D] = out.astype(BF)

    loop(6, dynamic)

    def attend(row0, nq, key0, nk, limit, pair, store):
        queries = packed[pl.ds(row0, nq), at(pair, 128)].astype(F32)
        keys = packed[pl.ds(key0, nk), pl.ds(pl.multiple_of(AH + pair * 128, 128), 128)]
        vals = packed[pl.ds(key0, nk), pl.ds(pl.multiple_of(2 * AH + pair * 128, 128), 128)]
        lane = iota((nq, 128), 1)
        outs = []
        for hh in range(2):
            mine = (lane >> 6) == hh
            scores = nt(jnp.where(mine, queries, 0.0).astype(BF), keys) * 0.125
            scores = jnp.where(iota((nq, nk), 1) < limit, scores, NEG)
            ex = jnp.exp(scores - jnp.max(scores, axis=1, keepdims=True))
            probs = (ex / jnp.sum(ex, axis=1, keepdims=True)).astype(BF)
            store(hh, probs)
            outs.append(nn(probs, vals))
        both = jnp.where(lane < 64, outs[0], outs[1])
        ctx[pl.ds(row0, nq), at(pair, 128)] = both.astype(BF)

    def long_attend(i):
        pair, block = i >> 1, i & 1
        row0 = pl.multiple_of(block * 256, 256)

        def store(hh, probs):
            plong[2 * pair + hh, pl.ds(row0, 256), :] = probs

        attend(row0, 256, 0, LONG, lens[0], pair, store)

    loop(6, long_attend)

    def short_attend(i):
        seg = jnp.where(i >= 3, 1, 0)
        pair = i - 3 * seg
        row0 = pl.multiple_of(LONG + 128 * seg, 128)

        def store(hh, probs):
            pshort[seg, 2 * pair + hh, :, :] = probs

        attend(row0, 128, row0, SHORT, slen[seg], pair, store)

    loop(6, short_attend)


ERFC = (
    -1.26551223, 1.00002368, 0.37409196, 0.09678418, -0.18628806,
    0.27886807, -1.13520398, 1.48851587, -0.82215223, 0.17087277,
)


def gelu_parts(hidden):
    z = jnp.abs(hidden) * 0.7071067811865476
    t = 1.0 / (1.0 + 0.5 * z)
    series = jnp.full_like(z, ERFC[-1])
    for coefficient in ERFC[-2::-1]:
        series = series * t + coefficient
    square = z * z
    tail = 0.5 * t * jnp.exp(series - square)
    cdf = jnp.where(hidden < 0.0, tail, 1.0 - tail)
    return cdf, jnp.exp(-square) * 0.3989422804014327


def ffn_both(
    place, llen, slen, xm, ctx, vec, cl, cs, p0, p1, p2, p3, p4, p5, p6, p7,
    ol, os, keep, send, gone, gctx, gvec,
    wo, wi, wu, res, xhat, grouped, gffn, active, slope, ffn, rstd, acc, ghid, gproj, sems,
):
    def fetch(part):
        for core, pieces in enumerate(((p0, p1, p2, p3), (p4, p5, p6, p7))):
            for chip, piece in enumerate(pieces):
                slot = slot_of(place[0], core, chip)
                g, r = slot >> 2, slot & 3

                def one(k):
                    n = place[1] ^ k
                    if part == 0:
                        rows = pl.ds(pl.multiple_of(192 * n + 48 * r, 48), 48)
                        source, target = pl.ds(192, 48), wo.at[g, rows, :]
                    elif part == 1:
                        source, target = pl.ds(0, 96), wi.at[slot, at(n, 96), :]
                    else:
                        source, target = pl.ds(96, 96), wu.at[4 * g + n, at(r, 96), :]
                    pltpu.make_async_copy(piece.at[k, source, :], target, sems.at[part]).start()

                loop(4, one)

    for part in range(3):
        fetch(part)

    def put(slot, shard, rows, values):
        store_relative(keep, send, place, slot, shard, rows, slice(None), values)

    gain_one, bias_one = vec[16:17, :], vec[17:18, :]
    gain_two, bias_two = vec[18:19, :], vec[19:20, :]
    gvec[...] = jnp.zeros((8, D), F32)

    pltpu.make_async_copy(wo, wo, sems.at[0]).wait()

    def mix(i):
        rows = at(i, 256)
        for c in range(2):
            lanes = slice(AH * c, AH * c + AH)
            res[rows, lanes] = nn(ctx[rows, :], wo[c]) + xm[rows, lanes].astype(F32)

    loop(3, mix)

    def norm_one(i):
        rows = at(i, 64)
        values = res[rows, :]
        center = values - jnp.mean(values, axis=1, keepdims=True)
        scale = lax.rsqrt(jnp.mean(center * center, axis=1, keepdims=True) + EPS)
        hat = center * scale
        first = hat * gain_one + bias_one
        xhat[rows, :] = hat
        rstd[rows, :] = jnp.broadcast_to(scale, (64, 128))
        res[rows, :] = first
        short = first.astype(BF)
        grouped[0, rows, :] = short[:, 0:AH]
        grouped[1, rows, :] = short[:, AH:D]

    loop(12, norm_one)
    ffn[...] = jnp.zeros((2, ROWS, AH), F32)
    pltpu.make_async_copy(wi, wi, sems.at[1]).wait()
    pltpu.make_async_copy(wu, wu, sems.at[2]).wait()

    def expand(b):
        acc[...] = nn(grouped[b >> 2], wi[b])

        def act(i):
            rows = at(i, 64)
            hidden = acc[rows, :]
            cdf, density = gelu_parts(hidden)
            active[b, rows, :] = (hidden * cdf).astype(BF)
            slope[b, rows, :] = cdf + hidden * density

        loop(12, act)
        ffn[b >> 2] += nn(active[b], wu[b])

    loop(8, expand)

    def norm_two(cot, out, offset):
        def run(i):
            rows = at(i, 64)
            whole = pl.ds(pl.multiple_of(offset + i * 64, 64), 64)
            values = jnp.concatenate([ffn[0, whole, :], ffn[1, whole, :]], axis=1) + res[whole, :]
            center = values - jnp.mean(values, axis=1, keepdims=True)
            scale = lax.rsqrt(jnp.mean(center * center, axis=1, keepdims=True) + EPS)
            hat = center * scale
            out[rows, :] = (hat * gain_two + bias_two).astype(BF)
            if offset:
                limit, base = slen[i >> 1], (i & 1) * 64
            else:
                limit, base = llen[0], i * 64
            live = base + iota((64, D), 0) < limit
            up = jnp.where(live, cot[rows, :].astype(F32), 0.0)
            gvec[2:3, :] += jnp.sum(up * hat, axis=0, keepdims=True)
            gvec[3:4, :] += jnp.sum(up, axis=0, keepdims=True)
            up = up * gain_two
            grad = scale * (
                up
                - jnp.mean(up, axis=1, keepdims=True)
                - hat * jnp.mean(up * hat, axis=1, keepdims=True)
            )
            res[whole, :] = grad
            short = grad.astype(BF)
            gffn[0, whole, :] = short[:, 0:AH]
            gffn[1, whole, :] = short[:, AH:D]

        return run

    loop(8, norm_two(cl, ol, 0))
    loop(4, norm_two(cs, os, LONG))
    ffn[...] = jnp.zeros((2, ROWS, AH), F32)

    def contract(b):
        g, n = b >> 2, b & 3
        acc[...] = nt(gffn[g], wu[b])

        def act(i):
            rows = at(i, 64)
            ghid[rows, :] = (acc[rows, :] * slope[b, rows, :]).astype(BF)

        loop(12, act)
        part = tn(active[b], gffn[g]).astype(BF)
        for w in range(4):
            put(4 * g + w, n, slice(96, 192), part[96 * w : 96 * w + 96, :])
        part = tn(grouped[g], ghid[...]).astype(BF)
        for m in range(4):
            put(b, m, slice(0, 96), part[96 * m : 96 * m + 96, :])
        ffn[g] += nt(ghid[...], wi[b])

    loop(8, contract)

    def norm_one_back(i):
        rows = at(i, 64)
        up = res[rows, :] + jnp.concatenate([ffn[0, rows, :], ffn[1, rows, :]], axis=1)
        hat = xhat[rows, :]
        gvec[0:1, :] += jnp.sum(up * hat, axis=0, keepdims=True)
        gvec[1:2, :] += jnp.sum(up, axis=0, keepdims=True)
        up = up * gain_one
        grad = rstd[rows, 0:1] * (
            up
            - jnp.mean(up, axis=1, keepdims=True)
            - hat * jnp.mean(up * hat, axis=1, keepdims=True)
        )
        gone[rows, :] = grad
        gproj[rows, :] = grad.astype(BF)

    loop(12, norm_one_back)
    for c in range(2):
        part = tn(ctx[...], gproj[:, AH * c : AH * c + AH]).astype(BF)
        for n in range(4):
            for r in range(4):
                row = 192 * n + 48 * r
                put(4 * c + r, n, slice(192, 240), part[row : row + 48, :])

    def unmix(i):
        rows = at(i, 256)
        part = nt(gproj[rows, 0:AH], wo[0]) + nt(gproj[rows, AH:D], wo[1])
        gctx[rows, :] = part.astype(BF)

    loop(3, unmix)


def mixer_backward(
    place, llen, slen, xm, packed, plong, pshort, dw, kc, cq, kp, cv, vec, gone, gctx, gvec, wm,
    keep, send, grads, rest,
    xpad, gcp, gdp, gqc, dkv, gkc, glog, gdep, spread, gather, wk,
):
    zero_gaps(xpad)
    zero_gaps(gcp)
    zero_gaps(gdp)
    for start, rows, pstart in SEGS:
        xpad[pstart : pstart + rows, :] = xm[start : start + rows, :].astype(F32)
        gcp[pstart : pstart + rows, :] = gctx[start : start + rows, AH:D].astype(F32)
    spread[...] = head_spread()
    gather[...] = head_gather()
    wk[...] = tap_kernel(wm)
    gdep[...] = jnp.zeros((8 * TAPS, D), F32)

    def dynamic(i):
        rows = at(i, 128)
        ps = padded_start(i)
        wide = pl.ds(pl.multiple_of(ps - 8, 8), 144)
        taps = kp[wide, :]
        grad_wide = gcp[wide, :]
        values = cv[wide, :]
        grad = gcp[pl.ds(ps, 128), :]
        total = jnp.zeros((128, AH), F32)
        gprob = jnp.zeros((128, 128), F32)
        for j in range(TAPS):
            moved = taps if j == 0 else pltpu.roll(taps, 128 - 8 * j, 1)
            part = nn(split_two(moved), spread[...]) * grad_wide
            total = total + part[12 - j : 140 - j, :]
            part = nn((grad * values[4 + j : 132 + j, :]).astype(BF), gather[...])
            gprob = gprob + (part if j == 0 else pltpu.roll(part, 8 * j, 1))
        grads[rows, 3 * AH : 4 * AH] = total.astype(BF)
        probs = kp[pl.ds(ps, 128), :]
        inner = probs * gprob
        for shift in (64, 32, 16, 8):
            inner = inner + pltpu.roll(inner, shift, 1)
        glogits = (probs * (gprob - inner)).astype(BF)
        glog[rows, :] = glogits
        gquery = nt(glogits, wk[...])
        gkc[rows, :] = (gquery * packed[rows, 0:AH].astype(F32)).astype(BF)
        gqc[rows, :] = gquery * kc[rows, :]

    loop(6, dynamic)

    def point_back(c):
        part = nt(gkc[:, 0:256], wm[6, at(c, 256), :])
        part = part + nt(gkc[:, 256:384], wm[7, at(c, 256), 0:128])
        part = part.astype(BF).astype(F32)
        for start, rows, pstart in SEGS:
            gdp[pstart : pstart + rows, at(c, 256)] = part[start : start + rows, :]

    loop(3, point_back)

    def depth(i):
        ps = padded_start(i)
        wide = pl.ds(pl.multiple_of(ps - 8, 8), 144)
        for c in range(3):
            lanes = slice(256 * c, 256 * c + 256)
            tokens = xpad[wide, lanes]
            grad_wide = gdp[wide, lanes]
            grad = gdp[pl.ds(ps, 128), lanes]
            total = gone[at(i, 128), lanes]
            for j in range(TAPS):
                total = total + vec[j : j + 1, lanes] * grad_wide[12 - j : 140 - j, :]
                part = tokens[4 + j : 132 + j, :] * grad
                gdep[8 * j : 8 * j + 8, lanes] += jnp.sum(part.reshape(16, 8, 256), axis=0)
            rest[at(i, 128), lanes] = total

    loop(6, depth)

    def attend(row0, nq, key0, nk, pair, load, first):
        queries = packed[pl.ds(row0, nq), at(pair, 128)].astype(F32)
        keys = packed[pl.ds(key0, nk), pl.ds(pl.multiple_of(AH + pair * 128, 128), 128)]
        vals = packed[pl.ds(key0, nk), pl.ds(pl.multiple_of(2 * AH + pair * 128, 128), 128)]
        up = gctx[pl.ds(row0, nq), at(pair, 128)].astype(F32)
        lane = iota((nq, 128), 1)
        outs = []
        gkeys = jnp.zeros((nk, 128), F32)
        gvals = jnp.zeros((nk, 128), F32)
        for hh in range(2):
            mine = (lane >> 6) == hh
            query = jnp.where(mine, queries, 0.0).astype(BF)
            upper = jnp.where(mine, up, 0.0).astype(BF)
            probs_low = load(hh)
            probs = probs_low.astype(F32)
            gprobs = nt(upper, vals)
            inner = jnp.sum(probs * gprobs, axis=1, keepdims=True)
            gscores = (probs * (gprobs - inner)).astype(BF)
            outs.append(nn(gscores, keys))
            gkeys = gkeys + tn(gscores, query)
            gvals = gvals + tn(probs_low, upper)
        both = jnp.where(lane < 64, outs[0], outs[1]) * 0.125
        both = both + gqc[pl.ds(row0, nq), at(pair, 128)]
        grads[pl.ds(row0, nq), at(pair, 128)] = both.astype(BF)
        span = pl.ds(key0, nk)
        if first:
            dkv[0, span, at(pair, 128)] = gkeys
            dkv[1, span, at(pair, 128)] = gvals
        else:
            dkv[0, span, at(pair, 128)] += gkeys
            dkv[1, span, at(pair, 128)] += gvals

    def long_attend(pair):
        for block in range(2):
            attend(
                256 * block, 256, 0, LONG, pair,
                lambda hh: plong[2 * pair + hh, 256 * block : 256 * block + 256, :],
                block == 0,
            )

    loop(3, long_attend)

    def short_attend(i):
        seg = jnp.where(i >= 3, 1, 0)
        pair = i - 3 * seg
        row0 = pl.multiple_of(LONG + 128 * seg, 128)
        attend(row0, 128, row0, SHORT, pair, lambda hh: pshort[seg, 2 * pair + hh, :, :], True)

    loop(6, short_attend)

    def pack(i):
        rows = at(i, 128)
        grads[rows, AH : 2 * AH] = (dkv[0, rows, :] * 0.125).astype(BF)
        grads[rows, 2 * AH : 3 * AH] = dkv[1, rows, :].astype(BF)

    loop(6, pack)

    def spill(b, values, lanes):
        for n in range(4):
            part = values[192 * n : 192 * n + 192, :]
            store_relative(keep, send, place, b, n, slice(None), lanes, part)

    def weights(b):
        spill(b, tn(xm[...], grads[:, at(b, 256)]).astype(BF), slice(0, 256))

    loop(6, weights)
    spill(6, tn(dw[...], gkc[:, 0:256]).astype(BF), slice(0, 256))
    spill(7, tn(dw[...], gkc[:, 256:384]).astype(BF), slice(0, 128))
    taps = [jnp.sum(gdep[8 * j : 8 * j + 8, :], axis=0, keepdims=True) for j in range(TAPS)]
    table = jnp.concatenate(
        taps + [jnp.zeros((7, D), F32), gvec[...], jnp.zeros((104, D), F32)], axis=0
    ).astype(BF)
    misc = tn(table, eye(128, BF))
    gkernel = nt(tn(cq[...], glog[...]).astype(BF), tap_permutation())
    parts = []
    for n in range(4):
        row = 192 * n
        parts.append(misc[row : row + 96, :] + gkernel[96 * n : 96 * n + 96, :])
        parts.append(misc[row + 96 : row + 192, :])
    spill(7, jnp.concatenate(parts, axis=0).astype(BF), slice(128, 256))


def input_gradient(llen, slen, grads, rest, wm, il, is_):
    def inputs(i):
        rows = at(i, 256)
        total = rest[rows, :]
        for b in range(6):
            total = total + nt(grads[rows, 256 * b : 256 * b + 256], wm[b])
        return total

    def inputs_long(i):
        live = i * 256 + iota((256, D), 0) < llen[0]
        il[at(i, 256), :] = jnp.where(live, inputs(i), 0.0).astype(BF)

    loop(2, inputs_long)
    total = inputs(2)
    row = iota((128, D), 0)
    for seg in range(2):
        part = total[128 * seg : 128 * seg + 128, :]
        is_[128 * seg : 128 * seg + 128, :] = jnp.where(row < slen[seg], part, 0.0).astype(BF)


def pack(
    place, qkv, depth, point, kernel, convout, g1, b1, inner, outer, out, g2, b2, mixer, ffn
):
    for w in range(SLOTS):

        @pl.when(place[0] == w)
        def _():
            g, r = w // 4, w % 4
            ffn[0:96, :] = inner[g, :, AH * r : AH * r + AH]
            ffn[96:192, :] = outer[g, 96 * r : 96 * r + 96, :]
            ffn[192:240, :] = out[48 * r : 48 * r + 48, AH * g : AH * g + AH]
            if w < 4:
                mixer[...] = qkv[:, 256 * w : 256 * w + 256]
            elif w == 4:
                mixer[:, 0:128] = qkv[:, 1024:1152]
                mixer[:, 128:256] = convout[:, 0:128]
            elif w == 5:
                mixer[...] = convout[:, 128:384]
            elif w == 6:
                mixer[...] = point[:, 0:256]
            else:
                mixer[:, 0:128] = point[:, 256:384]
                rows = [v[...].astype(F32).reshape(1, 192) for v in (g1, b1, g2, b2)]
                table = jnp.concatenate(
                    [depth[...].astype(F32), jnp.zeros((7, 192), F32)]
                    + rows
                    + [jnp.zeros((108, 192), F32)],
                    axis=0,
                )
                left = tn(table.astype(BF), eye(128, BF))
                row, col = iota((54, 128), 0), iota((54, 128), 1)
                right = tn(kernel[...], jnp.where(col == row + 64, 1.0, 0.0).astype(BF))
                mixer[0:96, 128:256] = (left[0:96, :] + right).astype(BF)
                mixer[96:192, 128:256] = left[96:192, :].astype(BF)


def unpack_ffn(packed, inner, outer, out):
    for w in range(SLOTS):
        g, r = w // 4, w % 4
        inner[g, :, AH * r : AH * r + AH] = packed[w, 0:96, :].astype(F32)
        outer[g, 96 * r : 96 * r + 96, :] = packed[w, 96:192, :].astype(F32)
        out[48 * r : 48 * r + 48, AH * g : AH * g + AH] = packed[w, 192:240, :].astype(F32)


def unpack_mixer(packed, qkv, depth, point, kernel, convout, g1, b1, g2, b2):
    for w in range(4):
        qkv[:, 256 * w : 256 * w + 256] = packed[w].astype(F32)
    qkv[:, 1024:1152] = packed[4, :, 0:128].astype(F32)
    convout[:, 0:128] = packed[4, :, 128:256].astype(F32)
    convout[:, 128:384] = packed[5].astype(F32)
    point[:, 0:256] = packed[6].astype(F32)
    point[:, 256:384] = packed[7, :, 0:128].astype(F32)
    misc = packed[7, :, 128:256]
    table = nt(eye(128, BF), misc)
    depth[...] = table[0:TAPS, :]
    for k, ref in enumerate((g1, b1, g2, b2)):
        ref[...] = table[16 + k : 17 + k, :].reshape(192)
    kernel[...] = table[64:118, 0:96]


SMEM = pl.BlockSpec(memory_space=pltpu.SMEM)
VMEM = pl.BlockSpec(memory_space=pltpu.VMEM)
ANY = pl.BlockSpec(memory_space=pl.ANY)


def call(kernel, specs, outs, scratch, flops, *args):
    return pl.pallas_call(
        kernel,
        out_shape=[jax.ShapeDtypeStruct(s, d) for s, d in outs],
        in_specs=specs,
        out_specs=[VMEM] * len(outs),
        scratch_shapes=[pltpu.VMEM(s, d) for s, d in scratch[0]] + list(scratch[1:]),
        compiler_params=pltpu.CompilerParams(vmem_limit_bytes=60 << 20),
        cost_estimate=pl.CostEstimate(flops=flops, bytes_accessed=1 << 20, transcendentals=0),
        name=kernel.__name__,
    )(*args)


def forward_mixer(scalars, xl, xs, pieces):
    outs = [
        ((ROWS, D), BF), ((ROWS, 3 * AH), BF),
        ((HEADS, LONG, LONG), BF), ((2, HEADS, SHORT, SHORT), BF),
        ((ROWS, D), BF), ((ROWS, AH), F32), ((ROWS, AH), BF), ((PAD, 128), F32),
        ((PAD, AH), F32), ((ROWS, D), BF), ((24, D), F32), ((SLOTS, D, 256), BF),
    ]
    scratch = [((PAD, D), F32), ((256, AH), BF), ((AH, 128), BF)]
    return call(
        mixer_forward, [SMEM] * 3 + [VMEM] * 2 + [ANY] * 8, outs,
        (scratch, pltpu.SemaphoreType.DMA), 30 * 10**9, *scalars, xl, xs, *pieces,
    )


def feed_forward(scalars, xm, ctx, vec, cl, cs, pieces):
    outs = [
        ((LONG, D), BF), ((2 * SHORT, D), BF), ((4, 4, 240, AH), BF), ((4, 4, 240, AH), BF),
        ((ROWS, D), F32), ((ROWS, D), BF), ((8, D), F32),
    ]
    scratch = [
        ((2, D, AH), BF), ((8, AH, AH), BF), ((8, AH, AH), BF), ((ROWS, D), F32), ((ROWS, D), F32),
        ((2, ROWS, AH), BF), ((2, ROWS, AH), BF), ((8, ROWS, AH), BF), ((8, ROWS, AH), F32),
        ((2, ROWS, AH), F32), ((ROWS, 128), F32), ((ROWS, AH), F32), ((ROWS, AH), BF),
        ((ROWS, D), BF),
    ]
    return call(
        ffn_both, [SMEM] * 3 + [VMEM] * 5 + [ANY] * 8, outs,
        (scratch, pltpu.SemaphoreType.DMA((3,))), 60 * 10**9,
        *scalars, xm, ctx, vec, cl, cs, *pieces,
    )


def backward_mixer(scalars, *args):
    outs = [
        ((4, 4, 192, 256), BF), ((4, 4, 192, 256), BF), ((ROWS, 4 * AH), BF), ((ROWS, D), F32),
    ]
    scratch = [
        ((PAD, D), F32), ((PAD, AH), F32), ((PAD, D), F32),
        ((ROWS, AH), F32), ((2, ROWS, AH), F32), ((ROWS, AH), BF), ((ROWS, 128), BF),
        ((8 * TAPS, D), F32), ((256, AH), BF), ((AH, 128), BF), ((AH, 128), BF),
    ]
    return call(
        mixer_backward, [SMEM] * 3 + [VMEM] * len(args), outs, (scratch,), 40 * 10**9,
        *scalars, *args,
    )


def backward_inputs(scalars, grads, rest, wm):
    return call(
        input_gradient, [SMEM] * 2 + [VMEM] * 3, [((LONG, D), BF), ((2 * SHORT, D), BF)],
        ([],), 5 * 10**9, *scalars[1:], grads, rest, wm,
    )


def far(values, bit):
    return lax.ppermute(values, "narrow", [(i, i ^ bit) for i in range(4)])


def near(values, bit):
    return lax.ppermute(values, "wide", [(i, i ^ bit) for i in range(SLOTS)])


def gather_narrow(piece):
    return jnp.stack([piece] + [far(piece, k) for k in (1, 2, 3)])


def gather_chips(block):
    return [block] + [near(block, k) for k in (2, 4, 6)]


def gather_cores(blocks):
    return blocks + [near(block, 1) for block in blocks]


def total(first, others):
    result = first.astype(F32)
    for other in others:
        result = result + other.astype(F32)
    return result.astype(BF)


def reduce_cores(keep, sent):
    return [total(keep[k], [sent[k]]) for k in range(4)]


def send_chips(parts):
    return [near(parts[k], 2 * k) for k in (1, 2, 3)]


def reduce_chips(first, others):
    return [total(first[k], [other[k] for other in others]) for k in range(4)]


def send_narrow(parts):
    return [far(parts[k], k) for k in (1, 2, 3)]


def gather_wide(parts):
    return lax.all_gather(parts, "wide", axis=0, tiled=False)


def body(
    long_tokens, long_lengths, short_tokens, short_lengths,
    w_qkv, w_depth, w_point, w_kernel, w_convout, w_out, norm1_gain, norm1_bias,
    w_inner, w_outer, norm2_gain, norm2_bias, long_cotangent, short_cotangent,
):
    place = jnp.stack([lax.axis_index("wide"), lax.axis_index("narrow")]).astype(jnp.int32)
    scalars = (place, long_lengths, short_lengths)
    xl, xs = long_tokens.reshape(LONG, D), short_tokens.reshape(2 * SHORT, D)
    cl, cs = long_cotangent.reshape(LONG, D), short_cotangent.reshape(2 * SHORT, D)
    mixer, ffn = call(
        pack, [SMEM] + [VMEM] * 12, [((192, 256), BF), ((240, AH), BF)], ([],), 10**9,
        place, w_qkv, w_depth, w_point, w_kernel.T, w_convout, norm1_gain, norm1_bias,
        w_inner, w_outer, w_out, norm2_gain, norm2_bias,
    )
    mixer = gather_narrow(mixer)
    mixer, ffn = lax.optimization_barrier((mixer, ffn))
    mixer = gather_chips(mixer)
    ffn = gather_narrow(ffn)
    mixer, ffn = lax.optimization_barrier((mixer, ffn))
    mixer = gather_cores(mixer)
    ffn = gather_chips(ffn)
    xm, packed, plong, pshort, dw, kc, cq, kp, cv, ctx, vec, wm = forward_mixer(
        scalars, xl, xs, mixer
    )
    ctx, ffn = lax.optimization_barrier((ctx, ffn))
    ffn = gather_cores(ffn)
    ol, os, keep, send, gone, gctx, gvec = feed_forward(scalars, xm, ctx, vec, cl, cs, ffn)
    ga = reduce_cores(keep, near(send, 1))
    ga_sent = send_chips(ga)
    gone, ga = lax.optimization_barrier((gone, ga))
    keep, send, grads, rest = backward_mixer(
        scalars, xm, packed, plong, pshort, dw, kc, cq, kp, cv, vec, gone, gctx, gvec, wm
    )
    keep, send, ga_sent = lax.optimization_barrier((keep, send, ga_sent))
    sent = near(send, 1)
    ga = reduce_chips(ga[0], ga_sent)
    ga_sent = send_narrow(ga)
    gb = reduce_cores(keep, sent)
    gb_sent = send_chips(gb)
    rest, gb = lax.optimization_barrier((rest, gb))
    il, is_ = backward_inputs(scalars, grads, rest, wm)
    ga_sent, gb_sent, il = lax.optimization_barrier((ga_sent, gb_sent, il))
    ga = lax.psum(total(ga[0], ga_sent), "hi")
    gb = reduce_chips(gb[0], gb_sent)
    gb = lax.psum(total(gb[0], send_narrow(gb)), "hi")
    inner, outer, out = call(
        unpack_ffn, [VMEM], [((2, 96, 4 * AH), F32), ((2, AH, AH), F32), ((192, D), F32)],
        ([],), 10**9, gather_wide(ga),
    )
    outs = [
        ((192, 3 * AH), F32), ((TAPS, 192), F32), ((192, AH), F32), ((54, 96), F32), ((192, AH), F32),
    ] + [((192,), F32)] * 4
    qkv, depth, point, kernel, convout, g1, b1, g2, b2 = call(
        unpack_mixer, [VMEM], outs, ([],), 10**9, gather_wide(gb)
    )
    return (
        ol.reshape(long_tokens.shape), os.reshape(short_tokens.shape),
        il.reshape(long_tokens.shape), is_.reshape(short_tokens.shape),
        qkv, depth, point, kernel.T, convout, out, g1, b1, inner, outer, g2, b2,
    )


def solution(mesh):
    wide, narrow = mesh.shape["wide"], mesh.shape["narrow"]
    inner_mesh = Mesh(mesh.devices.reshape(wide // SLOTS, SLOTS, narrow), ("hi", "wide", "narrow"))
    every = ("hi", "wide", "narrow")
    rows = P(every, None, None)
    weights = (
        P("narrow", None), P(None, "narrow"), P("narrow", None), P("narrow", None),
        P("narrow", None), P("narrow", None), P("narrow"), P("narrow"),
        P(None, "narrow", None), P(None, "narrow", None), P("narrow"), P("narrow"),
    )
    return jax.shard_map(
        body,
        mesh=inner_mesh,
        in_specs=(rows, P(every), rows, P(every)) + weights + (rows, rows),
        out_specs=(rows, rows, rows, rows) + weights,
        check_vma=False,
    )
```

```python
import jax
import jax.numpy as jnp
from jax import lax
from jax.experimental import pallas as pl
from jax.experimental.pallas import tpu as pltpu
from jax.sharding import Mesh
from jax.sharding import PartitionSpec as P

BF = jnp.bfloat16
F32 = jnp.float32
EPS = 1e-12
D = 768
AH = 384
HEADS = 6
TAPS = 9
LONG = 512
SHORT = 128
ROWS = 768
PAD = 800
SLOTS = 8
NEG = -1000000000.0
PSTART = tuple(8 + 128 * i + 8 * max(i - 3, 0) for i in range(6))
SEGS = ((0, 512, 8), (512, 128, 528), (640, 128, 664))


def nn(a, b):
    return lax.dot_general(a, b, (((1,), (0,)), ((), ())), preferred_element_type=F32)


def nt(a, b):
    return lax.dot_general(a, b, (((1,), (1,)), ((), ())), preferred_element_type=F32)


def tn(a, b):
    return lax.dot_general(a, b, (((0,), (0,)), ((), ())), preferred_element_type=F32)


def iota(shape, axis):
    return lax.broadcasted_iota(jnp.int32, shape, axis)


def loop(count, body):
    def step(i, carry):
        body(i)
        return carry

    lax.fori_loop(0, count, step, 0)


def at(i, size):
    if isinstance(i, int):
        return pl.ds(i * size, size)
    return pl.ds(pl.multiple_of(i * size, size), size)


def padded_start(i):
    return pl.multiple_of(8 + 128 * i + 8 * jnp.maximum(i - 3, 0), 8)


def zero_gaps(ref):
    for start in (0, 520, 656, 792):
        ref[start : start + 8, :] = jnp.zeros((8, ref.shape[1]), ref.dtype)


def eye(n, dtype):
    return jnp.where(iota((n, n), 0) == iota((n, n), 1), 1.0, 0.0).astype(dtype)


def tap_permutation():
    row, col = iota((128, 128), 0), iota((128, 128), 1)
    head, tap = col & 7, col >> 3
    keep = (head < HEADS) & (tap < TAPS) & (row == 64 + head * TAPS + tap)
    return jnp.where(keep, 1.0, 0.0).astype(BF)


def head_spread():
    row, col = iota((256, AH), 0), iota((256, AH), 1)
    return jnp.where((row & 127) == (col >> 6), 1.0, 0.0).astype(BF)


def head_gather():
    row, col = iota((AH, 128), 0), iota((AH, 128), 1)
    return jnp.where((row >> 6) == col, 1.0, 0.0).astype(BF)


def split_two(values):
    high = values.astype(BF)
    low = (values - high.astype(F32)).astype(BF)
    return jnp.concatenate([high, low], axis=1)


def spread_taps(probs):
    moved = [probs] + [pltpu.roll(probs, 128 - 8 * j, 1) for j in range(1, TAPS)]
    return split_two(jnp.concatenate(moved, axis=0))


def tap_kernel(wm):
    stored = jnp.concatenate([wm[7, 192 * n : 192 * n + 96, 128:256] for n in range(4)], axis=0)
    return nn(stored, tap_permutation()).astype(BF)


def slot_of(where, core, chip):
    return 2 * ((where >> 1) ^ chip) + ((where & 1) ^ core)


def fetch_mixer(place, pieces, wm, sem):
    for at_core in range(2):
        for chip in range(4):
            piece = pieces[4 * at_core + chip]
            slot = slot_of(place[0], at_core, chip)

            def fetch(k):
                pltpu.make_async_copy(piece.at[k], wm.at[slot, at(place[1] ^ k, 192), :], sem).start()

            loop(4, fetch)


def mixer_forward(
    place, llen, slen, xl, xs, p0, p1, p2, p3, p4, p5, p6, p7,
    xm_any, packed_any, plong_any, pshort_any, dw_any, kc_any, cq_any, kp_any, cv_any, ctx_any, vec,
    wm, xpad, spread, wk, xm, packed, plong, pshort, dw, kc, cq, kp, cv, ctx, sem, sems
):
    fetch_mixer(place, (p0, p1, p2, p3, p4, p5, p6, p7), wm, sem)
    lens = (llen[0], slen[0], slen[1])
    zero_gaps(xpad)
    zero_gaps(cv)
    zero_gaps(kp)
    for i in range(6):
        seg = max(i - 3, 0)
        base = 128 * i if i < 4 else 0
        tokens = xl[128 * i : 128 * i + 128, :] if i < 4 else xs[128 * (i - 4) : 128 * (i - 3), :]
        live = base + iota((128, D), 0) < lens[seg]
        values = jnp.where(live, tokens.astype(F32), 0.0)
        xpad[PSTART[i] : PSTART[i] + 128, :] = values
        xm[128 * i : 128 * i + 128, :] = values.astype(BF)
    stores = [start_copy(xm, xm_any, sems.at[0])]
    spread[...] = head_spread()
    pltpu.make_async_copy(wm, wm, sem).wait()
    vec[...] = nt(eye(128, BF), wm[7, :, 128:256])[0:24, :]
    wk[...] = tap_kernel(wm)

    def depth(i):
        ps = padded_start(i)
        for c in range(3):
            lanes = slice(256 * c, 256 * c + 256)
            window = xpad[pl.ds(pl.multiple_of(ps - 8, 8), 144), lanes]
            total = jnp.zeros((128, 256), F32)
            for j in range(TAPS):
                total = total + vec[j : j + 1, lanes] * window[4 + j : 132 + j, :]
            dw[at(i, 128), lanes] = total.astype(BF)

    def project(b):
        packed[:, at(b, 256)] = nn(xm[...], wm[b]).astype(BF)
        depth(b)

    loop(4, project)
    depth(jnp.int32(4))
    part = nn(xm[...], wm[4])
    packed[:, 1024:1152] = part[:, 0:128].astype(BF)
    for start, rows, pstart in SEGS:
        cv[pstart : pstart + rows, 0:128] = part[start : start + rows, 128:256]
    depth(jnp.int32(5))
    part = nn(xm[...], wm[5])
    for start, rows, pstart in SEGS:
        cv[pstart : pstart + rows, 128:384] = part[start : start + rows, :]
    stores += [
        start_copy(packed, packed_any, sems.at[1]), start_copy(dw, dw_any, sems.at[2]),
        start_copy(cv, cv_any, sems.at[3]),
    ]
    kc[:, 0:256] = nn(dw[...], wm[6])
    kc[:, 256:384] = nn(dw[...], wm[7, :, 0:128])
    stores.append(start_copy(kc, kc_any, sems.at[4]))

    def dynamic(i):
        rows = at(i, 128)
        ps = padded_start(i)
        query = (kc[rows, :] * packed[rows, 0:AH].astype(F32)).astype(BF)
        cq[rows, :] = query
        logits = nn(query, wk[...])
        real = iota((128, 128), 1) < 8 * TAPS
        top = jnp.where(real, logits, NEG * 1e20)
        for shift in (64, 32, 16, 8):
            top = jnp.maximum(top, pltpu.roll(top, shift, 1))
        ex = jnp.where(real, jnp.exp(logits - top), 0.0)
        total = ex
        for shift in (64, 32, 16, 8):
            total = total + pltpu.roll(total, shift, 1)
        probs = ex / total
        kp[pl.ds(ps, 128), :] = probs
        window = cv[pl.ds(pl.multiple_of(ps - 8, 8), 144), :]
        weights = nn(spread_taps(probs), spread[...])
        out = jnp.zeros((128, AH), F32)
        for j in range(TAPS):
            out = out + weights[128 * j : 128 * j + 128, :] * window[4 + j : 132 + j, :]
        ctx[rows, AH:D] = out.astype(BF)

    loop(6, dynamic)
    stores += [start_copy(cq, cq_any, sems.at[5]), start_copy(kp, kp_any, sems.at[6])]

    def attend(row0, nq, key0, nk, limit, pair, store):
        queries = packed[pl.ds(row0, nq), at(pair, 128)].astype(F32) * 0.125
        keys = packed[pl.ds(key0, nk), at(3 + pair, 128)].astype(F32)
        vals = packed[pl.ds(key0, nk), at(6 + pair, 128)]
        lane, key_lane = iota((nq, 128), 1), iota((nk, 128), 1)
        bias = jnp.where(iota((nk, 128), 0) < limit, 0.0, NEG)
        outs = []
        for hh in range(2):
            spare = 64 * (1 - hh)
            query = jnp.where((lane >> 6) == hh, queries, jnp.where(lane == spare, 1.0, 0.0))
            scores = nt(query.astype(BF), jnp.where(key_lane == spare, bias, keys).astype(BF))
            ex = jnp.exp(scores - jnp.max(scores, axis=1, keepdims=True))
            probs = (ex * (1.0 / jnp.sum(ex, axis=1, keepdims=True))).astype(BF)
            store(hh, probs)
            outs.append(nn(probs, vals))
        both = jnp.where(lane < 64, outs[0], outs[1])
        ctx[pl.ds(row0, nq), at(pair, 128)] = both.astype(BF)

    def long_attend(i):
        pair, block = i >> 1, i & 1
        row0 = pl.multiple_of(block * 256, 256)

        def store(hh, probs):
            plong[2 * pair + hh, pl.ds(row0, 256), :] = probs

        attend(row0, 256, 0, LONG, lens[0], pair, store)

    loop(6, long_attend)
    stores.append(start_copy(plong, plong_any, sems.at[7]))
    for seg in range(2):
        for pair in range(3):

            def store(hh, probs):
                pshort[seg, 2 * pair + hh, :, :] = probs

            row0 = LONG + 128 * seg
            attend(row0, 128, row0, SHORT, lens[1 + seg], pair, store)
    stores += [start_copy(pshort, pshort_any, sems.at[8]), start_copy(ctx, ctx_any, sems.at[9])]
    for copy in stores:
        copy.wait()


def gelu_parts(hidden):
    cdf = 0.5 + 0.5 * lax.erf(hidden * 0.7071067811865476)
    return cdf, jnp.exp(hidden * hidden * -0.5) * 0.3989422804014327


def fold(values):
    return jnp.sum(values.reshape(values.shape[0] // 8, 8, values.shape[1]), axis=0)


def start_copy(source, target, sem):
    copy = pltpu.make_async_copy(source, target, sem)
    copy.start()
    return copy


def ship(keep, send, place, slot, shard, rows, source, sem):
    where = slot ^ place[0]
    chip, far_off = where >> 1, shard ^ place[1]

    @pl.when((where & 1) == 0)
    def _():
        pltpu.make_async_copy(source, keep.at[chip, far_off, rows, :], sem).start()

    @pl.when((where & 1) == 1)
    def _():
        pltpu.make_async_copy(source, send.at[chip, far_off, rows, :], sem).start()


def ffn_both(
    place, llen, slen, vec, xm_any, ctx_any, cl, cs, p0, p1, p2, p3, p4, p5, p6, p7,
    ol, os, keep, send, gone_any, gctx_any, gvec,
    wo, wi, wu, xm, ctx, cot, out, res, xhat, grouped, gffn, active, slope, ffn, rstd,
    hid_a, hid_b, ghid_a, ghid_b, gproj, gout, ginner, gouter, gone, gctx, sums, sems,
):
    loads = [start_copy(ctx_any, ctx, sems.at[3]), start_copy(xm_any, xm, sems.at[4])]

    def fetch(part):
        for core, pieces in enumerate(((p0, p1, p2, p3), (p4, p5, p6, p7))):
            for chip, piece in enumerate(pieces):
                slot = slot_of(place[0], core, chip)
                g, r = slot >> 2, slot & 3

                def one(k):
                    n = place[1] ^ k
                    if part == 0:
                        rows = pl.ds(pl.multiple_of(192 * n + 48 * r, 48), 48)
                        source, target = pl.ds(192, 48), wo.at[g, rows, :]
                    elif part == 1:
                        source, target = pl.ds(0, 96), wi.at[slot, at(n, 96), :]
                    else:
                        source, target = pl.ds(96, 96), wu.at[4 * g + n, at(r, 96), :]
                    pltpu.make_async_copy(piece.at[k, source, :], target, sems.at[part]).start()

                loop(4, one)

    for part in range(3):
        fetch(part)
    cots = [
        start_copy(cl, cot.at[0:LONG], sems.at[5]), start_copy(cs, cot.at[LONG:ROWS], sems.at[6])
    ]
    gain_one, bias_one = vec[16:17, :], vec[17:18, :]
    gain_two, bias_two = vec[18:19, :], vec[19:20, :]
    sums[...] = jnp.zeros((32, D), F32)
    ffn[...] = jnp.zeros((2, ROWS, AH), F32)
    for copy in loads:
        copy.wait()
    pltpu.make_async_copy(wo, wo, sems.at[0]).wait()

    def mix(i):
        rows = at(i, 256)
        for c in range(2):
            lanes = slice(AH * c, AH * c + AH)
            res[rows, lanes] = nn(ctx[rows, :], wo[c]) + xm[rows, lanes].astype(F32)

    loop(3, mix)

    def norm_one(i):
        for half in range(2):
            rows = at(2 * i + half, 32)
            values = res[rows, :]
            center = values - jnp.mean(values, axis=1, keepdims=True)
            scale = lax.rsqrt(jnp.mean(center * center, axis=1, keepdims=True) + EPS)
            hat = center * scale
            first = hat * gain_one + bias_one
            xhat[rows, :] = hat
            rstd[rows, :] = jnp.broadcast_to(scale, (32, 128))
            res[rows, :] = first
            short = first.astype(BF)
            grouped[0, rows, :] = short[:, 0:AH]
            grouped[1, rows, :] = short[:, AH:D]

    loop(12, norm_one)
    pltpu.make_async_copy(wi, wi, sems.at[1]).wait()
    pltpu.make_async_copy(wu, wu, sems.at[2]).wait()

    def hidden(t, target):
        b = lax.div(t, 3)
        target[...] = nn(grouped[b >> 2, at(t - 3 * b, 256), :], wi[b])

    def outward(t):
        b = lax.div(t, 3)
        rows = at(t - 3 * b, 256)
        ffn[b >> 2, rows, :] += nn(active[b, rows, :], wu[b])

    def act(t, source):
        b = lax.div(t, 3)
        m = t - 3 * b
        for part in range(8):
            values = source[32 * part : 32 * part + 32, :]
            rows = pl.ds(pl.multiple_of(m * 256 + 32 * part, 32), 32)
            cdf, density = gelu_parts(values)
            active[b, rows, :] = (values * cdf).astype(BF)
            slope[b, rows, :] = cdf + values * density

    def pair(u, first=False):
        t = 2 * u
        if not first:
            outward(t - 1)
        hidden(t + 1, hid_b)
        act(t, hid_a)
        outward(t)
        hidden(jnp.minimum(t + 2, 23), hid_a)
        act(t + 1, hid_b)

    hidden(jnp.int32(0), hid_a)
    pair(jnp.int32(0), True)
    loop(11, lambda u: pair(u + 1))
    outward(jnp.int32(23))
    for copy in cots:
        copy.wait()

    def norm_two(i):
        limit = jnp.where(i < 8, llen[0], slen[jnp.clip((i - 8) >> 1, 0, 1)])
        base = jnp.where(i < 8, 64 * i, 64 * (i & 1))
        for half in range(2):
            rows = at(2 * i + half, 32)
            values = jnp.concatenate([ffn[0, rows, :], ffn[1, rows, :]], axis=1) + res[rows, :]
            center = values - jnp.mean(values, axis=1, keepdims=True)
            scale = lax.rsqrt(jnp.mean(center * center, axis=1, keepdims=True) + EPS)
            hat = center * scale
            out[rows, :] = (hat * gain_two + bias_two).astype(BF)
            live = base + 32 * half + iota((32, D), 0) < limit
            up = jnp.where(live, cot[rows, :].astype(F32), 0.0)
            sums[16:24, :] += fold(up * hat)
            sums[24:32, :] += fold(up)
            up = up * gain_two
            grad = scale * (
                up
                - jnp.mean(up, axis=1, keepdims=True)
                - hat * jnp.mean(up * hat, axis=1, keepdims=True)
            )
            res[rows, :] = grad
            short = grad.astype(BF)
            gffn[0, rows, :] = short[:, 0:AH]
            gffn[1, rows, :] = short[:, AH:D]

    loop(12, norm_two)
    stores = [
        start_copy(out.at[0:LONG], ol, sems.at[3]), start_copy(out.at[LONG:ROWS], os, sems.at[4])
    ]
    ffn[...] = jnp.zeros((2, ROWS, AH), F32)

    def slopes(b, target):
        for part in range(6):
            rows = slice(128 * part, 128 * part + 128)
            back = nt(gffn[b >> 2, rows, :], wu[b])
            target[rows, :] = (back * slope[b, rows, :]).astype(BF)

    def gradients(b, source):
        g, n = b >> 2, b & 3
        gouter[b] = tn(active[b], gffn[g]).astype(BF)
        ginner[b] = tn(grouped[g], source[...]).astype(BF)
        ffn[g] += nt(source[...], wi[b])
        for w in range(4):
            rows = pl.ds(96 * w, 96)
            ship(keep, send, place, 4 * g + w, n, pl.ds(96, 96), gouter.at[b, rows, :], sems.at[0])
            ship(keep, send, place, b, w, pl.ds(0, 96), ginner.at[b, rows, :], sems.at[1])

    slopes(jnp.int32(0), ghid_a)

    def contract(u):
        b = 2 * u
        slopes(b + 1, ghid_b)
        gradients(b, ghid_a)
        slopes(jnp.minimum(b + 2, 7), ghid_a)
        gradients(b + 1, ghid_b)

    loop(4, contract)

    def norm_one_back(i):
        for half in range(2):
            rows = at(2 * i + half, 32)
            up = res[rows, :] + jnp.concatenate([ffn[0, rows, :], ffn[1, rows, :]], axis=1)
            hat = xhat[rows, :]
            sums[0:8, :] += fold(up * hat)
            sums[8:16, :] += fold(up)
            up = up * gain_one
            grad = rstd[rows, 0:1] * (
                up
                - jnp.mean(up, axis=1, keepdims=True)
                - hat * jnp.mean(up * hat, axis=1, keepdims=True)
            )
            gone[rows, :] = grad
            gproj[rows, :] = grad.astype(BF)

    loop(12, norm_one_back)
    stores.append(start_copy(gone, gone_any, sems.at[5]))
    for k in range(4):
        gvec[k : k + 1, :] = jnp.sum(sums[8 * k : 8 * k + 8, :], axis=0, keepdims=True)
    gvec[4:8, :] = jnp.zeros((4, D), F32)
    for c in range(2):
        gout[c] = tn(ctx[...], gproj[:, AH * c : AH * c + AH]).astype(BF)
        for n in range(4):
            for r in range(4):
                source = gout.at[c, pl.ds(192 * n + 48 * r, 48), :]
                ship(keep, send, place, 4 * c + r, n, pl.ds(192, 48), source, sems.at[2])

    def unmix(i):
        rows = at(i, 256)
        part = nt(gproj[rows, 0:AH], wo[0]) + nt(gproj[rows, AH:D], wo[1])
        gctx[rows, :] = part.astype(BF)

    loop(3, unmix)
    stores.append(start_copy(gctx, gctx_any, sems.at[6]))
    for copy in stores:
        copy.wait()
    pltpu.make_async_copy(gouter, gouter, sems.at[0]).wait()
    pltpu.make_async_copy(ginner, ginner, sems.at[1]).wait()
    pltpu.make_async_copy(gout, gout, sems.at[2]).wait()


def mixer_backward(
    place, vec, gvec, xm_any, packed_any, plong_any, pshort_any, dw_any, kc_any, cq_any, kp_any,
    cv_any, gctx_any, p0, p1, p2, p3, p4, p5, p6, p7,
    keep, send, grads_any, gdep_any,
    wm, xm, packed, plong, pshort, dw, kc, cq, kp, cv, gctx,
    xpad, gcp, gdp, grads, gqc, dkv, gkc, glog, gdep, gb, spread, gather, wk, sem, sems, out_sem,
):
    arrays = (
        (gctx_any, gctx), (kp_any, kp), (cv_any, cv), (packed_any, packed), (kc_any, kc),
        (xm_any, xm), (plong_any, plong), (pshort_any, pshort), (dw_any, dw), (cq_any, cq),
    )
    loads = [start_copy(a, b, sems.at[k]) for k, (a, b) in enumerate(arrays[0:5])]
    fetch_mixer(place, (p0, p1, p2, p3, p4, p5, p6, p7), wm, sem)
    late = [start_copy(a, b, sems.at[5 + k]) for k, (a, b) in enumerate(arrays[5:])]
    zero_gaps(xpad)
    zero_gaps(gcp)
    zero_gaps(gdp)
    spread[...] = head_spread()
    gather[...] = head_gather()
    gdep[...] = jnp.zeros((8 * TAPS, D), F32)
    for copy in loads:
        copy.wait()
    for start, rows, pstart in SEGS:
        gcp[pstart : pstart + rows, :] = gctx[start : start + rows, AH:D].astype(F32)
    pltpu.make_async_copy(wm, wm, sem).wait()
    wk[...] = tap_kernel(wm)

    def dynamic(i):
        rows = at(i, 128)
        ps = padded_start(i)
        wide = pl.ds(pl.multiple_of(ps - 8, 8), 144)
        grad_wide = gcp[wide, :]
        values = cv[wide, :]
        grad = gcp[pl.ds(ps, 128), :]
        weights = nn(spread_taps(kp[wide, :]), spread[...])
        total = jnp.zeros((128, AH), F32)
        parts = []
        for j in range(TAPS):
            part = weights[144 * j : 144 * j + 144, :] * grad_wide
            total = total + part[12 - j : 140 - j, :]
            parts.append((grad * values[4 + j : 132 + j, :]).astype(BF))
        grads[rows, 3 * AH : 4 * AH] = total.astype(BF)
        sums = nn(jnp.concatenate(parts, axis=0), gather[...])
        gprob = sums[0:128, :]
        for j in range(1, TAPS):
            gprob = gprob + pltpu.roll(sums[128 * j : 128 * j + 128, :], 8 * j, 1)
        probs = kp[pl.ds(ps, 128), :]
        inner = probs * gprob
        for shift in (64, 32, 16, 8):
            inner = inner + pltpu.roll(inner, shift, 1)
        glogits = (probs * (gprob - inner)).astype(BF)
        glog[rows, :] = glogits
        gquery = nt(glogits, wk[...])
        gkc[rows, :] = (gquery * packed[rows, 0:AH].astype(F32)).astype(BF)
        gqc[rows, :] = gquery * kc[rows, :]

    loop(6, dynamic)
    for copy in late:
        copy.wait()

    def point_back(c):
        part = nt(gkc[:, 0:256], wm[6, at(c, 256), :])
        part = part + nt(gkc[:, 256:384], wm[7, at(c, 256), 0:128])
        part = part.astype(BF).astype(F32)
        for start, rows, pstart in SEGS:
            gdp[pstart : pstart + rows, at(c, 256)] = part[start : start + rows, :]

    loop(3, point_back)
    copy_depth = start_copy(gdp, gdep_any, out_sem.at[1])

    def attend(row0, nq, key0, nk, pair, load, first):
        queries = packed[pl.ds(row0, nq), at(pair, 128)].astype(F32) * 0.125
        keys = packed[pl.ds(key0, nk), at(3 + pair, 128)]
        vals = packed[pl.ds(key0, nk), at(6 + pair, 128)]
        up = gctx[pl.ds(row0, nq), at(pair, 128)].astype(F32)
        lane = iota((nq, 128), 1)
        outs = []
        gkeys = jnp.zeros((nk, 128), F32)
        gvals = jnp.zeros((nk, 128), F32)
        for hh in range(2):
            mine = (lane >> 6) == hh
            query = jnp.where(mine, queries, 0.0).astype(BF)
            upper = jnp.where(mine, up, 0.0).astype(BF)
            probs_low = load(hh)
            probs = probs_low.astype(F32)
            gprobs = nt(upper, vals)
            inner = jnp.sum(probs * gprobs, axis=1, keepdims=True)
            gscores = (probs * (gprobs - inner)).astype(BF)
            outs.append(nn(gscores, keys))
            gkeys = gkeys + tn(gscores, query)
            gvals = gvals + tn(probs_low, upper)
        both = jnp.where(lane < 64, outs[0], outs[1]) * 0.125
        both = both + gqc[pl.ds(row0, nq), at(pair, 128)]
        grads[pl.ds(row0, nq), at(pair, 128)] = both.astype(BF)
        span = pl.ds(key0, nk)
        if nq == nk:
            grads[span, at(3 + pair, 128)] = gkeys.astype(BF)
            grads[span, at(6 + pair, 128)] = gvals.astype(BF)
        elif first:
            dkv[0] = gkeys
            dkv[1] = gvals
        else:
            grads[span, at(3 + pair, 128)] = (dkv[0] + gkeys).astype(BF)
            grads[span, at(6 + pair, 128)] = (dkv[1] + gvals).astype(BF)

    def long_attend(pair):
        for block in range(2):
            attend(
                256 * block, 256, 0, LONG, pair,
                lambda hh: plong[2 * pair + hh, 256 * block : 256 * block + 256, :],
                block == 0,
            )

    loop(3, long_attend)
    for seg in range(2):
        for pair in range(3):
            row0 = LONG + 128 * seg
            attend(row0, 128, row0, SHORT, pair, lambda hh: pshort[seg, 2 * pair + hh, :, :], True)
    copy_grads = start_copy(grads, grads_any, out_sem.at[2])
    for start, rows, pstart in SEGS:
        xpad[pstart : pstart + rows, :] = xm[start : start + rows, :].astype(F32)

    def release(b):
        for n in range(4):
            where = b ^ place[0]
            chip, far_off = where >> 1, n ^ place[1]
            source = gb.at[b, pl.ds(192 * n, 192), :]

            @pl.when((where & 1) == 0)
            def _():
                pltpu.make_async_copy(source, keep.at[chip, far_off], out_sem.at[0]).start()

            @pl.when((where & 1) == 1)
            def _():
                pltpu.make_async_copy(source, send.at[chip, far_off], out_sem.at[0]).start()

    gb[6] = tn(dw[...], gkc[:, 0:256]).astype(BF)
    release(6)

    def depth(i):
        ps = padded_start(i)
        wide = pl.ds(pl.multiple_of(ps - 8, 8), 144)
        for c in range(3):
            lanes = slice(256 * c, 256 * c + 256)
            tokens = xpad[pl.ds(ps, 128), lanes]
            grad_wide = gdp[wide, lanes]
            for j in range(TAPS):
                gdep[8 * j : 8 * j + 8, lanes] += fold(tokens * grad_wide[12 - j : 140 - j, :])

    def weights(b):
        gb[b] = tn(xm[...], grads[:, at(b, 256)]).astype(BF)
        depth(b)
        release(b)

    loop(6, weights)
    gb[7, :, 0:128] = tn(dw[...], gkc[:, 256:384]).astype(BF)
    taps = [jnp.sum(gdep[8 * j : 8 * j + 8, :], axis=0, keepdims=True) for j in range(TAPS)]
    table = jnp.concatenate(
        taps + [jnp.zeros((7, D), F32), gvec[...], jnp.zeros((104, D), F32)], axis=0
    ).astype(BF)
    misc = tn(table, eye(128, BF))
    gkernel = nt(tn(cq[...], glog[...]).astype(BF), tap_permutation())
    for n in range(4):
        row = 192 * n
        part = misc[row : row + 96, :] + gkernel[96 * n : 96 * n + 96, :]
        gb[7, row : row + 96, 128:256] = part.astype(BF)
        gb[7, row + 96 : row + 192, 128:256] = misc[row + 96 : row + 192, :].astype(BF)
    release(7)
    copy_depth.wait()
    copy_grads.wait()
    pltpu.make_async_copy(gb, gb, out_sem.at[0]).wait()


def input_gradient(
    place, llen, slen, vec, grads_any, gdp_any, gone_any, p0, p1, p2, p3, p4, p5, p6, p7,
    il, is_, wm, grads, gdp, rest, sem, sems
):
    arrays = ((gone_any, rest), (gdp_any, gdp), (grads_any, grads))
    loads = [start_copy(a, b, sems.at[k]) for k, (a, b) in enumerate(arrays)]
    fetch_mixer(place, (p0, p1, p2, p3, p4, p5, p6, p7), wm, sem)
    for copy in loads:
        copy.wait()

    def depth(i):
        ps = padded_start(i)
        for c in range(3):
            lanes = slice(256 * c, 256 * c + 256)
            window = gdp[pl.ds(pl.multiple_of(ps - 8, 8), 144), lanes]
            total = rest[at(i, 128), lanes]
            for j in range(TAPS):
                total = total + vec[j : j + 1, lanes] * window[12 - j : 140 - j, :]
            rest[at(i, 128), lanes] = total

    loop(6, depth)
    pltpu.make_async_copy(wm, wm, sem).wait()

    def inputs(i):
        rows = at(i, 256)
        total = rest[rows, :]
        for b in range(6):
            total = total + nt(grads[rows, 256 * b : 256 * b + 256], wm[b])
        return total

    def inputs_long(i):
        live = i * 256 + iota((256, D), 0) < llen[0]
        il[at(i, 256), :] = jnp.where(live, inputs(i), 0.0).astype(BF)

    loop(2, inputs_long)
    total = inputs(2)
    row = iota((128, D), 0)
    for seg in range(2):
        part = total[128 * seg : 128 * seg + 128, :]
        is_[128 * seg : 128 * seg + 128, :] = jnp.where(row < slen[seg], part, 0.0).astype(BF)


def pack(
    place, qkv, depth, point, kernel, convout, g1, b1, inner, outer, out, g2, b2, mixer, ffn
):
    for w in range(SLOTS):

        @pl.when(place[0] == w)
        def _():
            g, r = w // 4, w % 4
            ffn[0:96, :] = inner[g, :, AH * r : AH * r + AH]
            ffn[96:192, :] = outer[g, 96 * r : 96 * r + 96, :]
            ffn[192:240, :] = out[48 * r : 48 * r + 48, AH * g : AH * g + AH]
            if w < 4:
                mixer[...] = qkv[:, 256 * w : 256 * w + 256]
            elif w == 4:
                mixer[:, 0:128] = qkv[:, 1024:1152]
                mixer[:, 128:256] = convout[:, 0:128]
            elif w == 5:
                mixer[...] = convout[:, 128:384]
            elif w == 6:
                mixer[...] = point[:, 0:256]
            else:
                mixer[:, 0:128] = point[:, 256:384]
                rows = [v[...].astype(F32).reshape(1, 192) for v in (g1, b1, g2, b2)]
                table = jnp.concatenate(
                    [depth[...].astype(F32), jnp.zeros((7, 192), F32)]
                    + rows
                    + [jnp.zeros((108, 192), F32)],
                    axis=0,
                )
                left = tn(table.astype(BF), eye(128, BF))
                row, col = iota((54, 128), 0), iota((54, 128), 1)
                right = tn(kernel[...], jnp.where(col == row + 64, 1.0, 0.0).astype(BF))
                mixer[0:96, 128:256] = (left[0:96, :] + right).astype(BF)
                mixer[96:192, 128:256] = left[96:192, :].astype(BF)


def unpack_ffn(packed, inner, outer, out):
    for w in range(SLOTS):
        g, r = w // 4, w % 4
        inner[g, :, AH * r : AH * r + AH] = packed[w, 0:96, :].astype(F32)
        outer[g, 96 * r : 96 * r + 96, :] = packed[w, 96:192, :].astype(F32)
        out[48 * r : 48 * r + 48, AH * g : AH * g + AH] = packed[w, 192:240, :].astype(F32)


def unpack_mixer(packed, qkv, depth, point, kernel, convout, g1, b1, g2, b2):
    for w in range(4):
        qkv[:, 256 * w : 256 * w + 256] = packed[w].astype(F32)
    qkv[:, 1024:1152] = packed[4, :, 0:128].astype(F32)
    convout[:, 0:128] = packed[4, :, 128:256].astype(F32)
    convout[:, 128:384] = packed[5].astype(F32)
    point[:, 0:256] = packed[6].astype(F32)
    point[:, 256:384] = packed[7, :, 0:128].astype(F32)
    misc = packed[7, :, 128:256]
    table = nt(eye(128, BF), misc)
    depth[...] = table[0:TAPS, :]
    for k, ref in enumerate((g1, b1, g2, b2)):
        ref[...] = table[16 + k : 17 + k, :].reshape(192)
    kernel[...] = table[64:118, 0:96]


SMEM = pl.BlockSpec(memory_space=pltpu.SMEM)
VMEM = pl.BlockSpec(memory_space=pltpu.VMEM)
ANY = pl.BlockSpec(memory_space=pl.ANY)


def call(kernel, specs, outs, scratch, flops, *args, out_specs=None):
    return pl.pallas_call(
        kernel,
        out_shape=[jax.ShapeDtypeStruct(s, d) for s, d in outs],
        in_specs=specs,
        out_specs=out_specs or [VMEM] * len(outs),
        scratch_shapes=[pltpu.VMEM(s, d) for s, d in scratch[0]] + list(scratch[1:]),
        compiler_params=pltpu.CompilerParams(vmem_limit_bytes=60 << 20),
        cost_estimate=pl.CostEstimate(flops=flops, bytes_accessed=1 << 20, transcendentals=0),
        name=kernel.__name__,
    )(*args)


def forward_mixer(scalars, xl, xs, pieces):
    outs = [
        ((ROWS, D), BF), ((ROWS, 3 * AH), BF),
        ((HEADS, LONG, LONG), BF), ((2, HEADS, SHORT, SHORT), BF),
        ((ROWS, D), BF), ((ROWS, AH), F32), ((ROWS, AH), BF), ((PAD, 128), F32),
        ((PAD, AH), F32), ((ROWS, D), BF), ((24, D), F32),
    ]
    scratch = [((SLOTS, D, 256), BF), ((PAD, D), F32), ((256, AH), BF), ((AH, 128), BF)]
    return call(
        mixer_forward, [SMEM] * 3 + [VMEM] * 2 + [ANY] * 8, outs,
        (scratch + outs[:-1], pltpu.SemaphoreType.DMA, pltpu.SemaphoreType.DMA((10,))), 30 * 10**9,
        *scalars, xl, xs, *pieces, out_specs=[ANY] * 10 + [VMEM],
    )


def feed_forward(scalars, xm, ctx, vec, cl, cs, pieces):
    outs = [
        ((LONG, D), BF), ((2 * SHORT, D), BF), ((4, 4, 240, AH), BF), ((4, 4, 240, AH), BF),
        ((ROWS, D), F32), ((ROWS, D), BF), ((8, D), F32),
    ]
    scratch = [
        ((2, D, AH), BF), ((8, AH, AH), BF), ((8, AH, AH), BF), ((ROWS, D), BF), ((ROWS, D), BF),
        ((ROWS, D), BF), ((ROWS, D), BF), ((ROWS, D), F32), ((ROWS, D), F32),
        ((2, ROWS, AH), BF), ((2, ROWS, AH), BF), ((8, ROWS, AH), BF), ((8, ROWS, AH), F32),
        ((2, ROWS, AH), F32), ((ROWS, 128), F32), ((256, AH), F32), ((256, AH), F32),
        ((ROWS, AH), BF), ((ROWS, AH), BF), ((ROWS, D), BF), ((2, ROWS, AH), BF),
        ((8, AH, AH), BF), ((8, AH, AH), BF), ((ROWS, D), F32), ((ROWS, D), BF), ((32, D), F32),
    ]
    return call(
        ffn_both, [SMEM] * 3 + [VMEM] + [ANY] * 12, outs,
        (scratch, pltpu.SemaphoreType.DMA((7,))), 60 * 10**9,
        *scalars, vec, xm, ctx, cl, cs, *pieces, out_specs=[ANY] * 6 + [VMEM],
    )


def backward_mixer(place, vec, gvec, arrays, pieces):
    outs = [
        ((4, 4, 192, 256), BF), ((4, 4, 192, 256), BF), ((ROWS, 4 * AH), BF), ((PAD, D), F32),
    ]
    scratch = [((SLOTS, D, 256), BF)] + [(a.shape, a.dtype) for a in arrays] + [
        ((PAD, D), F32), ((PAD, AH), F32), ((PAD, D), F32), ((ROWS, 4 * AH), BF),
        ((ROWS, AH), F32), ((2, LONG, 128), F32), ((ROWS, AH), BF), ((ROWS, 128), BF),
        ((8 * TAPS, D), F32), ((SLOTS, D, 256), BF), ((256, AH), BF), ((AH, 128), BF),
        ((AH, 128), BF),
    ]
    dma = pltpu.SemaphoreType.DMA
    return call(
        mixer_backward, [SMEM] + [VMEM] * 2 + [ANY] * 18, outs,
        (scratch, dma, dma((10,)), dma((3,))), 40 * 10**9,
        place, vec, gvec, *arrays, *pieces, out_specs=[ANY] * 4,
    )


def backward_inputs(scalars, vec, grads, gdp, gone, pieces):
    scratch = [
        ((SLOTS, D, 256), BF), ((ROWS, 4 * AH), BF), ((PAD, D), F32), ((ROWS, D), F32),
    ]
    dma = pltpu.SemaphoreType.DMA
    return call(
        input_gradient, [SMEM] * 3 + [VMEM] + [ANY] * 11, [((LONG, D), BF), ((2 * SHORT, D), BF)],
        (scratch, dma, dma((3,))), 5 * 10**9, *scalars, vec, grads, gdp, gone, *pieces,
    )


def far(values, bit):
    return lax.ppermute(values, "narrow", [(i, i ^ bit) for i in range(4)])


def near(values, bit):
    return lax.ppermute(values, "wide", [(i, i ^ bit) for i in range(SLOTS)])


def gather_narrow(piece):
    return jnp.stack([piece] + [far(piece, k) for k in (1, 2, 3)])


def gather_chips(block):
    return [block] + [near(block, k) for k in (2, 4, 6)]


def gather_cores(blocks):
    return blocks + [near(block, 1) for block in blocks]


def total(first, others):
    result = first.astype(F32)
    for other in others:
        result = result + other.astype(F32)
    return result.astype(BF)


def reduce_cores(keep, sent):
    return [total(keep[k], [sent[k]]) for k in range(4)]


def send_chips(parts):
    return [near(parts[k], 2 * k) for k in (1, 2, 3)]


def reduce_chips(first, others):
    return [total(first[k], [other[k] for other in others]) for k in range(4)]


def send_narrow(parts):
    return [far(parts[k], k) for k in (1, 2, 3)]


def gather_wide(parts):
    return lax.all_gather(parts, "wide", axis=0, tiled=False)


def body(
    long_tokens, long_lengths, short_tokens, short_lengths,
    w_qkv, w_depth, w_point, w_kernel, w_convout, w_out, norm1_gain, norm1_bias,
    w_inner, w_outer, norm2_gain, norm2_bias, long_cotangent, short_cotangent,
):
    place = jnp.stack([lax.axis_index("wide"), lax.axis_index("narrow")]).astype(jnp.int32)
    scalars = (place, long_lengths, short_lengths)
    xl, xs = long_tokens.reshape(LONG, D), short_tokens.reshape(2 * SHORT, D)
    cl, cs = long_cotangent.reshape(LONG, D), short_cotangent.reshape(2 * SHORT, D)
    mixer, ffn = call(
        pack, [SMEM] + [VMEM] * 12, [((192, 256), BF), ((240, AH), BF)], ([],), 10**9,
        place, w_qkv, w_depth, w_point, w_kernel.T, w_convout, norm1_gain, norm1_bias,
        w_inner, w_outer, w_out, norm2_gain, norm2_bias,
    )
    mixer = gather_narrow(mixer)
    mixer, ffn = lax.optimization_barrier((mixer, ffn))
    mixer = gather_chips(mixer)
    ffn = gather_narrow(ffn)
    mixer, ffn = lax.optimization_barrier((mixer, ffn))
    mixer = gather_cores(mixer)
    ffn = gather_chips(ffn)
    xm, packed, plong, pshort, dw, kc, cq, kp, cv, ctx, vec = forward_mixer(scalars, xl, xs, mixer)
    ctx, ffn = lax.optimization_barrier((ctx, ffn))
    ffn = gather_cores(ffn)
    ol, os, keep, send, gone, gctx, gvec = feed_forward(scalars, xm, ctx, vec, cl, cs, ffn)
    ga = reduce_cores(keep, near(send, 1))
    ga_sent = send_chips(ga)
    gctx, ga = lax.optimization_barrier((gctx, ga))
    keep, send, grads, gdp = backward_mixer(
        place, vec, gvec, (xm, packed, plong, pshort, dw, kc, cq, kp, cv, gctx), mixer
    )
    keep, send, ga_sent = lax.optimization_barrier((keep, send, ga_sent))
    sent = near(send, 1)
    ga = reduce_chips(ga[0], ga_sent)
    ga_sent = send_narrow(ga)
    gb = reduce_cores(keep, sent)
    gb_sent = send_chips(gb)
    grads, gb = lax.optimization_barrier((grads, gb))
    il, is_ = backward_inputs(scalars, vec, grads, gdp, gone, mixer)
    ga_sent, gb_sent, il = lax.optimization_barrier((ga_sent, gb_sent, il))
    ga = lax.psum(total(ga[0], ga_sent), "hi")
    gb = reduce_chips(gb[0], gb_sent)
    gb = lax.psum(total(gb[0], send_narrow(gb)), "hi")
    inner, outer, out = call(
        unpack_ffn, [VMEM], [((2, 96, 4 * AH), F32), ((2, AH, AH), F32), ((192, D), F32)],
        ([],), 10**9, gather_wide(ga),
    )
    outs = [
        ((192, 3 * AH), F32), ((TAPS, 192), F32), ((192, AH), F32), ((54, 96), F32), ((192, AH), F32),
    ] + [((192,), F32)] * 4
    qkv, depth, point, kernel, convout, g1, b1, g2, b2 = call(
        unpack_mixer, [VMEM], outs, ([],), 10**9, gather_wide(gb)
    )
    return (
        ol.reshape(long_tokens.shape), os.reshape(short_tokens.shape),
        il.reshape(long_tokens.shape), is_.reshape(short_tokens.shape),
        qkv, depth, point, kernel.T, convout, out, g1, b1, inner, outer, g2, b2,
    )


def solution(mesh):
    wide, narrow = mesh.shape["wide"], mesh.shape["narrow"]
    inner_mesh = Mesh(mesh.devices.reshape(wide // SLOTS, SLOTS, narrow), ("hi", "wide", "narrow"))
    every = ("hi", "wide", "narrow")
    rows = P(every, None, None)
    weights = (
        P("narrow", None), P(None, "narrow"), P("narrow", None), P("narrow", None),
        P("narrow", None), P("narrow", None), P("narrow"), P("narrow"),
        P(None, "narrow", None), P(None, "narrow", None), P("narrow"), P("narrow"),
    )
    return jax.shard_map(
        body,
        mesh=inner_mesh,
        in_specs=(rows, P(every), rows, P(every)) + weights + (rows, rows),
        out_specs=(rows, rows, rows, rows) + weights,
        check_vma=False,
    )
```

```python
import jax
import jax.numpy as jnp
from jax import lax
from jax.experimental import pallas as pl
from jax.experimental.pallas import tpu as pltpu
from jax.sharding import Mesh
from jax.sharding import PartitionSpec as P

BF = jnp.bfloat16
F32 = jnp.float32
EPS = 1e-12
D = 768
AH = 384
HEADS = 6
TAPS = 9
LONG = 512
SHORT = 128
ROWS = 768
PAD = 800
SLOTS = 8
NEG = -1000000000.0
PSTART = tuple(8 + 128 * i + 8 * max(i - 3, 0) for i in range(6))
SEGS = ((0, 512, 8), (512, 128, 528), (640, 128, 664))


def nn(a, b):
    return lax.dot_general(a, b, (((1,), (0,)), ((), ())), preferred_element_type=F32)


def nt(a, b):
    return lax.dot_general(a, b, (((1,), (1,)), ((), ())), preferred_element_type=F32)


def tn(a, b):
    return lax.dot_general(a, b, (((0,), (0,)), ((), ())), preferred_element_type=F32)


def iota(shape, axis):
    return lax.broadcasted_iota(jnp.int32, shape, axis)


def loop(count, body):
    def step(i, carry):
        body(i)
        return carry

    lax.fori_loop(0, count, step, 0)


def at(i, size):
    if isinstance(i, int):
        return pl.ds(i * size, size)
    return pl.ds(pl.multiple_of(i * size, size), size)


def padded_start(i):
    return pl.multiple_of(8 + 128 * i + 8 * jnp.maximum(i - 3, 0), 8)


def zero_gaps(ref):
    for start in (0, 520, 656, 792):
        ref[start : start + 8, :] = jnp.zeros((8, ref.shape[1]), ref.dtype)


def eye(n, dtype):
    return jnp.where(iota((n, n), 0) == iota((n, n), 1), 1.0, 0.0).astype(dtype)


def tap_permutation():
    row, col = iota((128, 128), 0), iota((128, 128), 1)
    head, tap = col & 7, col >> 3
    keep = (head < HEADS) & (tap < TAPS) & (row == 64 + head * TAPS + tap)
    return jnp.where(keep, 1.0, 0.0).astype(BF)


def head_spread():
    row, col = iota((256, AH), 0), iota((256, AH), 1)
    return jnp.where((row & 127) == (col >> 6), 1.0, 0.0).astype(BF)


def head_gather():
    row, col = iota((AH, 128), 0), iota((AH, 128), 1)
    return jnp.where((row >> 6) == col, 1.0, 0.0).astype(BF)


def split_two(values):
    high = values.astype(BF)
    low = (values - high.astype(F32)).astype(BF)
    return jnp.concatenate([high, low], axis=1)


def spread_taps(probs):
    moved = [probs] + [pltpu.roll(probs, 128 - 8 * j, 1) for j in range(1, TAPS)]
    return split_two(jnp.concatenate(moved, axis=0))


def tap_kernel(wm):
    stored = jnp.concatenate([wm[7, 192 * n : 192 * n + 96, 128:256] for n in range(4)], axis=0)
    return nn(stored, tap_permutation()).astype(BF)


def slot_of(where, core, chip):
    return 2 * ((where >> 1) ^ chip) + ((where & 1) ^ core)


def fetch_mixer(place, pieces, wm, sem):
    for at_core in range(2):
        for chip in range(4):
            piece = pieces[4 * at_core + chip]
            slot = slot_of(place[0], at_core, chip)

            def fetch(k):
                pltpu.make_async_copy(piece.at[k], wm.at[slot, at(place[1] ^ k, 192), :], sem).start()

            loop(4, fetch)


def mixer_forward(
    place, llen, slen, xl, xs, p0, p1, p2, p3, p4, p5, p6, p7,
    xm_any, packed_any, plong_any, pshort_any, dw_any, kc_any, cq_any, kp_any, cv_any, ctx_any, vec,
    wm, xpad, spread, wk, xm, packed, plong, pshort, dw, kc, cq, kp, cv, ctx, sem, sems
):
    fetch_mixer(place, (p0, p1, p2, p3, p4, p5, p6, p7), wm, sem)
    lens = (llen[0], slen[0], slen[1])
    zero_gaps(xpad)
    zero_gaps(cv)
    zero_gaps(kp)
    for i in range(6):
        seg = max(i - 3, 0)
        base = 128 * i if i < 4 else 0
        tokens = xl[128 * i : 128 * i + 128, :] if i < 4 else xs[128 * (i - 4) : 128 * (i - 3), :]
        live = base + iota((128, D), 0) < lens[seg]
        values = jnp.where(live, tokens.astype(F32), 0.0)
        xpad[PSTART[i] : PSTART[i] + 128, :] = values
        xm[128 * i : 128 * i + 128, :] = values.astype(BF)
    stores = [start_copy(xm, xm_any, sems.at[0])]
    spread[...] = head_spread()
    pltpu.make_async_copy(wm, wm, sem).wait()
    vec[...] = nt(eye(128, BF), wm[7, :, 128:256])[0:24, :]
    wk[...] = tap_kernel(wm)

    def depth(i):
        ps = padded_start(i)
        for c in range(3):
            lanes = slice(256 * c, 256 * c + 256)
            window = xpad[pl.ds(pl.multiple_of(ps - 8, 8), 144), lanes]
            total = jnp.zeros((128, 256), F32)
            for j in range(TAPS):
                total = total + vec[j : j + 1, lanes] * window[4 + j : 132 + j, :]
            dw[at(i, 128), lanes] = total.astype(BF)

    def project(b):
        packed[:, at(b, 256)] = nn(xm[...], wm[b]).astype(BF)
        depth(b)

    loop(4, project)
    depth(jnp.int32(4))
    part = nn(xm[...], wm[4])
    packed[:, 1024:1152] = part[:, 0:128].astype(BF)
    for start, rows, pstart in SEGS:
        cv[pstart : pstart + rows, 0:128] = part[start : start + rows, 128:256]
    depth(jnp.int32(5))
    part = nn(xm[...], wm[5])
    for start, rows, pstart in SEGS:
        cv[pstart : pstart + rows, 128:384] = part[start : start + rows, :]
    stores += [
        start_copy(packed, packed_any, sems.at[1]), start_copy(dw, dw_any, sems.at[2]),
        start_copy(cv, cv_any, sems.at[3]),
    ]
    kc[:, 0:256] = nn(dw[...], wm[6])
    kc[:, 256:384] = nn(dw[...], wm[7, :, 0:128])
    stores.append(start_copy(kc, kc_any, sems.at[4]))

    def dynamic(i):
        rows = at(i, 128)
        ps = padded_start(i)
        query = (kc[rows, :] * packed[rows, 0:AH].astype(F32)).astype(BF)
        cq[rows, :] = query
        logits = nn(query, wk[...])
        real = iota((128, 128), 1) < 8 * TAPS
        top = jnp.where(real, logits, NEG * 1e20)
        for shift in (64, 32, 16, 8):
            top = jnp.maximum(top, pltpu.roll(top, shift, 1))
        ex = jnp.where(real, jnp.exp(logits - top), 0.0)
        total = ex
        for shift in (64, 32, 16, 8):
            total = total + pltpu.roll(total, shift, 1)
        probs = ex / total
        kp[pl.ds(ps, 128), :] = probs
        window = cv[pl.ds(pl.multiple_of(ps - 8, 8), 144), :]
        weights = nn(spread_taps(probs), spread[...])
        out = jnp.zeros((128, AH), F32)
        for j in range(TAPS):
            out = out + weights[128 * j : 128 * j + 128, :] * window[4 + j : 132 + j, :]
        ctx[rows, AH:D] = out.astype(BF)

    loop(6, dynamic)
    stores += [start_copy(cq, cq_any, sems.at[5]), start_copy(kp, kp_any, sems.at[6])]

    def attend(row0, nq, key0, nk, limit, pair, store):
        queries = packed[pl.ds(row0, nq), at(pair, 128)].astype(F32) * 0.125
        keys = packed[pl.ds(key0, nk), at(3 + pair, 128)].astype(F32)
        vals = packed[pl.ds(key0, nk), at(6 + pair, 128)]
        lane, key_lane = iota((nq, 128), 1), iota((nk, 128), 1)
        bias = jnp.where(iota((nk, 128), 0) < limit, 0.0, NEG)
        outs = []
        for hh in range(2):
            spare = 64 * (1 - hh)
            query = jnp.where((lane >> 6) == hh, queries, jnp.where(lane == spare, 1.0, 0.0))
            scores = nt(query.astype(BF), jnp.where(key_lane == spare, bias, keys).astype(BF))
            ex = jnp.exp(scores - jnp.max(scores, axis=1, keepdims=True))
            probs = (ex * (1.0 / jnp.sum(ex, axis=1, keepdims=True))).astype(BF)
            store(hh, probs)
            outs.append(nn(probs, vals))
        both = jnp.where(lane < 64, outs[0], outs[1])
        ctx[pl.ds(row0, nq), at(pair, 128)] = both.astype(BF)

    def long_attend(i):
        pair, block = i >> 1, i & 1
        row0 = pl.multiple_of(block * 256, 256)

        def store(hh, probs):
            plong[2 * pair + hh, pl.ds(row0, 256), :] = probs

        attend(row0, 256, 0, LONG, lens[0], pair, store)

    loop(6, long_attend)
    stores.append(start_copy(plong, plong_any, sems.at[7]))
    for seg in range(2):
        for pair in range(3):

            def store(hh, probs):
                pshort[seg, 2 * pair + hh, :, :] = probs

            row0 = LONG + 128 * seg
            attend(row0, 128, row0, SHORT, lens[1 + seg], pair, store)
    stores += [start_copy(pshort, pshort_any, sems.at[8]), start_copy(ctx, ctx_any, sems.at[9])]
    for copy in stores:
        copy.wait()


def gelu_parts(hidden):
    cdf = 0.5 + 0.5 * lax.erf(hidden * 0.7071067811865476)
    return cdf, jnp.exp(hidden * hidden * -0.5) * 0.3989422804014327


def fold(values):
    return jnp.sum(values.reshape(values.shape[0] // 8, 8, values.shape[1]), axis=0)


def start_copy(source, target, sem):
    copy = pltpu.make_async_copy(source, target, sem)
    copy.start()
    return copy


def ship(keep, send, place, slot, shard, rows, source, sem):
    where = slot ^ place[0]
    chip, far_off = where >> 1, shard ^ place[1]

    @pl.when((where & 1) == 0)
    def _():
        pltpu.make_async_copy(source, keep.at[chip, far_off, rows, :], sem).start()

    @pl.when((where & 1) == 1)
    def _():
        pltpu.make_async_copy(source, send.at[chip, far_off, rows, :], sem).start()


def ffn_both(
    place, llen, slen, vec, xm_any, ctx_any, cl, cs, p0, p1, p2, p3, p4, p5, p6, p7,
    ol, os, keep, send, gone_any, gctx_any, gvec,
    wo, wi, wu, xm, ctx, cot, out, res, xhat, grouped, gffn, active, slope, ffn, rstd,
    hid_a, hid_b, ghid_a, ghid_b, gproj, gout, ginner, gouter, gone, gctx, sums, sems,
):
    loads = [start_copy(ctx_any, ctx, sems.at[3]), start_copy(xm_any, xm, sems.at[4])]

    def fetch(part):
        for core, pieces in enumerate(((p0, p1, p2, p3), (p4, p5, p6, p7))):
            for chip, piece in enumerate(pieces):
                slot = slot_of(place[0], core, chip)
                g, r = slot >> 2, slot & 3

                def one(k):
                    n = place[1] ^ k
                    if part == 0:
                        rows = pl.ds(pl.multiple_of(192 * n + 48 * r, 48), 48)
                        source, target = pl.ds(192, 48), wo.at[g, rows, :]
                    elif part == 1:
                        source, target = pl.ds(0, 96), wi.at[slot >> 1, at(n, 96), at(slot & 1, AH)]
                    else:
                        rows = at(4 * (n & 1) + r, 96)
                        source, target = pl.ds(96, 96), wu.at[2 * g + (n >> 1), rows, :]
                    pltpu.make_async_copy(piece.at[k, source, :], target, sems.at[part]).start()

                loop(4, one)

    for part in range(3):
        fetch(part)
    cots = [
        start_copy(cl, cot.at[0:LONG], sems.at[5]), start_copy(cs, cot.at[LONG:ROWS], sems.at[6])
    ]
    gain_one, bias_one = vec[16:17, :], vec[17:18, :]
    gain_two, bias_two = vec[18:19, :], vec[19:20, :]
    sums[...] = jnp.zeros((32, D), F32)
    ffn[...] = jnp.zeros((2, ROWS, AH), F32)
    for copy in loads:
        copy.wait()
    pltpu.make_async_copy(wo, wo, sems.at[0]).wait()

    def mix(i):
        rows = at(i, 256)
        for c in range(2):
            lanes = slice(AH * c, AH * c + AH)
            res[rows, lanes] = nn(ctx[rows, :], wo[c]) + xm[rows, lanes].astype(F32)

    loop(3, mix)

    def several(i):
        return [at(4 * i + k, 32) for k in range(4)]

    def norm_one(i):
        spots = several(i)
        done = []
        for values in [res[rows, :] for rows in spots]:
            center = values - jnp.mean(values, axis=1, keepdims=True)
            scale = lax.rsqrt(jnp.mean(center * center, axis=1, keepdims=True) + EPS)
            hat = center * scale
            done.append((hat, scale, hat * gain_one + bias_one))
        for rows, (hat, scale, first) in zip(spots, done):
            xhat[rows, :] = hat
            rstd[rows, :] = jnp.broadcast_to(scale, (32, 128))
            res[rows, :] = first
            short = first.astype(BF)
            grouped[0, rows, :] = short[:, 0:AH]
            grouped[1, rows, :] = short[:, AH:D]

    loop(6, norm_one)
    pltpu.make_async_copy(wi, wi, sems.at[1]).wait()
    pltpu.make_async_copy(wu, wu, sems.at[2]).wait()

    def hidden(t, target):
        b = lax.div(t, 3)
        target[...] = nn(grouped[b >> 1, at(t - 3 * b, 256), :], wi[b])

    def outward(t):
        b = lax.div(t, 3)
        rows = at(t - 3 * b, 256)
        ffn[b >> 1, rows, :] += nn(active[b, rows, :], wu[b])

    def act(t, source):
        b = lax.div(t, 3)
        m = t - 3 * b
        for part in range(16):
            values = source[16 * part : 16 * part + 16, :]
            rows = pl.ds(pl.multiple_of(m * 256 + 16 * part, 16), 16)
            cdf, density = gelu_parts(values)
            active[b, rows, :] = (values * cdf).astype(BF)
            slope[b, rows, :] = cdf + values * density

    def pair(u, first=False):
        t = 2 * u
        if not first:
            outward(t - 1)
        hidden(t + 1, hid_b)
        act(t, hid_a)
        outward(t)
        hidden(jnp.minimum(t + 2, 11), hid_a)
        act(t + 1, hid_b)

    hidden(jnp.int32(0), hid_a)
    pair(jnp.int32(0), True)
    loop(5, lambda u: pair(u + 1))
    outward(jnp.int32(11))
    for copy in cots:
        copy.wait()

    def norm_two(i):
        limit = jnp.where(i < 4, llen[0], slen[jnp.clip(i - 4, 0, 1)])
        base = jnp.where(i < 4, 128 * i, 0)
        spots = several(i)
        loaded = [
            (
                jnp.concatenate([ffn[0, rows, :], ffn[1, rows, :]], axis=1) + res[rows, :],
                cot[rows, :].astype(F32),
            )
            for rows in spots
        ]
        done = []
        for k, (values, up) in enumerate(loaded):
            center = values - jnp.mean(values, axis=1, keepdims=True)
            scale = lax.rsqrt(jnp.mean(center * center, axis=1, keepdims=True) + EPS)
            hat = center * scale
            result = (hat * gain_two + bias_two).astype(BF)
            live = base + 32 * k + iota((32, D), 0) < limit
            up = jnp.where(live, up, 0.0)
            gain_part, bias_part = fold(up * hat), fold(up)
            up = up * gain_two
            grad = scale * (
                up
                - jnp.mean(up, axis=1, keepdims=True)
                - hat * jnp.mean(up * hat, axis=1, keepdims=True)
            )
            done.append((result, gain_part, bias_part, grad))
        for rows, (result, _, _, grad) in zip(spots, done):
            out[rows, :] = result
            res[rows, :] = grad
            short = grad.astype(BF)
            gffn[0, rows, :] = short[:, 0:AH]
            gffn[1, rows, :] = short[:, AH:D]
        sums[16:24, :] += done[0][1] + done[1][1] + done[2][1] + done[3][1]
        sums[24:32, :] += done[0][2] + done[1][2] + done[2][2] + done[3][2]

    loop(6, norm_two)
    stores = [
        start_copy(out.at[0:LONG], ol, sems.at[3]), start_copy(out.at[LONG:ROWS], os, sems.at[4])
    ]
    ffn[...] = jnp.zeros((2, ROWS, AH), F32)

    def slopes(b, target):
        for part in range(6):
            rows = slice(128 * part, 128 * part + 128)
            back = nt(gffn[b >> 1, rows, :], wu[b])
            target[rows, :] = (back * slope[b, rows, :]).astype(BF)

    def gradients(b, source):
        g = b >> 1
        gouter[b] = tn(active[b], gffn[g]).astype(BF)
        ginner[b] = tn(grouped[g], source[...]).astype(BF)
        ffn[g] += nt(source[...], wi[b])
        for half in range(2):
            n = 2 * (b & 1) + half
            for w in range(4):
                outer = gouter.at[b, pl.ds(AH * half + 96 * w, 96), :]
                ship(keep, send, place, 4 * g + w, n, pl.ds(96, 96), outer, sems.at[0])
                inner = ginner.at[b, pl.ds(96 * w, 96), pl.ds(AH * half, AH)]
                ship(keep, send, place, 2 * b + half, w, pl.ds(0, 96), inner, sems.at[1])

    slopes(jnp.int32(0), ghid_a)

    def contract(u):
        b = 2 * u
        slopes(b + 1, ghid_b)
        gradients(b, ghid_a)
        slopes(jnp.minimum(b + 2, 3), ghid_a)
        gradients(b + 1, ghid_b)

    loop(2, contract)

    def norm_one_back(i):
        spots = several(i)
        loaded = [
            (
                res[rows, :] + jnp.concatenate([ffn[0, rows, :], ffn[1, rows, :]], axis=1),
                xhat[rows, :], rstd[rows, 0:1],
            )
            for rows in spots
        ]
        done = []
        for up, hat, scale in loaded:
            gain_part, bias_part = fold(up * hat), fold(up)
            up = up * gain_one
            grad = scale * (
                up
                - jnp.mean(up, axis=1, keepdims=True)
                - hat * jnp.mean(up * hat, axis=1, keepdims=True)
            )
            done.append((gain_part, bias_part, grad))
        for rows, (_, _, grad) in zip(spots, done):
            gone[rows, :] = grad
            gproj[rows, :] = grad.astype(BF)
        sums[0:8, :] += done[0][0] + done[1][0] + done[2][0] + done[3][0]
        sums[8:16, :] += done[0][1] + done[1][1] + done[2][1] + done[3][1]

    loop(6, norm_one_back)
    stores.append(start_copy(gone, gone_any, sems.at[5]))
    for k in range(4):
        gvec[k : k + 1, :] = jnp.sum(sums[8 * k : 8 * k + 8, :], axis=0, keepdims=True)
    gvec[4:8, :] = jnp.zeros((4, D), F32)
    for c in range(2):
        gout[c] = tn(ctx[...], gproj[:, AH * c : AH * c + AH]).astype(BF)
        for n in range(4):
            for r in range(4):
                source = gout.at[c, pl.ds(192 * n + 48 * r, 48), :]
                ship(keep, send, place, 4 * c + r, n, pl.ds(192, 48), source, sems.at[2])

    def unmix(i):
        rows = at(i, 256)
        part = nt(gproj[rows, 0:AH], wo[0]) + nt(gproj[rows, AH:D], wo[1])
        gctx[rows, :] = part.astype(BF)

    loop(3, unmix)
    stores.append(start_copy(gctx, gctx_any, sems.at[6]))
    for copy in stores:
        copy.wait()
    pltpu.make_async_copy(gouter, gouter, sems.at[0]).wait()
    pltpu.make_async_copy(ginner, ginner, sems.at[1]).wait()
    pltpu.make_async_copy(gout, gout, sems.at[2]).wait()


def mixer_backward(
    place, vec, gvec, xm_any, packed_any, plong_any, pshort_any, dw_any, kc_any, cq_any, kp_any,
    cv_any, gctx_any, p0, p1, p2, p3, p4, p5, p6, p7,
    keep, send, grads_any, gdep_any,
    wm, xm, packed, plong, pshort, dw, kc, cq, kp, cv, gctx,
    xpad, gcp, gdp, grads, gqc, dkv, gkc, glog, gdep, gb, spread, gather, wk, sem, sems, out_sem,
):
    arrays = (
        (gctx_any, gctx), (kp_any, kp), (cv_any, cv), (packed_any, packed), (kc_any, kc),
        (xm_any, xm), (plong_any, plong), (pshort_any, pshort), (dw_any, dw), (cq_any, cq),
    )
    loads = [start_copy(a, b, sems.at[k]) for k, (a, b) in enumerate(arrays[0:5])]
    fetch_mixer(place, (p0, p1, p2, p3, p4, p5, p6, p7), wm, sem)
    late = [start_copy(a, b, sems.at[5 + k]) for k, (a, b) in enumerate(arrays[5:])]
    zero_gaps(xpad)
    zero_gaps(gcp)
    zero_gaps(gdp)
    spread[...] = head_spread()
    gather[...] = head_gather()
    gdep[...] = jnp.zeros((8 * TAPS, D), F32)
    for copy in loads:
        copy.wait()
    for start, rows, pstart in SEGS:
        gcp[pstart : pstart + rows, :] = gctx[start : start + rows, AH:D].astype(F32)
    pltpu.make_async_copy(wm, wm, sem).wait()
    wk[...] = tap_kernel(wm)

    def dynamic(i):
        rows = at(i, 128)
        ps = padded_start(i)
        wide = pl.ds(pl.multiple_of(ps - 8, 8), 144)
        grad_wide = gcp[wide, :]
        values = cv[wide, :]
        grad = gcp[pl.ds(ps, 128), :]
        weights = nn(spread_taps(kp[wide, :]), spread[...])
        total = jnp.zeros((128, AH), F32)
        parts = []
        for j in range(TAPS):
            part = weights[144 * j : 144 * j + 144, :] * grad_wide
            total = total + part[12 - j : 140 - j, :]
            parts.append((grad * values[4 + j : 132 + j, :]).astype(BF))
        grads[rows, 3 * AH : 4 * AH] = total.astype(BF)
        sums = nn(jnp.concatenate(parts, axis=0), gather[...])
        gprob = sums[0:128, :]
        for j in range(1, TAPS):
            gprob = gprob + pltpu.roll(sums[128 * j : 128 * j + 128, :], 8 * j, 1)
        probs = kp[pl.ds(ps, 128), :]
        inner = probs * gprob
        for shift in (64, 32, 16, 8):
            inner = inner + pltpu.roll(inner, shift, 1)
        glogits = (probs * (gprob - inner)).astype(BF)
        glog[rows, :] = glogits
        gquery = nt(glogits, wk[...])
        gkc[rows, :] = (gquery * packed[rows, 0:AH].astype(F32)).astype(BF)
        gqc[rows, :] = gquery * kc[rows, :]

    loop(6, dynamic)
    for copy in late:
        copy.wait()

    def point_back(c):
        part = nt(gkc[:, 0:256], wm[6, at(c, 256), :])
        part = part + nt(gkc[:, 256:384], wm[7, at(c, 256), 0:128])
        part = part.astype(BF).astype(F32)
        for start, rows, pstart in SEGS:
            gdp[pstart : pstart + rows, at(c, 256)] = part[start : start + rows, :]

    loop(3, point_back)
    copy_depth = start_copy(gdp, gdep_any, out_sem.at[1])

    def attend(row0, nq, key0, nk, pair, load, first):
        queries = packed[pl.ds(row0, nq), at(pair, 128)].astype(F32) * 0.125
        keys = packed[pl.ds(key0, nk), at(3 + pair, 128)]
        vals = packed[pl.ds(key0, nk), at(6 + pair, 128)]
        up = gctx[pl.ds(row0, nq), at(pair, 128)].astype(F32)
        lane = iota((nq, 128), 1)
        outs = []
        gkeys = jnp.zeros((nk, 128), F32)
        gvals = jnp.zeros((nk, 128), F32)
        for hh in range(2):
            mine = (lane >> 6) == hh
            query = jnp.where(mine, queries, 0.0).astype(BF)
            upper = jnp.where(mine, up, 0.0).astype(BF)
            probs_low = load(hh)
            probs = probs_low.astype(F32)
            gprobs = nt(upper, vals)
            inner = jnp.sum(probs * gprobs, axis=1, keepdims=True)
            gscores = (probs * (gprobs - inner)).astype(BF)
            outs.append(nn(gscores, keys))
            gkeys = gkeys + tn(gscores, query)
            gvals = gvals + tn(probs_low, upper)
        both = jnp.where(lane < 64, outs[0], outs[1]) * 0.125
        both = both + gqc[pl.ds(row0, nq), at(pair, 128)]
        grads[pl.ds(row0, nq), at(pair, 128)] = both.astype(BF)
        span = pl.ds(key0, nk)
        if nq == nk:
            grads[span, at(3 + pair, 128)] = gkeys.astype(BF)
            grads[span, at(6 + pair, 128)] = gvals.astype(BF)
        elif first:
            dkv[0] = gkeys
            dkv[1] = gvals
        else:
            grads[span, at(3 + pair, 128)] = (dkv[0] + gkeys).astype(BF)
            grads[span, at(6 + pair, 128)] = (dkv[1] + gvals).astype(BF)

    def long_attend(pair):
        for block in range(2):
            attend(
                256 * block, 256, 0, LONG, pair,
                lambda hh: plong[2 * pair + hh, 256 * block : 256 * block + 256, :],
                block == 0,
            )

    loop(3, long_attend)
    for seg in range(2):
        for pair in range(3):
            row0 = LONG + 128 * seg
            attend(row0, 128, row0, SHORT, pair, lambda hh: pshort[seg, 2 * pair + hh, :, :], True)
    copy_grads = start_copy(grads, grads_any, out_sem.at[2])
    for start, rows, pstart in SEGS:
        xpad[pstart : pstart + rows, :] = xm[start : start + rows, :].astype(F32)

    def release(b):
        for n in range(4):
            where = b ^ place[0]
            chip, far_off = where >> 1, n ^ place[1]
            source = gb.at[b, pl.ds(192 * n, 192), :]

            @pl.when((where & 1) == 0)
            def _():
                pltpu.make_async_copy(source, keep.at[chip, far_off], out_sem.at[0]).start()

            @pl.when((where & 1) == 1)
            def _():
                pltpu.make_async_copy(source, send.at[chip, far_off], out_sem.at[0]).start()

    gb[6] = tn(dw[...], gkc[:, 0:256]).astype(BF)
    release(6)

    def depth(i):
        ps = padded_start(i)
        wide = pl.ds(pl.multiple_of(ps - 8, 8), 144)
        for c in range(3):
            lanes = slice(256 * c, 256 * c + 256)
            tokens = xpad[pl.ds(ps, 128), lanes]
            grad_wide = gdp[wide, lanes]
            for j in range(TAPS):
                gdep[8 * j : 8 * j + 8, lanes] += fold(tokens * grad_wide[12 - j : 140 - j, :])

    def weights(b):
        gb[b] = tn(xm[...], grads[:, at(b, 256)]).astype(BF)
        depth(b)
        release(b)

    loop(6, weights)
    gb[7, :, 0:128] = tn(dw[...], gkc[:, 256:384]).astype(BF)
    taps = [jnp.sum(gdep[8 * j : 8 * j + 8, :], axis=0, keepdims=True) for j in range(TAPS)]
    table = jnp.concatenate(
        taps + [jnp.zeros((7, D), F32), gvec[...], jnp.zeros((104, D), F32)], axis=0
    ).astype(BF)
    misc = tn(table, eye(128, BF))
    gkernel = nt(tn(cq[...], glog[...]).astype(BF), tap_permutation())
    for n in range(4):
        row = 192 * n
        part = misc[row : row + 96, :] + gkernel[96 * n : 96 * n + 96, :]
        gb[7, row : row + 96, 128:256] = part.astype(BF)
        gb[7, row + 96 : row + 192, 128:256] = misc[row + 96 : row + 192, :].astype(BF)
    release(7)
    copy_depth.wait()
    copy_grads.wait()
    pltpu.make_async_copy(gb, gb, out_sem.at[0]).wait()


def input_gradient(
    place, llen, slen, vec, grads_any, gdp_any, gone_any, p0, p1, p2, p3, p4, p5, p6, p7,
    il, is_, wm, grads, gdp, rest, sem, sems
):
    arrays = ((gone_any, rest), (gdp_any, gdp), (grads_any, grads))
    loads = [start_copy(a, b, sems.at[k]) for k, (a, b) in enumerate(arrays)]
    fetch_mixer(place, (p0, p1, p2, p3, p4, p5, p6, p7), wm, sem)
    for copy in loads:
        copy.wait()

    def depth(i):
        ps = padded_start(i)
        for c in range(3):
            lanes = slice(256 * c, 256 * c + 256)
            window = gdp[pl.ds(pl.multiple_of(ps - 8, 8), 144), lanes]
            total = rest[at(i, 128), lanes]
            for j in range(TAPS):
                total = total + vec[j : j + 1, lanes] * window[12 - j : 140 - j, :]
            rest[at(i, 128), lanes] = total

    loop(6, depth)
    pltpu.make_async_copy(wm, wm, sem).wait()

    def inputs(i):
        rows = at(i, 256)
        total = rest[rows, :]
        for b in range(6):
            total = total + nt(grads[rows, 256 * b : 256 * b + 256], wm[b])
        return total

    def inputs_long(i):
        live = i * 256 + iota((256, D), 0) < llen[0]
        il[at(i, 256), :] = jnp.where(live, inputs(i), 0.0).astype(BF)

    loop(2, inputs_long)
    total = inputs(2)
    row = iota((128, D), 0)
    for seg in range(2):
        part = total[128 * seg : 128 * seg + 128, :]
        is_[128 * seg : 128 * seg + 128, :] = jnp.where(row < slen[seg], part, 0.0).astype(BF)


def pack(
    place, qkv, depth, point, kernel, convout, g1, b1, inner, outer, out, g2, b2, mixer, ffn
):
    for w in range(SLOTS):

        @pl.when(place[0] == w)
        def _():
            g, r = w // 4, w % 4
            ffn[0:96, :] = inner[g, :, AH * r : AH * r + AH]
            ffn[96:192, :] = outer[g, 96 * r : 96 * r + 96, :]
            ffn[192:240, :] = out[48 * r : 48 * r + 48, AH * g : AH * g + AH]
            if w < 4:
                mixer[...] = qkv[:, 256 * w : 256 * w + 256]
            elif w == 4:
                mixer[:, 0:128] = qkv[:, 1024:1152]
                mixer[:, 128:256] = convout[:, 0:128]
            elif w == 5:
                mixer[...] = convout[:, 128:384]
            elif w == 6:
                mixer[...] = point[:, 0:256]
            else:
                mixer[:, 0:128] = point[:, 256:384]
                rows = [v[...].astype(F32).reshape(1, 192) for v in (g1, b1, g2, b2)]
                table = jnp.concatenate(
                    [depth[...].astype(F32), jnp.zeros((7, 192), F32)]
                    + rows
                    + [jnp.zeros((108, 192), F32)],
                    axis=0,
                )
                left = tn(table.astype(BF), eye(128, BF))
                row, col = iota((54, 128), 0), iota((54, 128), 1)
                right = tn(kernel[...], jnp.where(col == row + 64, 1.0, 0.0).astype(BF))
                mixer[0:96, 128:256] = (left[0:96, :] + right).astype(BF)
                mixer[96:192, 128:256] = left[96:192, :].astype(BF)


def unpack_ffn(place, p0, p1, p2, p3, p4, p5, p6, p7, inner, outer, out):
    for core, pieces in enumerate(((p0, p1, p2, p3), (p4, p5, p6, p7))):
        for chip, piece in enumerate(pieces):
            slot = slot_of(place[0], core, chip)
            g, r = slot >> 2, slot & 3
            inner[g, :, at(r, AH)] = piece[0:96, :].astype(F32)
            outer[g, at(r, 96), :] = piece[96:192, :].astype(F32)
            out[at(r, 48), at(g, AH)] = piece[192:240, :].astype(F32)


def unpack_mixer(packed, qkv, depth, point, kernel, convout, g1, b1, g2, b2):
    for w in range(4):
        qkv[:, 256 * w : 256 * w + 256] = packed[w].astype(F32)
    qkv[:, 1024:1152] = packed[4, :, 0:128].astype(F32)
    convout[:, 0:128] = packed[4, :, 128:256].astype(F32)
    convout[:, 128:384] = packed[5].astype(F32)
    point[:, 0:256] = packed[6].astype(F32)
    point[:, 256:384] = packed[7, :, 0:128].astype(F32)
    misc = packed[7, :, 128:256]
    table = nt(eye(128, BF), misc)
    depth[...] = table[0:TAPS, :]
    for k, ref in enumerate((g1, b1, g2, b2)):
        ref[...] = table[16 + k : 17 + k, :].reshape(192)
    kernel[...] = table[64:118, 0:96]


SMEM = pl.BlockSpec(memory_space=pltpu.SMEM)
VMEM = pl.BlockSpec(memory_space=pltpu.VMEM)
ANY = pl.BlockSpec(memory_space=pl.ANY)


def call(kernel, specs, outs, scratch, flops, *args, out_specs=None):
    return pl.pallas_call(
        kernel,
        out_shape=[jax.ShapeDtypeStruct(s, d) for s, d in outs],
        in_specs=specs,
        out_specs=out_specs or [VMEM] * len(outs),
        scratch_shapes=[pltpu.VMEM(s, d) for s, d in scratch[0]] + list(scratch[1:]),
        compiler_params=pltpu.CompilerParams(vmem_limit_bytes=60 << 20),
        cost_estimate=pl.CostEstimate(flops=flops, bytes_accessed=1 << 20, transcendentals=0),
        name=kernel.__name__,
    )(*args)


def forward_mixer(scalars, xl, xs, pieces):
    outs = [
        ((ROWS, D), BF), ((ROWS, 3 * AH), BF),
        ((HEADS, LONG, LONG), BF), ((2, HEADS, SHORT, SHORT), BF),
        ((ROWS, D), BF), ((ROWS, AH), F32), ((ROWS, AH), BF), ((PAD, 128), F32),
        ((PAD, AH), F32), ((ROWS, D), BF), ((24, D), F32),
    ]
    scratch = [((SLOTS, D, 256), BF), ((PAD, D), F32), ((256, AH), BF), ((AH, 128), BF)]
    return call(
        mixer_forward, [SMEM] * 3 + [VMEM] * 2 + [ANY] * 8, outs,
        (scratch + outs[:-1], pltpu.SemaphoreType.DMA, pltpu.SemaphoreType.DMA((10,))), 30 * 10**9,
        *scalars, xl, xs, *pieces, out_specs=[ANY] * 10 + [VMEM],
    )


def feed_forward(scalars, xm, ctx, vec, cl, cs, pieces):
    outs = [
        ((LONG, D), BF), ((2 * SHORT, D), BF), ((4, 4, 240, AH), BF), ((4, 4, 240, AH), BF),
        ((ROWS, D), F32), ((ROWS, D), BF), ((8, D), F32),
    ]
    scratch = [
        ((2, D, AH), BF), ((4, AH, D), BF), ((4, D, AH), BF), ((ROWS, D), BF), ((ROWS, D), BF),
        ((ROWS, D), BF), ((ROWS, D), BF), ((ROWS, D), F32), ((ROWS, D), F32),
        ((2, ROWS, AH), BF), ((2, ROWS, AH), BF), ((4, ROWS, D), BF), ((4, ROWS, D), F32),
        ((2, ROWS, AH), F32), ((ROWS, 128), F32), ((256, D), F32), ((256, D), F32),
        ((ROWS, D), BF), ((ROWS, D), BF), ((ROWS, D), BF), ((2, ROWS, AH), BF),
        ((4, AH, D), BF), ((4, D, AH), BF), ((ROWS, D), F32), ((ROWS, D), BF), ((32, D), F32),
    ]
    return call(
        ffn_both, [SMEM] * 3 + [VMEM] + [ANY] * 12, outs,
        (scratch, pltpu.SemaphoreType.DMA((7,))), 60 * 10**9,
        *scalars, vec, xm, ctx, cl, cs, *pieces, out_specs=[ANY] * 6 + [VMEM],
    )


def backward_mixer(place, vec, gvec, arrays, pieces):
    outs = [
        ((4, 4, 192, 256), BF), ((4, 4, 192, 256), BF), ((ROWS, 4 * AH), BF), ((PAD, D), F32),
    ]
    scratch = [((SLOTS, D, 256), BF)] + [(a.shape, a.dtype) for a in arrays] + [
        ((PAD, D), F32), ((PAD, AH), F32), ((PAD, D), F32), ((ROWS, 4 * AH), BF),
        ((ROWS, AH), F32), ((2, LONG, 128), F32), ((ROWS, AH), BF), ((ROWS, 128), BF),
        ((8 * TAPS, D), F32), ((SLOTS, D, 256), BF), ((256, AH), BF), ((AH, 128), BF),
        ((AH, 128), BF),
    ]
    dma = pltpu.SemaphoreType.DMA
    return call(
        mixer_backward, [SMEM] + [VMEM] * 2 + [ANY] * 18, outs,
        (scratch, dma, dma((10,)), dma((3,))), 40 * 10**9,
        place, vec, gvec, *arrays, *pieces, out_specs=[ANY] * 4,
    )


def backward_inputs(scalars, vec, grads, gdp, gone, pieces):
    scratch = [
        ((SLOTS, D, 256), BF), ((ROWS, 4 * AH), BF), ((PAD, D), F32), ((ROWS, D), F32),
    ]
    dma = pltpu.SemaphoreType.DMA
    return call(
        input_gradient, [SMEM] * 3 + [VMEM] + [ANY] * 11, [((LONG, D), BF), ((2 * SHORT, D), BF)],
        (scratch, dma, dma((3,))), 5 * 10**9, *scalars, vec, grads, gdp, gone, *pieces,
    )


def far(values, bit):
    return lax.ppermute(values, "narrow", [(i, i ^ bit) for i in range(4)])


def near(values, bit):
    return lax.ppermute(values, "wide", [(i, i ^ bit) for i in range(SLOTS)])


def gather_narrow(piece):
    return jnp.stack([piece] + [far(piece, k) for k in (1, 2, 3)])


def gather_chips(block):
    return [block] + [near(block, k) for k in (2, 4, 6)]


def gather_cores(blocks):
    return blocks + [near(block, 1) for block in blocks]


def total(first, others):
    result = first.astype(F32)
    for other in others:
        result = result + other.astype(F32)
    return result.astype(BF)


def reduce_cores(keep, sent):
    return [total(keep[k], [sent[k]]) for k in range(4)]


def send_chips(parts):
    return [near(parts[k], 2 * k) for k in (1, 2, 3)]


def reduce_chips(first, others):
    return [total(first[k], [other[k] for other in others]) for k in range(4)]


def send_narrow(parts):
    return [far(parts[k], k) for k in (1, 2, 3)]


def gather_wide(parts):
    return lax.all_gather(parts, "wide", axis=0, tiled=False)


def body(
    long_tokens, long_lengths, short_tokens, short_lengths,
    w_qkv, w_depth, w_point, w_kernel, w_convout, w_out, norm1_gain, norm1_bias,
    w_inner, w_outer, norm2_gain, norm2_bias, long_cotangent, short_cotangent,
):
    place = jnp.stack([lax.axis_index("wide"), lax.axis_index("narrow")]).astype(jnp.int32)
    scalars = (place, long_lengths, short_lengths)
    xl, xs = long_tokens.reshape(LONG, D), short_tokens.reshape(2 * SHORT, D)
    cl, cs = long_cotangent.reshape(LONG, D), short_cotangent.reshape(2 * SHORT, D)
    mixer, ffn = call(
        pack, [SMEM] + [VMEM] * 12, [((192, 256), BF), ((240, AH), BF)], ([],), 10**9,
        place, w_qkv, w_depth, w_point, w_kernel.T, w_convout, norm1_gain, norm1_bias,
        w_inner, w_outer, w_out, norm2_gain, norm2_bias,
    )
    mixer = gather_narrow(mixer)
    mixer, ffn = lax.optimization_barrier((mixer, ffn))
    mixer = gather_chips(mixer)
    ffn = gather_narrow(ffn)
    mixer, ffn = lax.optimization_barrier((mixer, ffn))
    mixer = gather_cores(mixer)
    ffn = gather_chips(ffn)
    xm, packed, plong, pshort, dw, kc, cq, kp, cv, ctx, vec = forward_mixer(scalars, xl, xs, mixer)
    ctx, ffn = lax.optimization_barrier((ctx, ffn))
    ffn = gather_cores(ffn)
    ol, os, keep, send, gone, gctx, gvec = feed_forward(scalars, xm, ctx, vec, cl, cs, ffn)
    ga = reduce_cores(keep, near(send, 1))
    ga_sent = send_chips(ga)
    gctx, ga = lax.optimization_barrier((gctx, ga))
    keep, send, grads, gdp = backward_mixer(
        place, vec, gvec, (xm, packed, plong, pshort, dw, kc, cq, kp, cv, gctx), mixer
    )
    keep, send, ga_sent = lax.optimization_barrier((keep, send, ga_sent))
    sent = near(send, 1)
    ga = reduce_chips(ga[0], ga_sent)
    ga_sent = send_narrow(ga)
    gb = reduce_cores(keep, sent)
    gb_sent = send_chips(gb)
    grads, gb = lax.optimization_barrier((grads, gb))
    il, is_ = backward_inputs(scalars, vec, grads, gdp, gone, mixer)
    ga_sent, gb_sent, il = lax.optimization_barrier((ga_sent, gb_sent, il))
    ga = lax.psum(total(ga[0], ga_sent), "hi")
    gb = reduce_chips(gb[0], gb_sent)
    gb = lax.psum(total(gb[0], send_narrow(gb)), "hi")
    inner, outer, out = call(
        unpack_ffn, [SMEM] + [VMEM] * 8,
        [((2, 96, 4 * AH), F32), ((2, AH, AH), F32), ((192, D), F32)],
        ([],), 10**9, place, *gather_cores(gather_chips(ga)),
    )
    outs = [
        ((192, 3 * AH), F32), ((TAPS, 192), F32), ((192, AH), F32), ((54, 96), F32), ((192, AH), F32),
    ] + [((192,), F32)] * 4
    qkv, depth, point, kernel, convout, g1, b1, g2, b2 = call(
        unpack_mixer, [VMEM], outs, ([],), 10**9, gather_wide(gb)
    )
    return (
        ol.reshape(long_tokens.shape), os.reshape(short_tokens.shape),
        il.reshape(long_tokens.shape), is_.reshape(short_tokens.shape),
        qkv, depth, point, kernel.T, convout, out, g1, b1, inner, outer, g2, b2,
    )


def solution(mesh):
    wide, narrow = mesh.shape["wide"], mesh.shape["narrow"]
    inner_mesh = Mesh(mesh.devices.reshape(wide // SLOTS, SLOTS, narrow), ("hi", "wide", "narrow"))
    every = ("hi", "wide", "narrow")
    rows = P(every, None, None)
    weights = (
        P("narrow", None), P(None, "narrow"), P("narrow", None), P("narrow", None),
        P("narrow", None), P("narrow", None), P("narrow"), P("narrow"),
        P(None, "narrow", None), P(None, "narrow", None), P("narrow"), P("narrow"),
    )
    return jax.shard_map(
        body,
        mesh=inner_mesh,
        in_specs=(rows, P(every), rows, P(every)) + weights + (rows, rows),
        out_specs=(rows, rows, rows, rows) + weights,
        check_vma=False,
    )
```

```python
import jax
import jax.numpy as jnp
from jax import lax
from jax.experimental import pallas as pl
from jax.experimental.pallas import tpu as pltpu
from jax.sharding import Mesh
from jax.sharding import PartitionSpec as P

BF = jnp.bfloat16
F32 = jnp.float32
EPS = 1e-12
D = 768
AH = 384
HEADS = 6
TAPS = 9
LONG = 512
SHORT = 128
ROWS = 768
PAD = 800
SLOTS = 8
NEG = -1000000000.0
PSTART = tuple(8 + 128 * i + 8 * max(i - 3, 0) for i in range(6))
SEGS = ((0, 512, 8), (512, 128, 528), (640, 128, 664))


def nn(a, b):
    return lax.dot_general(a, b, (((1,), (0,)), ((), ())), preferred_element_type=F32)


def nt(a, b):
    return lax.dot_general(a, b, (((1,), (1,)), ((), ())), preferred_element_type=F32)


def tn(a, b):
    return lax.dot_general(a, b, (((0,), (0,)), ((), ())), preferred_element_type=F32)


def iota(shape, axis):
    return lax.broadcasted_iota(jnp.int32, shape, axis)


def loop(count, body):
    def step(i, carry):
        body(i)
        return carry

    lax.fori_loop(0, count, step, 0)


def at(i, size):
    if isinstance(i, int):
        return pl.ds(i * size, size)
    return pl.ds(pl.multiple_of(i * size, size), size)


def padded_start(i):
    return pl.multiple_of(8 + 128 * i + 8 * jnp.maximum(i - 3, 0), 8)


def zero_gaps(ref):
    for start in (0, 520, 656, 792):
        ref[start : start + 8, :] = jnp.zeros((8, ref.shape[1]), ref.dtype)


def eye(n, dtype):
    return jnp.where(iota((n, n), 0) == iota((n, n), 1), 1.0, 0.0).astype(dtype)


def tap_permutation():
    row, col = iota((128, 128), 0), iota((128, 128), 1)
    head, tap = col & 7, col >> 3
    keep = (head < HEADS) & (tap < TAPS) & (row == 64 + head * TAPS + tap)
    return jnp.where(keep, 1.0, 0.0).astype(BF)


def head_spread():
    row, col = iota((256, AH), 0), iota((256, AH), 1)
    return jnp.where((row & 127) == (col >> 6), 1.0, 0.0).astype(BF)


def head_gather():
    row, col = iota((AH, 128), 0), iota((AH, 128), 1)
    return jnp.where((row >> 6) == col, 1.0, 0.0).astype(BF)


def split_two(values):
    high = values.astype(BF)
    low = (values - high.astype(F32)).astype(BF)
    return jnp.concatenate([high, low], axis=1)


def spread_taps(probs):
    moved = [probs] + [pltpu.roll(probs, 128 - 8 * j, 1) for j in range(1, TAPS)]
    return split_two(jnp.concatenate(moved, axis=0))


def tap_kernel(wm):
    stored = jnp.concatenate([wm[7, 192 * n : 192 * n + 96, 128:256] for n in range(4)], axis=0)
    return nn(stored, tap_permutation()).astype(BF)


def slot_of(where, core, chip):
    return 2 * ((where >> 1) ^ chip) + ((where & 1) ^ core)


def fetch_mixer(place, pieces, wm, sem):
    for at_core in range(2):
        for chip in range(4):
            piece = pieces[4 * at_core + chip]
            slot = slot_of(place[0], at_core, chip)

            def fetch(k):
                pltpu.make_async_copy(piece.at[k], wm.at[slot, at(place[1] ^ k, 192), :], sem).start()

            loop(4, fetch)


def mixer_forward(
    place, llen, slen, xl, xs, p0, p1, p2, p3, p4, p5, p6, p7,
    xm_any, packed_any, plong_any, pshort_any, dw_any, kc_any, cq_any, kp_any, cv_any, ctx_any, vec,
    wm, xpad, spread, wk, xm, packed, plong, pshort, dw, kc, cq, kp, cv, ctx, sem, sems
):
    fetch_mixer(place, (p0, p1, p2, p3, p4, p5, p6, p7), wm, sem)
    lens = (llen[0], slen[0], slen[1])
    zero_gaps(xpad)
    zero_gaps(cv)
    zero_gaps(kp)
    for i in range(6):
        seg = max(i - 3, 0)
        base = 128 * i if i < 4 else 0
        tokens = xl[128 * i : 128 * i + 128, :] if i < 4 else xs[128 * (i - 4) : 128 * (i - 3), :]
        live = base + iota((128, D), 0) < lens[seg]
        values = jnp.where(live, tokens.astype(F32), 0.0)
        xpad[PSTART[i] : PSTART[i] + 128, :] = values
        xm[128 * i : 128 * i + 128, :] = values.astype(BF)
    stores = [start_copy(xm, xm_any, sems.at[0])]
    spread[...] = head_spread()
    pltpu.make_async_copy(wm, wm, sem).wait()
    vec[...] = nt(eye(128, BF), wm[7, :, 128:256])[0:24, :]
    wk[...] = tap_kernel(wm)

    def depth(i):
        ps = padded_start(i)
        for c in range(6):
            lanes = slice(128 * c, 128 * c + 128)
            window = xpad[pl.ds(pl.multiple_of(ps - 8, 8), 144), lanes]
            total = jnp.zeros((128, 128), F32)
            for j in range(TAPS):
                total = total + vec[j : j + 1, lanes] * window[4 + j : 132 + j, :]
            dw[at(i, 128), lanes] = total.astype(BF)

    def project(b):
        packed[:, at(b, 256)] = nn(xm[...], wm[b]).astype(BF)
        depth(b)

    loop(4, project)
    depth(jnp.int32(4))
    part = nn(xm[...], wm[4])
    packed[:, 1024:1152] = part[:, 0:128].astype(BF)
    for start, rows, pstart in SEGS:
        cv[pstart : pstart + rows, 0:128] = part[start : start + rows, 128:256]
    depth(jnp.int32(5))
    part = nn(xm[...], wm[5])
    for start, rows, pstart in SEGS:
        cv[pstart : pstart + rows, 128:384] = part[start : start + rows, :]
    stores += [
        start_copy(packed, packed_any, sems.at[1]), start_copy(dw, dw_any, sems.at[2]),
        start_copy(cv, cv_any, sems.at[3]),
    ]
    kc[:, 0:256] = nn(dw[...], wm[6])
    kc[:, 256:384] = nn(dw[...], wm[7, :, 0:128])
    stores.append(start_copy(kc, kc_any, sems.at[4]))

    def tap_softmax(i):
        rows = at(i, 384)
        query = (kc[rows, :] * packed[rows, 0:AH].astype(F32)).astype(BF)
        cq[rows, :] = query
        logits = nn(query, wk[...])
        real = iota((384, 128), 1) < 8 * TAPS
        top = jnp.where(real, logits, NEG * 1e20)
        for shift in (64, 32, 16, 8):
            top = jnp.maximum(top, pltpu.roll(top, shift, 1))
        ex = jnp.where(real, jnp.exp(logits - top), 0.0)
        total = ex
        for shift in (64, 32, 16, 8):
            total = total + pltpu.roll(total, shift, 1)
        probs = ex * (1.0 / total)
        for k in range(3):
            kp[pl.ds(padded_start(3 * i + k), 128), :] = probs[128 * k : 128 * k + 128, :]

    loop(2, tap_softmax)

    def dynamic(u):
        for i in (2 * u, 2 * u + 1):
            ps = padded_start(i)
            weights = nn(spread_taps(kp[pl.ds(ps, 128), :]), spread[...])
            for c in range(3):
                lanes = slice(128 * c, 128 * c + 128)
                window = cv[pl.ds(pl.multiple_of(ps - 8, 8), 144), lanes]
                out = jnp.zeros((128, 128), F32)
                for j in range(TAPS):
                    out = out + weights[128 * j : 128 * j + 128, lanes] * window[4 + j : 132 + j, :]
                ctx[at(i, 128), AH + 128 * c : AH + 128 * c + 128] = out.astype(BF)

    loop(3, dynamic)
    stores += [start_copy(cq, cq_any, sems.at[5]), start_copy(kp, kp_any, sems.at[6])]

    def attend(row0, nq, key0, nk, limit, pair, store):
        queries = packed[pl.ds(row0, nq), at(pair, 128)].astype(F32) * 0.125
        keys = packed[pl.ds(key0, nk), at(3 + pair, 128)].astype(F32)
        vals = packed[pl.ds(key0, nk), at(6 + pair, 128)]
        lane, key_lane = iota((nq, 128), 1), iota((nk, 128), 1)
        bias = jnp.where(iota((nk, 128), 0) < limit, 0.0, NEG)
        outs = []
        for hh in range(2):
            spare = 64 * (1 - hh)
            query = jnp.where((lane >> 6) == hh, queries, jnp.where(lane == spare, 1.0, 0.0))
            scores = nt(query.astype(BF), jnp.where(key_lane == spare, bias, keys).astype(BF))
            parts = []
            for r in range(0, nq, 32):
                part = scores[r : r + 32, :]
                part = jnp.exp(part - jnp.max(part, axis=1, keepdims=True))
                part = part * (1.0 / jnp.sum(part, axis=1, keepdims=True))
                parts.append(part.astype(BF))
            probs = jnp.concatenate(parts, axis=0)
            store(hh, probs)
            outs.append(nn(probs, vals))
        both = jnp.where(lane < 64, outs[0], outs[1])
        ctx[pl.ds(row0, nq), at(pair, 128)] = both.astype(BF)

    def long_attend(i):
        pair, block = i >> 1, i & 1
        row0 = pl.multiple_of(block * 256, 256)

        def store(hh, probs):
            plong[2 * pair + hh, pl.ds(row0, 256), :] = probs

        attend(row0, 256, 0, LONG, lens[0], pair, store)

    loop(6, long_attend)
    stores.append(start_copy(plong, plong_any, sems.at[7]))
    for seg in range(2):
        for pair in range(3):

            def store(hh, probs):
                pshort[seg, 2 * pair + hh, :, :] = probs

            row0 = LONG + 128 * seg
            attend(row0, 128, row0, SHORT, lens[1 + seg], pair, store)
    stores += [start_copy(pshort, pshort_any, sems.at[8]), start_copy(ctx, ctx_any, sems.at[9])]
    for copy in stores:
        copy.wait()


def gelu_parts(hidden):
    cdf = 0.5 + 0.5 * lax.erf(hidden * 0.7071067811865476)
    return cdf, jnp.exp(hidden * hidden * -0.5) * 0.3989422804014327


def fold(values):
    return jnp.sum(values.reshape(values.shape[0] // 8, 8, values.shape[1]), axis=0)


def start_copy(source, target, sem):
    copy = pltpu.make_async_copy(source, target, sem)
    copy.start()
    return copy


def ship(keep, send, place, slot, shard, rows, source, sem):
    where = slot ^ place[0]
    chip, far_off = where >> 1, shard ^ place[1]

    @pl.when((where & 1) == 0)
    def _():
        pltpu.make_async_copy(source, keep.at[chip, far_off, rows, :], sem).start()

    @pl.when((where & 1) == 1)
    def _():
        pltpu.make_async_copy(source, send.at[chip, far_off, rows, :], sem).start()


def ffn_both(
    place, llen, slen, vec, xm_any, ctx_any, cl, cs, p0, p1, p2, p3, p4, p5, p6, p7,
    ol, os, keep, send, gone_any, gctx_any, gvec,
    wo, wi, wu, xm, ctx, cot, out, res, xhat, grouped, gffn, active, slope, ffn, rstd,
    hid_a, hid_b, ghid_a, ghid_b, gproj, gout, ginner, gouter, gone, gctx, sums, sems,
):
    loads = [start_copy(ctx_any, ctx, sems.at[3]), start_copy(xm_any, xm, sems.at[4])]

    def fetch(part):
        for core, pieces in enumerate(((p0, p1, p2, p3), (p4, p5, p6, p7))):
            for chip, piece in enumerate(pieces):
                slot = slot_of(place[0], core, chip)
                g, r = slot >> 2, slot & 3

                def one(k):
                    n = place[1] ^ k
                    if part == 0:
                        rows = pl.ds(pl.multiple_of(192 * n + 48 * r, 48), 48)
                        source, target = pl.ds(192, 48), wo.at[g, rows, :]
                    elif part == 1:
                        source, target = pl.ds(0, 96), wi.at[slot >> 1, at(n, 96), at(slot & 1, AH)]
                    else:
                        rows = at(4 * (n & 1) + r, 96)
                        source, target = pl.ds(96, 96), wu.at[2 * g + (n >> 1), rows, :]
                    pltpu.make_async_copy(piece.at[k, source, :], target, sems.at[part]).start()

                loop(4, one)

    fetch(0)
    gain_one, bias_one = vec[16:17, :], vec[17:18, :]
    gain_two, bias_two = vec[18:19, :], vec[19:20, :]
    sums[...] = jnp.zeros((32, D), F32)
    ffn[...] = jnp.zeros((2, ROWS, AH), F32)
    for copy in loads:
        copy.wait()
    pltpu.make_async_copy(wo, wo, sems.at[0]).wait()
    fetch(1)
    fetch(2)
    cots = [
        start_copy(cl, cot.at[0:LONG], sems.at[5]), start_copy(cs, cot.at[LONG:ROWS], sems.at[6])
    ]

    def mix(i):
        rows = at(i, 256)
        for c in range(2):
            lanes = slice(AH * c, AH * c + AH)
            res[rows, lanes] = nn(ctx[rows, :], wo[c]) + xm[rows, lanes].astype(F32)

    def several(i):
        return [at(4 * i + k, 32) for k in range(4)]

    def norm_one(i):
        spots = several(i)
        done = []
        for values in [res[rows, :] for rows in spots]:
            center = values - jnp.mean(values, axis=1, keepdims=True)
            scale = lax.rsqrt(jnp.mean(center * center, axis=1, keepdims=True) + EPS)
            hat = center * scale
            done.append((hat, scale, hat * gain_one + bias_one))
        for rows, (hat, scale, first) in zip(spots, done):
            xhat[rows, :] = hat
            rstd[rows, :] = jnp.broadcast_to(scale, (32, 128))
            res[rows, :] = first
            short = first.astype(BF)
            grouped[0, rows, :] = short[:, 0:AH]
            grouped[1, rows, :] = short[:, AH:D]

    mix(0)
    for tile in range(3):
        if tile < 2:
            mix(tile + 1)
        norm_one(2 * tile)
        norm_one(2 * tile + 1)
    pltpu.make_async_copy(wi, wi, sems.at[1]).wait()
    pltpu.make_async_copy(wu, wu, sems.at[2]).wait()

    def hidden(t, target):
        b = lax.div(t, 3)
        target[...] = nn(grouped[b >> 1, at(t - 3 * b, 256), :], wi[b])

    def outward(t):
        b = lax.div(t, 3)
        rows = at(t - 3 * b, 256)
        ffn[b >> 1, rows, :] += nn(active[b, rows, :], wu[b])

    def act(t, source):
        b = lax.div(t, 3)
        m = t - 3 * b
        for part in range(16):
            values = source[16 * part : 16 * part + 16, :]
            rows = pl.ds(pl.multiple_of(m * 256 + 16 * part, 16), 16)
            cdf, density = gelu_parts(values)
            active[b, rows, :] = (values * cdf).astype(BF)
            slope[b, rows, :] = cdf + values * density

    def pair(u, first=False):
        t = 2 * u
        if not first:
            outward(t - 1)
        hidden(t + 1, hid_b)
        act(t, hid_a)
        outward(t)
        hidden(jnp.minimum(t + 2, 11), hid_a)
        act(t + 1, hid_b)

    hidden(jnp.int32(0), hid_a)
    pair(jnp.int32(0), True)
    loop(5, lambda u: pair(u + 1))
    outward(jnp.int32(11))
    for copy in cots:
        copy.wait()

    def norm_two(i):
        limit = jnp.where(i < 4, llen[0], slen[jnp.clip(i - 4, 0, 1)])
        base = jnp.where(i < 4, 128 * i, 0)
        spots = several(i)
        loaded = [
            (
                jnp.concatenate([ffn[0, rows, :], ffn[1, rows, :]], axis=1) + res[rows, :],
                cot[rows, :].astype(F32),
            )
            for rows in spots
        ]
        done = []
        for k, (values, up) in enumerate(loaded):
            center = values - jnp.mean(values, axis=1, keepdims=True)
            scale = lax.rsqrt(jnp.mean(center * center, axis=1, keepdims=True) + EPS)
            hat = center * scale
            result = (hat * gain_two + bias_two).astype(BF)
            live = base + 32 * k + iota((32, D), 0) < limit
            up = jnp.where(live, up, 0.0)
            gain_part, bias_part = fold(up * hat), fold(up)
            up = up * gain_two
            grad = scale * (
                up
                - jnp.mean(up, axis=1, keepdims=True)
                - hat * jnp.mean(up * hat, axis=1, keepdims=True)
            )
            done.append((result, gain_part, bias_part, grad))
        for rows, (result, _, _, grad) in zip(spots, done):
            out[rows, :] = result
            res[rows, :] = grad
            short = grad.astype(BF)
            gffn[0, rows, :] = short[:, 0:AH]
            gffn[1, rows, :] = short[:, AH:D]
        sums[16:24, :] += done[0][1] + done[1][1] + done[2][1] + done[3][1]
        sums[24:32, :] += done[0][2] + done[1][2] + done[2][2] + done[3][2]

    loop(6, norm_two)
    stores = [
        start_copy(out.at[0:LONG], ol, sems.at[3]), start_copy(out.at[LONG:ROWS], os, sems.at[4])
    ]
    ffn[...] = jnp.zeros((2, ROWS, AH), F32)

    def slopes(b, target):
        for part in range(6):
            rows = slice(128 * part, 128 * part + 128)
            back = nt(gffn[b >> 1, rows, :], wu[b])
            target[rows, :] = (back * slope[b, rows, :]).astype(BF)

    def gradients(b, source):
        g = b >> 1
        gouter[b] = tn(active[b], gffn[g]).astype(BF)
        ginner[b] = tn(grouped[g], source[...]).astype(BF)
        ffn[g] += nt(source[...], wi[b])
        for half in range(2):
            n = 2 * (b & 1) + half
            for w in range(4):
                outer = gouter.at[b, pl.ds(AH * half + 96 * w, 96), :]
                ship(keep, send, place, 4 * g + w, n, pl.ds(96, 96), outer, sems.at[0])
                inner = ginner.at[b, pl.ds(96 * w, 96), pl.ds(AH * half, AH)]
                ship(keep, send, place, 2 * b + half, w, pl.ds(0, 96), inner, sems.at[1])

    slopes(jnp.int32(0), ghid_a)

    def contract(u):
        b = 2 * u
        slopes(b + 1, ghid_b)
        gradients(b, ghid_a)
        slopes(jnp.minimum(b + 2, 3), ghid_a)
        gradients(b + 1, ghid_b)

    loop(2, contract)

    def norm_one_back(i):
        spots = several(i)
        loaded = [
            (
                res[rows, :] + jnp.concatenate([ffn[0, rows, :], ffn[1, rows, :]], axis=1),
                xhat[rows, :], rstd[rows, 0:1],
            )
            for rows in spots
        ]
        done = []
        for up, hat, scale in loaded:
            gain_part, bias_part = fold(up * hat), fold(up)
            up = up * gain_one
            grad = scale * (
                up
                - jnp.mean(up, axis=1, keepdims=True)
                - hat * jnp.mean(up * hat, axis=1, keepdims=True)
            )
            done.append((gain_part, bias_part, grad))
        for rows, (_, _, grad) in zip(spots, done):
            gone[rows, :] = grad
            gproj[rows, :] = grad.astype(BF)
        sums[0:8, :] += done[0][0] + done[1][0] + done[2][0] + done[3][0]
        sums[8:16, :] += done[0][1] + done[1][1] + done[2][1] + done[3][1]

    def unmix(i):
        rows = at(i, 256)
        part = nt(gproj[rows, 0:AH], wo[0]) + nt(gproj[rows, AH:D], wo[1])
        gctx[rows, :] = part.astype(BF)

    loop(6, norm_one_back)
    loop(2, unmix)
    stores.append(start_copy(gone, gone_any, sems.at[5]))
    for c in range(2):
        gout[c] = tn(ctx[...], gproj[:, AH * c : AH * c + AH]).astype(BF)
        for n in range(4):
            for r in range(4):
                source = gout.at[c, pl.ds(192 * n + 48 * r, 48), :]
                ship(keep, send, place, 4 * c + r, n, pl.ds(192, 48), source, sems.at[2])
    unmix(2)
    for k in range(4):
        gvec[k : k + 1, :] = jnp.sum(sums[8 * k : 8 * k + 8, :], axis=0, keepdims=True)
    gvec[4:8, :] = jnp.zeros((4, D), F32)
    stores.append(start_copy(gctx, gctx_any, sems.at[6]))
    for copy in stores:
        copy.wait()
    pltpu.make_async_copy(gouter, gouter, sems.at[0]).wait()
    pltpu.make_async_copy(ginner, ginner, sems.at[1]).wait()
    pltpu.make_async_copy(gout, gout, sems.at[2]).wait()


def mixer_backward(
    place, vec, gvec, xm_any, packed_any, plong_any, pshort_any, dw_any, kc_any, cq_any, kp_any,
    cv_any, gctx_any, p0, p1, p2, p3, p4, p5, p6, p7,
    keep, send, grads_any, gdep_any,
    wm, xm, packed, plong, pshort, dw, kc, cq, kp, cv, gctx,
    xpad, gcp, gdp, grads, gqc, dkv, gkc, glog, gprob, gdep, gb, spread, gather, wk, sem, sems,
    out_sem,
):
    arrays = (
        (gctx_any, gctx), (kp_any, kp), (cv_any, cv), (packed_any, packed), (kc_any, kc),
        (xm_any, xm), (plong_any, plong), (pshort_any, pshort), (dw_any, dw), (cq_any, cq),
    )
    def begin(first, last):
        return [start_copy(*arrays[k], sems.at[k]) for k in range(first, last)]

    loads = begin(0, 3)
    zero_gaps(xpad)
    zero_gaps(gcp)
    zero_gaps(gdp)
    spread[...] = head_spread()
    gather[...] = head_gather()
    gdep[...] = jnp.zeros((8 * TAPS, D), F32)
    for copy in loads:
        copy.wait()
    loads = begin(3, 6)
    fetch_mixer(place, (p0, p1, p2, p3, p4, p5, p6, p7), wm, sem)
    late = begin(6, 10)
    for start, rows, pstart in SEGS:
        gcp[pstart : pstart + rows, :] = gctx[start : start + rows, AH:D].astype(F32)

    def dynamic(i):
        rows = at(i, 128)
        ps = padded_start(i)
        wide = pl.ds(pl.multiple_of(ps - 8, 8), 144)
        weights = nn(spread_taps(kp[wide, :]), spread[...])
        columns = []
        for c in range(3):
            lanes = slice(128 * c, 128 * c + 128)
            grad_wide = gcp[wide, lanes]
            values = cv[wide, lanes]
            grad = gcp[pl.ds(ps, 128), lanes]
            total = jnp.zeros((128, 128), F32)
            parts = []
            for j in range(TAPS):
                part = weights[144 * j : 144 * j + 144, lanes] * grad_wide
                total = total + part[12 - j : 140 - j, :]
                parts.append((grad * values[4 + j : 132 + j, :]).astype(BF))
            grads[rows, 3 * AH + 128 * c : 3 * AH + 128 * c + 128] = total.astype(BF)
            columns.append(jnp.concatenate(parts, axis=0))
        sums = nn(jnp.concatenate(columns, axis=1), gather[...])
        total = sums[0:128, :]
        for j in range(1, TAPS):
            total = total + pltpu.roll(sums[128 * j : 128 * j + 128, :], 8 * j, 1)
        gprob[rows, :] = total

    loop(6, dynamic)
    for copy in loads:
        copy.wait()
    pltpu.make_async_copy(wm, wm, sem).wait()
    wk[...] = tap_kernel(wm)

    def tap_softmax_back(i):
        rows = at(i, 384)
        probs = jnp.concatenate([kp[pl.ds(padded_start(3 * i + k), 128), :] for k in range(3)], axis=0)
        upper = gprob[rows, :]
        inner = probs * upper
        for shift in (64, 32, 16, 8):
            inner = inner + pltpu.roll(inner, shift, 1)
        glogits = (probs * (upper - inner)).astype(BF)
        glog[rows, :] = glogits
        gquery = nt(glogits, wk[...])
        gkc[rows, :] = (gquery * packed[rows, 0:AH].astype(F32)).astype(BF)
        gqc[rows, :] = gquery * kc[rows, :]

    loop(2, tap_softmax_back)
    for start, rows, pstart in SEGS:
        xpad[pstart : pstart + rows, :] = xm[start : start + rows, :].astype(F32)

    def point_back(c):
        part = nt(gkc[:, 0:256], wm[6, at(c, 256), :])
        part = part + nt(gkc[:, 256:384], wm[7, at(c, 256), 0:128])
        part = part.astype(BF).astype(F32)
        for start, rows, pstart in SEGS:
            gdp[pstart : pstart + rows, at(c, 256)] = part[start : start + rows, :]

    loop(3, point_back)
    copy_depth = start_copy(gdp, gdep_any, out_sem.at[1])

    def release(b):
        for n in range(4):
            where = b ^ place[0]
            chip, far_off = where >> 1, n ^ place[1]
            source = gb.at[b, pl.ds(192 * n, 192), :]

            @pl.when((where & 1) == 0)
            def _():
                pltpu.make_async_copy(source, keep.at[chip, far_off], out_sem.at[0]).start()

            @pl.when((where & 1) == 1)
            def _():
                pltpu.make_async_copy(source, send.at[chip, far_off], out_sem.at[0]).start()

    def depth(i):
        ps = padded_start(i)
        wide = pl.ds(pl.multiple_of(ps - 8, 8), 144)
        for c in range(6):
            lanes = slice(128 * c, 128 * c + 128)
            tokens = xpad[pl.ds(ps, 128), lanes]
            grad_wide = gdp[wide, lanes]
            for j in range(TAPS):
                gdep[8 * j : 8 * j + 8, lanes] += fold(tokens * grad_wide[12 - j : 140 - j, :])

    loop(6, depth)
    for copy in late:
        copy.wait()
    gb[6] = tn(dw[...], gkc[:, 0:256]).astype(BF)
    gb[7, :, 0:128] = tn(dw[...], gkc[:, 256:384]).astype(BF)
    taps = [jnp.sum(gdep[8 * j : 8 * j + 8, :], axis=0, keepdims=True) for j in range(TAPS)]
    table = jnp.concatenate(
        taps + [jnp.zeros((7, D), F32), gvec[...], jnp.zeros((104, D), F32)], axis=0
    ).astype(BF)
    misc = tn(table, eye(128, BF))
    gkernel = nt(tn(cq[...], glog[...]).astype(BF), tap_permutation())
    for n in range(4):
        row = 192 * n
        part = misc[row : row + 96, :] + gkernel[96 * n : 96 * n + 96, :]
        gb[7, row : row + 96, 128:256] = part.astype(BF)
        gb[7, row + 96 : row + 192, 128:256] = misc[row + 96 : row + 192, :].astype(BF)
    release(6)
    release(7)

    def attend(row0, nq, key0, nk, pair, load, first):
        queries = packed[pl.ds(row0, nq), at(pair, 128)].astype(F32) * 0.125
        keys = packed[pl.ds(key0, nk), at(3 + pair, 128)]
        vals = packed[pl.ds(key0, nk), at(6 + pair, 128)]
        up = gctx[pl.ds(row0, nq), at(pair, 128)].astype(F32)
        lane = iota((nq, 128), 1)
        outs = []
        gkeys = jnp.zeros((nk, 128), F32)
        gvals = jnp.zeros((nk, 128), F32)
        for hh in range(2):
            mine = (lane >> 6) == hh
            query = jnp.where(mine, queries, 0.0).astype(BF)
            upper = jnp.where(mine, up, 0.0).astype(BF)
            probs_low = load(hh)
            gprobs = nt(upper, vals)
            parts = []
            for r in range(0, nq, 32):
                probs, part = probs_low[r : r + 32, :].astype(F32), gprobs[r : r + 32, :]
                inner = jnp.sum(probs * part, axis=1, keepdims=True)
                parts.append((probs * (part - inner)).astype(BF))
            gscores = jnp.concatenate(parts, axis=0)
            outs.append(nn(gscores, keys))
            gkeys = gkeys + tn(gscores, query)
            gvals = gvals + tn(probs_low, upper)
        both = jnp.where(lane < 64, outs[0], outs[1]) * 0.125
        both = both + gqc[pl.ds(row0, nq), at(pair, 128)]
        grads[pl.ds(row0, nq), at(pair, 128)] = both.astype(BF)
        span = pl.ds(key0, nk)
        if nq == nk:
            grads[span, at(3 + pair, 128)] = gkeys.astype(BF)
            grads[span, at(6 + pair, 128)] = gvals.astype(BF)
        elif first:
            dkv[0] = gkeys
            dkv[1] = gvals
        else:
            grads[span, at(3 + pair, 128)] = (dkv[0] + gkeys).astype(BF)
            grads[span, at(6 + pair, 128)] = (dkv[1] + gvals).astype(BF)

    def long_attend(pair):
        for block in range(2):
            attend(
                256 * block, 256, 0, LONG, pair,
                lambda hh: plong[2 * pair + hh, 256 * block : 256 * block + 256, :],
                block == 0,
            )

    loop(3, long_attend)
    for seg in range(2):
        for pair in range(3):
            row0 = LONG + 128 * seg
            attend(row0, 128, row0, SHORT, pair, lambda hh: pshort[seg, 2 * pair + hh, :, :], True)
    copy_grads = start_copy(grads, grads_any, out_sem.at[2])

    def weights(b):
        gb[b] = tn(xm[...], grads[:, at(b, 256)]).astype(BF)
        release(b)

    loop(6, weights)
    copy_depth.wait()
    copy_grads.wait()
    pltpu.make_async_copy(gb, gb, out_sem.at[0]).wait()


def input_gradient(
    place, llen, slen, vec, grads_any, gdp_any, gone_any, p0, p1, p2, p3, p4, p5, p6, p7,
    il, is_, wm, grads, gdp, rest, sem, sems
):
    arrays = ((gone_any, rest), (gdp_any, gdp), (grads_any, grads))
    loads = [start_copy(a, b, sems.at[k]) for k, (a, b) in enumerate(arrays)]
    fetch_mixer(place, (p0, p1, p2, p3, p4, p5, p6, p7), wm, sem)
    for copy in loads:
        copy.wait()

    def depth(i):
        ps = padded_start(i)
        for c in range(6):
            lanes = slice(128 * c, 128 * c + 128)
            window = gdp[pl.ds(pl.multiple_of(ps - 8, 8), 144), lanes]
            total = rest[at(i, 128), lanes]
            for j in range(TAPS):
                total = total + vec[j : j + 1, lanes] * window[12 - j : 140 - j, :]
            rest[at(i, 128), lanes] = total

    loop(6, depth)
    pltpu.make_async_copy(wm, wm, sem).wait()

    def inputs(i):
        rows = at(i, 256)
        total = rest[rows, :]
        for b in range(6):
            total = total + nt(grads[rows, 256 * b : 256 * b + 256], wm[b])
        return total

    def inputs_long(i):
        live = i * 256 + iota((256, D), 0) < llen[0]
        il[at(i, 256), :] = jnp.where(live, inputs(i), 0.0).astype(BF)

    loop(2, inputs_long)
    total = inputs(2)
    row = iota((128, D), 0)
    for seg in range(2):
        part = total[128 * seg : 128 * seg + 128, :]
        is_[128 * seg : 128 * seg + 128, :] = jnp.where(row < slen[seg], part, 0.0).astype(BF)


def pack(
    place, qkv, depth, point, kernel, convout, g1, b1, inner, outer, out, g2, b2, mixer, ffn
):
    for w in range(SLOTS):

        @pl.when(place[0] == w)
        def _():
            g, r = w // 4, w % 4
            ffn[0:96, :] = inner[g, :, AH * r : AH * r + AH]
            ffn[96:192, :] = outer[g, 96 * r : 96 * r + 96, :]
            ffn[192:240, :] = out[48 * r : 48 * r + 48, AH * g : AH * g + AH]
            if w < 4:
                mixer[...] = qkv[:, 256 * w : 256 * w + 256]
            elif w == 4:
                mixer[:, 0:128] = qkv[:, 1024:1152]
                mixer[:, 128:256] = convout[:, 0:128]
            elif w == 5:
                mixer[...] = convout[:, 128:384]
            elif w == 6:
                mixer[...] = point[:, 0:256]
            else:
                mixer[:, 0:128] = point[:, 256:384]
                rows = [v[...].astype(F32).reshape(1, 192) for v in (g1, b1, g2, b2)]
                table = jnp.concatenate(
                    [depth[...].astype(F32), jnp.zeros((7, 192), F32)]
                    + rows
                    + [jnp.zeros((108, 192), F32)],
                    axis=0,
                )
                left = tn(table.astype(BF), eye(128, BF))
                row, col = iota((54, 128), 0), iota((54, 128), 1)
                right = tn(kernel[...], jnp.where(col == row + 64, 1.0, 0.0).astype(BF))
                mixer[0:96, 128:256] = (left[0:96, :] + right).astype(BF)
                mixer[96:192, 128:256] = left[96:192, :].astype(BF)


def unpack_ffn(place, p0, p1, p2, p3, p4, p5, p6, p7, inner, outer, out):
    for core, pieces in enumerate(((p0, p1, p2, p3), (p4, p5, p6, p7))):
        for chip, piece in enumerate(pieces):
            slot = slot_of(place[0], core, chip)
            g, r = slot >> 2, slot & 3
            inner[g, :, at(r, AH)] = piece[0:96, :].astype(F32)
            outer[g, at(r, 96), :] = piece[96:192, :].astype(F32)
            out[at(r, 48), at(g, AH)] = piece[192:240, :].astype(F32)


def unpack_mixer(
    place, p0, p1, p2, p3, p4, p5, p6, p7,
    qkv, depth, point, kernel, convout, g1, b1, g2, b2, packed,
):
    for core, pieces in enumerate(((p0, p1, p2, p3), (p4, p5, p6, p7))):
        for chip, piece in enumerate(pieces):
            packed[slot_of(place[0], core, chip)] = piece[...]
    for w in range(4):
        qkv[:, 256 * w : 256 * w + 256] = packed[w].astype(F32)
    qkv[:, 1024:1152] = packed[4, :, 0:128].astype(F32)
    convout[:, 0:128] = packed[4, :, 128:256].astype(F32)
    convout[:, 128:384] = packed[5].astype(F32)
    point[:, 0:256] = packed[6].astype(F32)
    point[:, 256:384] = packed[7, :, 0:128].astype(F32)
    misc = packed[7, :, 128:256]
    table = nt(eye(128, BF), misc)
    depth[...] = table[0:TAPS, :]
    for k, ref in enumerate((g1, b1, g2, b2)):
        ref[...] = table[16 + k : 17 + k, :].reshape(192)
    kernel[...] = table[64:118, 0:96]


SMEM = pl.BlockSpec(memory_space=pltpu.SMEM)
VMEM = pl.BlockSpec(memory_space=pltpu.VMEM)
ANY = pl.BlockSpec(memory_space=pl.ANY)


VMEM_MIB = {'unpack_ffn': 12, 'unpack_mixer': 12, 'input_gradient': 24}


def call(kernel, specs, outs, scratch, flops, *args, out_specs=None):
    return pl.pallas_call(
        kernel,
        out_shape=[jax.ShapeDtypeStruct(s, d) for s, d in outs],
        in_specs=specs,
        out_specs=out_specs or [VMEM] * len(outs),
        scratch_shapes=[pltpu.VMEM(s, d) for s, d in scratch[0]] + list(scratch[1:]),
        compiler_params=pltpu.CompilerParams(vmem_limit_bytes=VMEM_MIB.get(kernel.__name__, 60) << 20),
        cost_estimate=pl.CostEstimate(flops=flops, bytes_accessed=1 << 20, transcendentals=0),
        name=kernel.__name__,
    )(*args)


def forward_mixer(scalars, xl, xs, pieces):
    outs = [
        ((ROWS, D), BF), ((ROWS, 3 * AH), BF),
        ((HEADS, LONG, LONG), BF), ((2, HEADS, SHORT, SHORT), BF),
        ((ROWS, D), BF), ((ROWS, AH), F32), ((ROWS, AH), BF), ((PAD, 128), F32),
        ((PAD, AH), F32), ((ROWS, D), BF), ((24, D), F32),
    ]
    scratch = [((SLOTS, D, 256), BF), ((PAD, D), F32), ((256, AH), BF), ((AH, 128), BF)]
    return call(
        mixer_forward, [SMEM] * 3 + [VMEM] * 2 + [ANY] * 8, outs,
        (scratch + outs[:-1], pltpu.SemaphoreType.DMA, pltpu.SemaphoreType.DMA((10,))), 30 * 10**9,
        *scalars, xl, xs, *pieces, out_specs=[ANY] * 10 + [VMEM],
    )


def feed_forward(scalars, xm, ctx, vec, cl, cs, pieces):
    outs = [
        ((LONG, D), BF), ((2 * SHORT, D), BF), ((4, 4, 240, AH), BF), ((4, 4, 240, AH), BF),
        ((ROWS, D), F32), ((ROWS, D), BF), ((8, D), F32),
    ]
    scratch = [
        ((2, D, AH), BF), ((4, AH, D), BF), ((4, D, AH), BF), ((ROWS, D), BF), ((ROWS, D), BF),
        ((ROWS, D), BF), ((ROWS, D), BF), ((ROWS, D), F32), ((ROWS, D), F32),
        ((2, ROWS, AH), BF), ((2, ROWS, AH), BF), ((4, ROWS, D), BF), ((4, ROWS, D), F32),
        ((2, ROWS, AH), F32), ((ROWS, 128), F32), ((256, D), F32), ((256, D), F32),
        ((ROWS, D), BF), ((ROWS, D), BF), ((ROWS, D), BF), ((2, ROWS, AH), BF),
        ((4, AH, D), BF), ((4, D, AH), BF), ((ROWS, D), F32), ((ROWS, D), BF), ((32, D), F32),
    ]
    return call(
        ffn_both, [SMEM] * 3 + [VMEM] + [ANY] * 12, outs,
        (scratch, pltpu.SemaphoreType.DMA((7,))), 60 * 10**9,
        *scalars, vec, xm, ctx, cl, cs, *pieces, out_specs=[ANY] * 6 + [VMEM],
    )


def backward_mixer(place, vec, gvec, arrays, pieces):
    outs = [
        ((4, 4, 192, 256), BF), ((4, 4, 192, 256), BF), ((ROWS, 4 * AH), BF), ((PAD, D), F32),
    ]
    scratch = [((SLOTS, D, 256), BF)] + [(a.shape, a.dtype) for a in arrays] + [
        ((PAD, D), F32), ((PAD, AH), F32), ((PAD, D), F32), ((ROWS, 4 * AH), BF),
        ((ROWS, AH), F32), ((2, LONG, 128), F32), ((ROWS, AH), BF), ((ROWS, 128), BF),
        ((ROWS, 128), F32),
        ((8 * TAPS, D), F32), ((SLOTS, D, 256), BF), ((256, AH), BF), ((AH, 128), BF),
        ((AH, 128), BF),
    ]
    dma = pltpu.SemaphoreType.DMA
    return call(
        mixer_backward, [SMEM] + [VMEM] * 2 + [ANY] * 18, outs,
        (scratch, dma, dma((10,)), dma((3,))), 40 * 10**9,
        place, vec, gvec, *arrays, *pieces, out_specs=[ANY] * 4,
    )


def backward_inputs(scalars, vec, grads, gdp, gone, pieces):
    scratch = [
        ((SLOTS, D, 256), BF), ((ROWS, 4 * AH), BF), ((PAD, D), F32), ((ROWS, D), F32),
    ]
    dma = pltpu.SemaphoreType.DMA
    return call(
        input_gradient, [SMEM] * 3 + [VMEM] + [ANY] * 11, [((LONG, D), BF), ((2 * SHORT, D), BF)],
        (scratch, dma, dma((3,))), 5 * 10**9, *scalars, vec, grads, gdp, gone, *pieces,
    )


def far(values, bit):
    return lax.ppermute(values, "narrow", [(i, i ^ bit) for i in range(4)])


def near(values, bit):
    return lax.ppermute(values, "wide", [(i, i ^ bit) for i in range(SLOTS)])


def gather_narrow(piece):
    return jnp.stack([piece] + [far(piece, k) for k in (1, 2, 3)])


def gather_chips(block):
    return [block] + [near(block, k) for k in (2, 4, 6)]


def gather_cores(blocks):
    return blocks + [near(block, 1) for block in blocks]


def total(first, others):
    result = first.astype(F32)
    for other in others:
        result = result + other.astype(F32)
    return result.astype(BF)


def reduce_cores(keep, sent):
    return [total(keep[k], [sent[k]]) for k in range(4)]


def send_chips(parts):
    return [near(parts[k], 2 * k) for k in (1, 2, 3)]


def reduce_chips(first, others):
    return [total(first[k], [other[k] for other in others]) for k in range(4)]


def send_narrow(parts):
    return [far(parts[k], k) for k in (1, 2, 3)]


def body(
    long_tokens, long_lengths, short_tokens, short_lengths,
    w_qkv, w_depth, w_point, w_kernel, w_convout, w_out, norm1_gain, norm1_bias,
    w_inner, w_outer, norm2_gain, norm2_bias, long_cotangent, short_cotangent,
):
    place = jnp.stack([lax.axis_index("wide"), lax.axis_index("narrow")]).astype(jnp.int32)
    scalars = (place, long_lengths, short_lengths)
    xl, xs = long_tokens.reshape(LONG, D), short_tokens.reshape(2 * SHORT, D)
    cl, cs = long_cotangent.reshape(LONG, D), short_cotangent.reshape(2 * SHORT, D)
    mixer, ffn = call(
        pack, [SMEM] + [VMEM] * 12, [((192, 256), BF), ((240, AH), BF)], ([],), 10**9,
        place, w_qkv, w_depth, w_point, w_kernel.T, w_convout, norm1_gain, norm1_bias,
        w_inner, w_outer, w_out, norm2_gain, norm2_bias,
    )
    mixer = gather_narrow(mixer)
    mixer, ffn = lax.optimization_barrier((mixer, ffn))
    mixer = gather_chips(mixer)
    ffn = gather_narrow(ffn)
    mixer, ffn = lax.optimization_barrier((mixer, ffn))
    mixer = gather_cores(mixer)
    ffn = gather_chips(ffn)
    xm, packed, plong, pshort, dw, kc, cq, kp, cv, ctx, vec = forward_mixer(scalars, xl, xs, mixer)
    ctx, ffn = lax.optimization_barrier((ctx, ffn))
    ffn = gather_cores(ffn)
    ol, os, keep, send, gone, gctx, gvec = feed_forward(scalars, xm, ctx, vec, cl, cs, ffn)
    ga = reduce_cores(keep, near(send, 1))
    ga_sent = send_chips(ga)
    gctx, ga = lax.optimization_barrier((gctx, ga))
    keep, send, grads, gdp = backward_mixer(
        place, vec, gvec, (xm, packed, plong, pshort, dw, kc, cq, kp, cv, gctx), mixer
    )
    keep, send, ga_sent = lax.optimization_barrier((keep, send, ga_sent))
    gb = reduce_cores(keep, near(send, 1))
    gb_sent = send_chips(gb)
    ga_sent, gb = lax.optimization_barrier((ga_sent, gb))
    ga = reduce_chips(ga[0], ga_sent)
    ga_sent = [far(ga[1], 1), far(ga[2], 2)]
    grads, ga = lax.optimization_barrier((grads, ga))
    il, is_ = backward_inputs(scalars, vec, grads, gdp, gone, mixer)
    last, il = lax.optimization_barrier((ga[3], il))
    ga_sent, gb_sent, il = lax.optimization_barrier((ga_sent, gb_sent, il))
    ga_sent.append(far(last, 3))
    ga = gather_chips(lax.psum(total(ga[0], ga_sent), "hi"))
    gb = reduce_chips(gb[0], gb_sent)
    gb = gather_chips(lax.psum(total(gb[0], send_narrow(gb)), "hi"))
    inner, outer, out = call(
        unpack_ffn, [SMEM] + [VMEM] * 8,
        [((2, 96, 4 * AH), F32), ((2, AH, AH), F32), ((192, D), F32)],
        ([],), 10**9, place, *gather_cores(ga),
    )
    gb, inner = lax.optimization_barrier((gb, inner))
    outs = [
        ((192, 3 * AH), F32), ((TAPS, 192), F32), ((192, AH), F32), ((54, 96), F32), ((192, AH), F32),
    ] + [((192,), F32)] * 4
    qkv, depth, point, kernel, convout, g1, b1, g2, b2 = call(
        unpack_mixer, [SMEM] + [VMEM] * 8, outs, ([((SLOTS, 192, 256), BF)],), 10**9,
        place, *gather_cores(gb),
    )
    return (
        ol.reshape(long_tokens.shape), os.reshape(short_tokens.shape),
        il.reshape(long_tokens.shape), is_.reshape(short_tokens.shape),
        qkv, depth, point, kernel.T, convout, out, g1, b1, inner, outer, g2, b2,
    )


def solution(mesh):
    wide, narrow = mesh.shape["wide"], mesh.shape["narrow"]
    inner_mesh = Mesh(mesh.devices.reshape(wide // SLOTS, SLOTS, narrow), ("hi", "wide", "narrow"))
    every = ("hi", "wide", "narrow")
    rows = P(every, None, None)
    weights = (
        P("narrow", None), P(None, "narrow"), P("narrow", None), P("narrow", None),
        P("narrow", None), P("narrow", None), P("narrow"), P("narrow"),
        P(None, "narrow", None), P(None, "narrow", None), P("narrow"), P("narrow"),
    )
    return jax.shard_map(
        body,
        mesh=inner_mesh,
        in_specs=(rows, P(every), rows, P(every)) + weights + (rows, rows),
        out_specs=(rows, rows, rows, rows) + weights,
        check_vma=False,
    )
```

```python
import jax
import jax.numpy as jnp
from jax import lax
from jax.experimental import pallas as pl
from jax.experimental.pallas import tpu as pltpu
from jax.sharding import Mesh
from jax.sharding import PartitionSpec as P

BF = jnp.bfloat16
F32 = jnp.float32
EPS = 1e-12
D = 768
AH = 384
HEADS = 6
TAPS = 9
LONG = 512
SHORT = 128
ROWS = 768
PAD = 800
SLOTS = 8
NEG = -1000000000.0
PSTART = tuple(8 + 128 * i + 8 * max(i - 3, 0) for i in range(6))
SEGS = ((0, 512, 8), (512, 128, 528), (640, 128, 664))


def nn(a, b):
    return lax.dot_general(a, b, (((1,), (0,)), ((), ())), preferred_element_type=F32)


def nt(a, b):
    return lax.dot_general(a, b, (((1,), (1,)), ((), ())), preferred_element_type=F32)


def tn(a, b):
    return lax.dot_general(a, b, (((0,), (0,)), ((), ())), preferred_element_type=F32)


def iota(shape, axis):
    return lax.broadcasted_iota(jnp.int32, shape, axis)


def loop(count, body):
    def step(i, carry):
        body(i)
        return carry

    lax.fori_loop(0, count, step, 0)


def at(i, size):
    if isinstance(i, int):
        return pl.ds(i * size, size)
    return pl.ds(pl.multiple_of(i * size, size), size)


def padded_start(i):
    return pl.multiple_of(8 + 128 * i + 8 * jnp.maximum(i - 3, 0), 8)


def zero_gaps(ref):
    for start in (0, 520, 656, 792):
        ref[start : start + 8, :] = jnp.zeros((8, ref.shape[1]), ref.dtype)


def eye(n, dtype):
    return jnp.where(iota((n, n), 0) == iota((n, n), 1), 1.0, 0.0).astype(dtype)


def tap_permutation():
    row, col = iota((128, 128), 0), iota((128, 128), 1)
    head, tap = col & 7, col >> 3
    keep = (head < HEADS) & (tap < TAPS) & (row == 64 + head * TAPS + tap)
    return jnp.where(keep, 1.0, 0.0).astype(BF)


def head_spread():
    row, col = iota((256, AH), 0), iota((256, AH), 1)
    return jnp.where((row & 127) == (col >> 6), 1.0, 0.0).astype(BF)


def head_gather():
    row, col = iota((AH, 128), 0), iota((AH, 128), 1)
    return jnp.where((row >> 6) == col, 1.0, 0.0).astype(BF)


def split_two(values):
    high = values.astype(BF)
    low = (values - high.astype(F32)).astype(BF)
    return jnp.concatenate([high, low], axis=1)


def spread_taps(probs):
    moved = [probs] + [pltpu.roll(probs, 128 - 8 * j, 1) for j in range(1, TAPS)]
    return split_two(jnp.concatenate(moved, axis=0))


def tap_kernel(wm):
    stored = jnp.concatenate([wm[7, 192 * n : 192 * n + 96, 128:256] for n in range(4)], axis=0)
    return nn(stored, tap_permutation()).astype(BF)


def slot_of(where, core, chip):
    return 2 * ((where >> 1) ^ chip) + ((where & 1) ^ core)


def fetch_mixer(place, pieces, wm, sem):
    for at_core in range(2):
        for chip in range(4):
            piece = pieces[4 * at_core + chip]
            slot = slot_of(place[0], at_core, chip)

            def fetch(k):
                pltpu.make_async_copy(piece.at[k], wm.at[slot, at(place[1] ^ k, 192), :], sem).start()

            loop(4, fetch)


def mixer_forward(
    place, llen, slen, xl, xs, p0, p1, p2, p3, p4, p5, p6, p7,
    xm_any, packed_any, plong_any, pshort_any, dw_any, kc_any, cq_any, kp_any, cv_any, ctx_any, vec,
    wm, xpad, spread, wk, xm, packed, plong, pshort, dw, kc, cq, kp, cv, ctx, sem, sems
):
    fetch_mixer(place, (p0, p1, p2, p3, p4, p5, p6, p7), wm, sem)
    lens = (llen[0], slen[0], slen[1])
    zero_gaps(xpad)
    zero_gaps(cv)
    zero_gaps(kp)
    for i in range(6):
        seg = max(i - 3, 0)
        base = 128 * i if i < 4 else 0
        tokens = xl[128 * i : 128 * i + 128, :] if i < 4 else xs[128 * (i - 4) : 128 * (i - 3), :]
        live = base + iota((128, D), 0) < lens[seg]
        values = jnp.where(live, tokens.astype(F32), 0.0)
        xpad[PSTART[i] : PSTART[i] + 128, :] = values
        xm[128 * i : 128 * i + 128, :] = values.astype(BF)
    stores = [start_copy(xm, xm_any, sems.at[0])]
    spread[...] = head_spread()
    pltpu.make_async_copy(wm, wm, sem).wait()
    vec[...] = nt(eye(128, BF), wm[7, :, 128:256])[0:24, :]
    wk[...] = tap_kernel(wm)

    def depth(i):
        ps = padded_start(i)
        for c in range(6):
            lanes = slice(128 * c, 128 * c + 128)
            window = xpad[pl.ds(pl.multiple_of(ps - 8, 8), 144), lanes]
            total = jnp.zeros((128, 128), F32)
            for j in range(TAPS):
                total = total + vec[j : j + 1, lanes] * window[4 + j : 132 + j, :]
            dw[at(i, 128), lanes] = total.astype(BF)

    def project(b):
        packed[:, at(b, 256)] = nn(xm[...], wm[b]).astype(BF)
        depth(b)

    loop(4, project)
    depth(jnp.int32(4))
    part = nn(xm[...], wm[4])
    packed[:, 1024:1152] = part[:, 0:128].astype(BF)
    for start, rows, pstart in SEGS:
        cv[pstart : pstart + rows, 0:128] = part[start : start + rows, 128:256]
    depth(jnp.int32(5))
    part = nn(xm[...], wm[5])
    for start, rows, pstart in SEGS:
        cv[pstart : pstart + rows, 128:384] = part[start : start + rows, :]
    stores += [
        start_copy(packed, packed_any, sems.at[1]), start_copy(dw, dw_any, sems.at[2]),
        start_copy(cv, cv_any, sems.at[3]),
    ]
    kc[:, 0:256] = nn(dw[...], wm[6])
    kc[:, 256:384] = nn(dw[...], wm[7, :, 0:128])
    stores.append(start_copy(kc, kc_any, sems.at[4]))

    def tap_softmax(i):
        rows = at(i, 384)
        query = (kc[rows, :] * packed[rows, 0:AH].astype(F32)).astype(BF)
        cq[rows, :] = query
        logits = nn(query, wk[...])
        real = iota((384, 128), 1) < 8 * TAPS
        top = jnp.where(real, logits, NEG * 1e20)
        for shift in (64, 32, 16, 8):
            top = jnp.maximum(top, pltpu.roll(top, shift, 1))
        ex = jnp.where(real, jnp.exp(logits - top), 0.0)
        total = ex
        for shift in (64, 32, 16, 8):
            total = total + pltpu.roll(total, shift, 1)
        probs = ex * (1.0 / total)
        for k in range(3):
            kp[pl.ds(padded_start(3 * i + k), 128), :] = probs[128 * k : 128 * k + 128, :]

    loop(2, tap_softmax)

    def dynamic(u):
        for i in (2 * u, 2 * u + 1):
            ps = padded_start(i)
            weights = nn(spread_taps(kp[pl.ds(ps, 128), :]), spread[...])
            for c in range(3):
                lanes = slice(128 * c, 128 * c + 128)
                window = cv[pl.ds(pl.multiple_of(ps - 8, 8), 144), lanes]
                out = jnp.zeros((128, 128), F32)
                for j in range(TAPS):
                    out = out + weights[128 * j : 128 * j + 128, lanes] * window[4 + j : 132 + j, :]
                ctx[at(i, 128), AH + 128 * c : AH + 128 * c + 128] = out.astype(BF)

    loop(3, dynamic)
    stores += [start_copy(cq, cq_any, sems.at[5]), start_copy(kp, kp_any, sems.at[6])]

    def attend(row0, nq, key0, nk, limit, pair, store):
        queries = packed[pl.ds(row0, nq), at(pair, 128)].astype(F32) * 0.125
        keys = packed[pl.ds(key0, nk), at(3 + pair, 128)].astype(F32)
        vals = packed[pl.ds(key0, nk), at(6 + pair, 128)]
        lane, key_lane = iota((nq, 128), 1), iota((nk, 128), 1)
        bias = jnp.where(iota((nk, 128), 0) < limit, 0.0, NEG)
        outs = []
        for hh in range(2):
            spare = 64 * (1 - hh)
            query = jnp.where((lane >> 6) == hh, queries, jnp.where(lane == spare, 1.0, 0.0))
            scores = nt(query.astype(BF), jnp.where(key_lane == spare, bias, keys).astype(BF))
            parts = []
            for r in range(0, nq, 32):
                part = scores[r : r + 32, :]
                part = jnp.exp(part - jnp.max(part, axis=1, keepdims=True))
                part = part * (1.0 / jnp.sum(part, axis=1, keepdims=True))
                parts.append(part.astype(BF))
            probs = jnp.concatenate(parts, axis=0)
            store(hh, probs)
            outs.append(nn(probs, vals))
        both = jnp.where(lane < 64, outs[0], outs[1])
        ctx[pl.ds(row0, nq), at(pair, 128)] = both.astype(BF)

    def long_attend(i):
        pair, block = i >> 1, i & 1
        row0 = pl.multiple_of(block * 256, 256)

        def store(hh, probs):
            plong[2 * pair + hh, pl.ds(row0, 256), :] = probs

        attend(row0, 256, 0, LONG, lens[0], pair, store)

    loop(6, long_attend)
    stores.append(start_copy(plong, plong_any, sems.at[7]))
    for seg in range(2):
        for pair in range(3):

            def store(hh, probs):
                pshort[seg, 2 * pair + hh, :, :] = probs

            row0 = LONG + 128 * seg
            attend(row0, 128, row0, SHORT, lens[1 + seg], pair, store)
    stores += [start_copy(pshort, pshort_any, sems.at[8]), start_copy(ctx, ctx_any, sems.at[9])]
    for copy in stores:
        copy.wait()


def gelu_parts(hidden):
    cdf = 0.5 + 0.5 * lax.erf(hidden * 0.7071067811865476)
    return cdf, jnp.exp(hidden * hidden * -0.5) * 0.3989422804014327


def fold(values):
    return jnp.sum(values.reshape(values.shape[0] // 8, 8, values.shape[1]), axis=0)


def start_copy(source, target, sem):
    copy = pltpu.make_async_copy(source, target, sem)
    copy.start()
    return copy


def ship(keep, send, place, slot, shard, rows, source, sem):
    where = slot ^ place[0]
    chip, far_off = where >> 1, shard ^ place[1]

    @pl.when((where & 1) == 0)
    def _():
        pltpu.make_async_copy(source, keep.at[chip, far_off, rows, :], sem).start()

    @pl.when((where & 1) == 1)
    def _():
        pltpu.make_async_copy(source, send.at[chip, far_off, rows, :], sem).start()


def ffn_both(
    place, llen, slen, vec, xm_any, ctx_any, cl, cs, p0, p1, p2, p3, p4, p5, p6, p7,
    ol, os, keep, send, gone_any, gctx_any, gvec,
    wo, wi, wu, xm, ctx, cot, out, res, xhat, grouped, gffn, active, slope, ffn, rstd,
    hid_a, hid_b, ghid_a, ghid_b, gproj, gout, ginner, gouter, gone, gctx, sums, sems,
):
    loads = [start_copy(ctx_any, ctx, sems.at[3]), start_copy(xm_any, xm, sems.at[4])]

    def fetch(part):
        for core, pieces in enumerate(((p0, p1, p2, p3), (p4, p5, p6, p7))):
            for chip, piece in enumerate(pieces):
                slot = slot_of(place[0], core, chip)
                g, r = slot >> 2, slot & 3

                def one(k):
                    n = place[1] ^ k
                    if part == 0:
                        rows = pl.ds(pl.multiple_of(192 * n + 48 * r, 48), 48)
                        source, target = pl.ds(192, 48), wo.at[g, rows, :]
                    elif part == 1:
                        source, target = pl.ds(0, 96), wi.at[slot >> 1, at(n, 96), at(slot & 1, AH)]
                    else:
                        rows = at(4 * (n & 1) + r, 96)
                        source, target = pl.ds(96, 96), wu.at[2 * g + (n >> 1), rows, :]
                    pltpu.make_async_copy(piece.at[k, source, :], target, sems.at[part]).start()

                loop(4, one)

    fetch(0)
    gain_one, bias_one = vec[16:17, :], vec[17:18, :]
    gain_two, bias_two = vec[18:19, :], vec[19:20, :]
    sums[...] = jnp.zeros((32, D), F32)
    ffn[...] = jnp.zeros((2, ROWS, AH), F32)
    for copy in loads:
        copy.wait()
    pltpu.make_async_copy(wo, wo, sems.at[0]).wait()
    fetch(1)
    fetch(2)
    cots = [
        start_copy(cl, cot.at[0:LONG], sems.at[5]), start_copy(cs, cot.at[LONG:ROWS], sems.at[6])
    ]

    def mix(i):
        rows = at(i, 256)
        for c in range(2):
            lanes = slice(AH * c, AH * c + AH)
            res[rows, lanes] = nn(ctx[rows, :], wo[c]) + xm[rows, lanes].astype(F32)

    def several(i):
        return [at(4 * i + k, 32) for k in range(4)]

    def norm_one(i):
        spots = several(i)
        done = []
        for values in [res[rows, :] for rows in spots]:
            center = values - jnp.mean(values, axis=1, keepdims=True)
            scale = lax.rsqrt(jnp.mean(center * center, axis=1, keepdims=True) + EPS)
            hat = center * scale
            done.append((hat, scale, hat * gain_one + bias_one))
        for rows, (hat, scale, first) in zip(spots, done):
            xhat[rows, :] = hat
            rstd[rows, :] = jnp.broadcast_to(scale, (32, 128))
            res[rows, :] = first
            short = first.astype(BF)
            grouped[0, rows, :] = short[:, 0:AH]
            grouped[1, rows, :] = short[:, AH:D]

    mix(0)
    for tile in range(3):
        if tile < 2:
            mix(tile + 1)
        norm_one(2 * tile)
        norm_one(2 * tile + 1)
    pltpu.make_async_copy(wi, wi, sems.at[1]).wait()
    pltpu.make_async_copy(wu, wu, sems.at[2]).wait()

    def hidden(t, target):
        b = lax.div(t, 3)
        target[...] = nn(grouped[b >> 1, at(t - 3 * b, 256), :], wi[b])

    def outward(t):
        b = lax.div(t, 3)
        rows = at(t - 3 * b, 256)
        ffn[b >> 1, rows, :] += nn(active[b, rows, :], wu[b])

    def act(t, source):
        b = lax.div(t, 3)
        m = t - 3 * b
        for part in range(16):
            values = source[16 * part : 16 * part + 16, :]
            rows = pl.ds(pl.multiple_of(m * 256 + 16 * part, 16), 16)
            cdf, density = gelu_parts(values)
            active[b, rows, :] = (values * cdf).astype(BF)
            slope[b, rows, :] = cdf + values * density

    def pair(u, first=False):
        t = 2 * u
        if not first:
            outward(t - 1)
        hidden(t + 1, hid_b)
        act(t, hid_a)
        outward(t)
        hidden(jnp.minimum(t + 2, 11), hid_a)
        act(t + 1, hid_b)

    hidden(jnp.int32(0), hid_a)
    pair(jnp.int32(0), True)
    loop(5, lambda u: pair(u + 1))
    outward(jnp.int32(11))
    for copy in cots:
        copy.wait()

    def norm_two(i):
        limit = jnp.where(i < 4, llen[0], slen[jnp.clip(i - 4, 0, 1)])
        base = jnp.where(i < 4, 128 * i, 0)
        spots = several(i)
        loaded = [
            (
                jnp.concatenate([ffn[0, rows, :], ffn[1, rows, :]], axis=1) + res[rows, :],
                cot[rows, :].astype(F32),
            )
            for rows in spots
        ]
        done = []
        for k, (values, up) in enumerate(loaded):
            center = values - jnp.mean(values, axis=1, keepdims=True)
            scale = lax.rsqrt(jnp.mean(center * center, axis=1, keepdims=True) + EPS)
            hat = center * scale
            result = (hat * gain_two + bias_two).astype(BF)
            live = base + 32 * k + iota((32, D), 0) < limit
            up = jnp.where(live, up, 0.0)
            gain_part, bias_part = fold(up * hat), fold(up)
            up = up * gain_two
            grad = scale * (
                up
                - jnp.mean(up, axis=1, keepdims=True)
                - hat * jnp.mean(up * hat, axis=1, keepdims=True)
            )
            done.append((result, gain_part, bias_part, grad))
        for rows, (result, _, _, grad) in zip(spots, done):
            out[rows, :] = result
            res[rows, :] = grad
            short = grad.astype(BF)
            gffn[0, rows, :] = short[:, 0:AH]
            gffn[1, rows, :] = short[:, AH:D]
        sums[16:24, :] += done[0][1] + done[1][1] + done[2][1] + done[3][1]
        sums[24:32, :] += done[0][2] + done[1][2] + done[2][2] + done[3][2]

    loop(6, norm_two)
    stores = [
        start_copy(out.at[0:LONG], ol, sems.at[3]), start_copy(out.at[LONG:ROWS], os, sems.at[4])
    ]
    ffn[...] = jnp.zeros((2, ROWS, AH), F32)

    def slopes(b, target):
        for part in range(6):
            rows = slice(128 * part, 128 * part + 128)
            back = nt(gffn[b >> 1, rows, :], wu[b])
            target[rows, :] = (back * slope[b, rows, :]).astype(BF)

    def gradients(b, source):
        g = b >> 1
        gouter[b] = tn(active[b], gffn[g]).astype(BF)
        ginner[b] = tn(grouped[g], source[...]).astype(BF)
        ffn[g] += nt(source[...], wi[b])
        for half in range(2):
            n = 2 * (b & 1) + half
            for w in range(4):
                outer = gouter.at[b, pl.ds(AH * half + 96 * w, 96), :]
                ship(keep, send, place, 4 * g + w, n, pl.ds(96, 96), outer, sems.at[0])
                inner = ginner.at[b, pl.ds(96 * w, 96), pl.ds(AH * half, AH)]
                ship(keep, send, place, 2 * b + half, w, pl.ds(0, 96), inner, sems.at[1])

    slopes(jnp.int32(0), ghid_a)

    def contract(u):
        b = 2 * u
        slopes(b + 1, ghid_b)
        gradients(b, ghid_a)
        slopes(jnp.minimum(b + 2, 3), ghid_a)
        gradients(b + 1, ghid_b)

    loop(2, contract)

    def norm_one_back(i):
        spots = several(i)
        loaded = [
            (
                res[rows, :] + jnp.concatenate([ffn[0, rows, :], ffn[1, rows, :]], axis=1),
                xhat[rows, :], rstd[rows, 0:1],
            )
            for rows in spots
        ]
        done = []
        for up, hat, scale in loaded:
            gain_part, bias_part = fold(up * hat), fold(up)
            up = up * gain_one
            grad = scale * (
                up
                - jnp.mean(up, axis=1, keepdims=True)
                - hat * jnp.mean(up * hat, axis=1, keepdims=True)
            )
            done.append((gain_part, bias_part, grad))
        for rows, (_, _, grad) in zip(spots, done):
            gone[rows, :] = grad
            gproj[rows, :] = grad.astype(BF)
        sums[0:8, :] += done[0][0] + done[1][0] + done[2][0] + done[3][0]
        sums[8:16, :] += done[0][1] + done[1][1] + done[2][1] + done[3][1]

    def unmix(i):
        rows = at(i, 256)
        part = nt(gproj[rows, 0:AH], wo[0]) + nt(gproj[rows, AH:D], wo[1])
        gctx[rows, :] = part.astype(BF)

    loop(6, norm_one_back)
    loop(2, unmix)
    stores.append(start_copy(gone, gone_any, sems.at[5]))
    for c in range(2):
        gout[c] = tn(ctx[...], gproj[:, AH * c : AH * c + AH]).astype(BF)
        for n in range(4):
            for r in range(4):
                source = gout.at[c, pl.ds(192 * n + 48 * r, 48), :]
                ship(keep, send, place, 4 * c + r, n, pl.ds(192, 48), source, sems.at[2])
    unmix(2)
    for k in range(4):
        gvec[k : k + 1, :] = jnp.sum(sums[8 * k : 8 * k + 8, :], axis=0, keepdims=True)
    gvec[4:8, :] = jnp.zeros((4, D), F32)
    stores.append(start_copy(gctx, gctx_any, sems.at[6]))
    for copy in stores:
        copy.wait()
    pltpu.make_async_copy(gouter, gouter, sems.at[0]).wait()
    pltpu.make_async_copy(ginner, ginner, sems.at[1]).wait()
    pltpu.make_async_copy(gout, gout, sems.at[2]).wait()


def mixer_backward(
    place, vec, gvec, xm_any, packed_any, plong_any, pshort_any, dw_any, kc_any, cq_any, kp_any,
    cv_any, gctx_any, p0, p1, p2, p3, p4, p5, p6, p7,
    keep, send0, send1, send2, send3, grads_any, gdep_any,
    wm, xm, packed, plong, pshort, dw, kc, cq, kp, cv, gctx,
    xpad, gcp, gdp, grads, gqc, dkv, gkc, glog, gprob, gdep, gb, spread, gather, wk, sem, sems,
    out_sem,
):
    arrays = (
        (gctx_any, gctx), (kp_any, kp), (cv_any, cv), (packed_any, packed), (kc_any, kc),
        (xm_any, xm), (plong_any, plong), (pshort_any, pshort), (dw_any, dw), (cq_any, cq),
    )
    def begin(first, last):
        return [start_copy(*arrays[k], sems.at[k]) for k in range(first, last)]

    loads = begin(0, 3)
    zero_gaps(xpad)
    zero_gaps(gcp)
    zero_gaps(gdp)
    spread[...] = head_spread()
    gather[...] = head_gather()
    gdep[...] = jnp.zeros((8 * TAPS, D), F32)
    for copy in loads:
        copy.wait()
    loads = begin(3, 6)
    fetch_mixer(place, (p0, p1, p2, p3, p4, p5, p6, p7), wm, sem)
    late = begin(6, 10)
    for start, rows, pstart in SEGS:
        gcp[pstart : pstart + rows, :] = gctx[start : start + rows, AH:D].astype(F32)

    def dynamic(i):
        rows = at(i, 128)
        ps = padded_start(i)
        wide = pl.ds(pl.multiple_of(ps - 8, 8), 144)
        weights = nn(spread_taps(kp[wide, :]), spread[...])
        columns = []
        for c in range(3):
            lanes = slice(128 * c, 128 * c + 128)
            grad_wide = gcp[wide, lanes]
            values = cv[wide, lanes]
            grad = gcp[pl.ds(ps, 128), lanes]
            total = jnp.zeros((128, 128), F32)
            parts = []
            for j in range(TAPS):
                part = weights[144 * j : 144 * j + 144, lanes] * grad_wide
                total = total + part[12 - j : 140 - j, :]
                parts.append((grad * values[4 + j : 132 + j, :]).astype(BF))
            grads[rows, 3 * AH + 128 * c : 3 * AH + 128 * c + 128] = total.astype(BF)
            columns.append(jnp.concatenate(parts, axis=0))
        sums = nn(jnp.concatenate(columns, axis=1), gather[...])
        total = sums[0:128, :]
        for j in range(1, TAPS):
            total = total + pltpu.roll(sums[128 * j : 128 * j + 128, :], 8 * j, 1)
        gprob[rows, :] = total

    loop(6, dynamic)
    for copy in loads:
        copy.wait()
    pltpu.make_async_copy(wm, wm, sem).wait()
    wk[...] = tap_kernel(wm)

    def tap_softmax_back(i):
        rows = at(i, 384)
        probs = jnp.concatenate([kp[pl.ds(padded_start(3 * i + k), 128), :] for k in range(3)], axis=0)
        upper = gprob[rows, :]
        inner = probs * upper
        for shift in (64, 32, 16, 8):
            inner = inner + pltpu.roll(inner, shift, 1)
        glogits = (probs * (upper - inner)).astype(BF)
        glog[rows, :] = glogits
        gquery = nt(glogits, wk[...])
        gkc[rows, :] = (gquery * packed[rows, 0:AH].astype(F32)).astype(BF)
        gqc[rows, :] = gquery * kc[rows, :]

    loop(2, tap_softmax_back)
    for start, rows, pstart in SEGS:
        xpad[pstart : pstart + rows, :] = xm[start : start + rows, :].astype(F32)

    def point_back(c):
        part = nt(gkc[:, 0:256], wm[6, at(c, 256), :])
        part = part + nt(gkc[:, 256:384], wm[7, at(c, 256), 0:128])
        part = part.astype(BF).astype(F32)
        for start, rows, pstart in SEGS:
            gdp[pstart : pstart + rows, at(c, 256)] = part[start : start + rows, :]

    loop(3, point_back)
    copy_depth = start_copy(gdp, gdep_any, out_sem.at[1])

    def release(b):
        for n in range(4):
            where = b ^ place[0]
            chip, far_off = where >> 1, n ^ place[1]
            source = gb.at[b, pl.ds(192 * n, 192), :]

            @pl.when((where & 1) == 0)
            def _():
                pltpu.make_async_copy(source, keep.at[chip, far_off], out_sem.at[0]).start()

            for k, send in enumerate((send0, send1, send2, send3)):

                @pl.when(where == 2 * k + 1)
                def _():
                    pltpu.make_async_copy(source, send.at[far_off], out_sem.at[0]).start()

    def depth(i):
        ps = padded_start(i)
        wide = pl.ds(pl.multiple_of(ps - 8, 8), 144)
        for c in range(6):
            lanes = slice(128 * c, 128 * c + 128)
            tokens = xpad[pl.ds(ps, 128), lanes]
            grad_wide = gdp[wide, lanes]
            for j in range(TAPS):
                gdep[8 * j : 8 * j + 8, lanes] += fold(tokens * grad_wide[12 - j : 140 - j, :])

    loop(6, depth)
    for copy in late:
        copy.wait()
    gb[6] = tn(dw[...], gkc[:, 0:256]).astype(BF)
    gb[7, :, 0:128] = tn(dw[...], gkc[:, 256:384]).astype(BF)
    taps = [jnp.sum(gdep[8 * j : 8 * j + 8, :], axis=0, keepdims=True) for j in range(TAPS)]
    table = jnp.concatenate(
        taps + [jnp.zeros((7, D), F32), gvec[...], jnp.zeros((104, D), F32)], axis=0
    ).astype(BF)
    misc = tn(table, eye(128, BF))
    gkernel = nt(tn(cq[...], glog[...]).astype(BF), tap_permutation())
    for n in range(4):
        row = 192 * n
        part = misc[row : row + 96, :] + gkernel[96 * n : 96 * n + 96, :]
        gb[7, row : row + 96, 128:256] = part.astype(BF)
        gb[7, row + 96 : row + 192, 128:256] = misc[row + 96 : row + 192, :].astype(BF)
    release(6)
    release(7)

    def attend(row0, nq, key0, nk, pair, load, first):
        queries = packed[pl.ds(row0, nq), at(pair, 128)].astype(F32) * 0.125
        keys = packed[pl.ds(key0, nk), at(3 + pair, 128)]
        vals = packed[pl.ds(key0, nk), at(6 + pair, 128)]
        up = gctx[pl.ds(row0, nq), at(pair, 128)].astype(F32)
        lane = iota((nq, 128), 1)
        outs = []
        gkeys = jnp.zeros((nk, 128), F32)
        gvals = jnp.zeros((nk, 128), F32)
        for hh in range(2):
            mine = (lane >> 6) == hh
            query = jnp.where(mine, queries, 0.0).astype(BF)
            upper = jnp.where(mine, up, 0.0).astype(BF)
            probs_low = load(hh)
            gprobs = nt(upper, vals)
            parts = []
            for r in range(0, nq, 32):
                probs, part = probs_low[r : r + 32, :].astype(F32), gprobs[r : r + 32, :]
                inner = jnp.sum(probs * part, axis=1, keepdims=True)
                parts.append((probs * (part - inner)).astype(BF))
            gscores = jnp.concatenate(parts, axis=0)
            outs.append(nn(gscores, keys))
            gkeys = gkeys + tn(gscores, query)
            gvals = gvals + tn(probs_low, upper)
        both = jnp.where(lane < 64, outs[0], outs[1]) * 0.125
        both = both + gqc[pl.ds(row0, nq), at(pair, 128)]
        grads[pl.ds(row0, nq), at(pair, 128)] = both.astype(BF)
        span = pl.ds(key0, nk)
        if nq == nk:
            grads[span, at(3 + pair, 128)] = gkeys.astype(BF)
            grads[span, at(6 + pair, 128)] = gvals.astype(BF)
        elif first:
            dkv[0] = gkeys
            dkv[1] = gvals
        else:
            grads[span, at(3 + pair, 128)] = (dkv[0] + gkeys).astype(BF)
            grads[span, at(6 + pair, 128)] = (dkv[1] + gvals).astype(BF)

    def long_attend(pair):
        for block in range(2):
            attend(
                256 * block, 256, 0, LONG, pair,
                lambda hh: plong[2 * pair + hh, 256 * block : 256 * block + 256, :],
                block == 0,
            )

    loop(3, long_attend)
    for seg in range(2):
        for pair in range(3):
            row0 = LONG + 128 * seg
            attend(row0, 128, row0, SHORT, pair, lambda hh: pshort[seg, 2 * pair + hh, :, :], True)
    copy_grads = start_copy(grads, grads_any, out_sem.at[2])

    def weights(b):
        gb[b] = tn(xm[...], grads[:, at(b, 256)]).astype(BF)
        release(b)

    loop(6, weights)
    copy_depth.wait()
    copy_grads.wait()
    pltpu.make_async_copy(gb, gb, out_sem.at[0]).wait()


def input_gradient(
    place, llen, slen, vec, grads_any, gdp_any, gone_any, p0, p1, p2, p3, p4, p5, p6, p7,
    il, is_, wm, grads, gdp, rest, sem, sems
):
    arrays = ((gone_any, rest), (gdp_any, gdp), (grads_any, grads))
    loads = [start_copy(a, b, sems.at[k]) for k, (a, b) in enumerate(arrays)]
    fetch_mixer(place, (p0, p1, p2, p3, p4, p5, p6, p7), wm, sem)
    for copy in loads:
        copy.wait()

    def depth(i):
        ps = padded_start(i)
        for c in range(6):
            lanes = slice(128 * c, 128 * c + 128)
            window = gdp[pl.ds(pl.multiple_of(ps - 8, 8), 144), lanes]
            total = rest[at(i, 128), lanes]
            for j in range(TAPS):
                total = total + vec[j : j + 1, lanes] * window[12 - j : 140 - j, :]
            rest[at(i, 128), lanes] = total

    loop(6, depth)
    pltpu.make_async_copy(wm, wm, sem).wait()

    def inputs(i):
        rows = at(i, 256)
        total = rest[rows, :]
        for b in range(6):
            total = total + nt(grads[rows, 256 * b : 256 * b + 256], wm[b])
        return total

    def inputs_long(i):
        live = i * 256 + iota((256, D), 0) < llen[0]
        il[at(i, 256), :] = jnp.where(live, inputs(i), 0.0).astype(BF)

    loop(2, inputs_long)
    total = inputs(2)
    row = iota((128, D), 0)
    for seg in range(2):
        part = total[128 * seg : 128 * seg + 128, :]
        is_[128 * seg : 128 * seg + 128, :] = jnp.where(row < slen[seg], part, 0.0).astype(BF)


def pack(
    place, qkv, depth, point, kernel, convout, g1, b1, inner, outer, out, g2, b2, mixer, ffn
):
    for w in range(SLOTS):

        @pl.when(place[0] == w)
        def _():
            g, r = w // 4, w % 4
            ffn[0:96, :] = inner[g, :, AH * r : AH * r + AH]
            ffn[96:192, :] = outer[g, 96 * r : 96 * r + 96, :]
            ffn[192:240, :] = out[48 * r : 48 * r + 48, AH * g : AH * g + AH]
            if w < 4:
                mixer[...] = qkv[:, 256 * w : 256 * w + 256]
            elif w == 4:
                mixer[:, 0:128] = qkv[:, 1024:1152]
                mixer[:, 128:256] = convout[:, 0:128]
            elif w == 5:
                mixer[...] = convout[:, 128:384]
            elif w == 6:
                mixer[...] = point[:, 0:256]
            else:
                mixer[:, 0:128] = point[:, 256:384]
                rows = [v[...].astype(F32).reshape(1, 192) for v in (g1, b1, g2, b2)]
                table = jnp.concatenate(
                    [depth[...].astype(F32), jnp.zeros((7, 192), F32)]
                    + rows
                    + [jnp.zeros((108, 192), F32)],
                    axis=0,
                )
                left = tn(table.astype(BF), eye(128, BF))
                row, col = iota((54, 128), 0), iota((54, 128), 1)
                right = tn(kernel[...], jnp.where(col == row + 64, 1.0, 0.0).astype(BF))
                mixer[0:96, 128:256] = (left[0:96, :] + right).astype(BF)
                mixer[96:192, 128:256] = left[96:192, :].astype(BF)


def unpack_ffn(place, p0, p1, p2, p3, p4, p5, p6, p7, inner, outer, out):
    for core, pieces in enumerate(((p0, p1, p2, p3), (p4, p5, p6, p7))):
        for chip, piece in enumerate(pieces):
            slot = slot_of(place[0], core, chip)
            g, r = slot >> 2, slot & 3
            inner[g, :, at(r, AH)] = piece[0:96, :].astype(F32)
            outer[g, at(r, 96), :] = piece[96:192, :].astype(F32)
            out[at(r, 48), at(g, AH)] = piece[192:240, :].astype(F32)


def unpack_mixer(
    place, p0, p1, p2, p3, p4, p5, p6, p7,
    qkv, depth, point, kernel, convout, g1, b1, g2, b2, packed,
):
    for core, pieces in enumerate(((p0, p1, p2, p3), (p4, p5, p6, p7))):
        for chip, piece in enumerate(pieces):
            packed[slot_of(place[0], core, chip)] = piece[...]
    for w in range(4):
        qkv[:, 256 * w : 256 * w + 256] = packed[w].astype(F32)
    qkv[:, 1024:1152] = packed[4, :, 0:128].astype(F32)
    convout[:, 0:128] = packed[4, :, 128:256].astype(F32)
    convout[:, 128:384] = packed[5].astype(F32)
    point[:, 0:256] = packed[6].astype(F32)
    point[:, 256:384] = packed[7, :, 0:128].astype(F32)
    misc = packed[7, :, 128:256]
    table = nt(eye(128, BF), misc)
    depth[...] = table[0:TAPS, :]
    for k, ref in enumerate((g1, b1, g2, b2)):
        ref[...] = table[16 + k : 17 + k, :].reshape(192)
    kernel[...] = table[64:118, 0:96]


SMEM = pl.BlockSpec(memory_space=pltpu.SMEM)
VMEM = pl.BlockSpec(memory_space=pltpu.VMEM)
ANY = pl.BlockSpec(memory_space=pl.ANY)


VMEM_MIB = {'unpack_ffn': 12, 'unpack_mixer': 12}


def call(kernel, specs, outs, scratch, flops, *args, out_specs=None):
    return pl.pallas_call(
        kernel,
        out_shape=[jax.ShapeDtypeStruct(s, d) for s, d in outs],
        in_specs=specs,
        out_specs=out_specs or [VMEM] * len(outs),
        scratch_shapes=[pltpu.VMEM(s, d) for s, d in scratch[0]] + list(scratch[1:]),
        compiler_params=pltpu.CompilerParams(vmem_limit_bytes=VMEM_MIB.get(kernel.__name__, 60) << 20),
        cost_estimate=pl.CostEstimate(flops=flops, bytes_accessed=1 << 20, transcendentals=0),
        name=kernel.__name__,
    )(*args)


def forward_mixer(scalars, xl, xs, pieces):
    outs = [
        ((ROWS, D), BF), ((ROWS, 3 * AH), BF),
        ((HEADS, LONG, LONG), BF), ((2, HEADS, SHORT, SHORT), BF),
        ((ROWS, D), BF), ((ROWS, AH), F32), ((ROWS, AH), BF), ((PAD, 128), F32),
        ((PAD, AH), F32), ((ROWS, D), BF), ((24, D), F32),
    ]
    scratch = [((SLOTS, D, 256), BF), ((PAD, D), F32), ((256, AH), BF), ((AH, 128), BF)]
    return call(
        mixer_forward, [SMEM] * 3 + [VMEM] * 2 + [ANY] * 8, outs,
        (scratch + outs[:-1], pltpu.SemaphoreType.DMA, pltpu.SemaphoreType.DMA((10,))), 30 * 10**9,
        *scalars, xl, xs, *pieces, out_specs=[ANY] * 10 + [VMEM],
    )


def feed_forward(scalars, xm, ctx, vec, cl, cs, pieces):
    outs = [
        ((LONG, D), BF), ((2 * SHORT, D), BF), ((4, 4, 240, AH), BF), ((4, 4, 240, AH), BF),
        ((ROWS, D), F32), ((ROWS, D), BF), ((8, D), F32),
    ]
    scratch = [
        ((2, D, AH), BF), ((4, AH, D), BF), ((4, D, AH), BF), ((ROWS, D), BF), ((ROWS, D), BF),
        ((ROWS, D), BF), ((ROWS, D), BF), ((ROWS, D), F32), ((ROWS, D), F32),
        ((2, ROWS, AH), BF), ((2, ROWS, AH), BF), ((4, ROWS, D), BF), ((4, ROWS, D), F32),
        ((2, ROWS, AH), F32), ((ROWS, 128), F32), ((256, D), F32), ((256, D), F32),
        ((ROWS, D), BF), ((ROWS, D), BF), ((ROWS, D), BF), ((2, ROWS, AH), BF),
        ((4, AH, D), BF), ((4, D, AH), BF), ((ROWS, D), F32), ((ROWS, D), BF), ((32, D), F32),
    ]
    return call(
        ffn_both, [SMEM] * 3 + [VMEM] + [ANY] * 12, outs,
        (scratch, pltpu.SemaphoreType.DMA((7,))), 60 * 10**9,
        *scalars, vec, xm, ctx, cl, cs, *pieces, out_specs=[ANY] * 6 + [VMEM],
    )


def backward_mixer(place, vec, gvec, arrays, pieces):
    outs = [((4, 4, 192, 256), BF)] + [((4, 192, 256), BF)] * 4
    outs += [((ROWS, 4 * AH), BF), ((PAD, D), F32)]
    scratch = [((SLOTS, D, 256), BF)] + [(a.shape, a.dtype) for a in arrays] + [
        ((PAD, D), F32), ((PAD, AH), F32), ((PAD, D), F32), ((ROWS, 4 * AH), BF),
        ((ROWS, AH), F32), ((2, LONG, 128), F32), ((ROWS, AH), BF), ((ROWS, 128), BF),
        ((ROWS, 128), F32),
        ((8 * TAPS, D), F32), ((SLOTS, D, 256), BF), ((256, AH), BF), ((AH, 128), BF),
        ((AH, 128), BF),
    ]
    dma = pltpu.SemaphoreType.DMA
    return call(
        mixer_backward, [SMEM] + [VMEM] * 2 + [ANY] * 18, outs,
        (scratch, dma, dma((10,)), dma((3,))), 40 * 10**9,
        place, vec, gvec, *arrays, *pieces, out_specs=[ANY] * 7,
    )


def backward_inputs(scalars, vec, grads, gdp, gone, pieces):
    scratch = [
        ((SLOTS, D, 256), BF), ((ROWS, 4 * AH), BF), ((PAD, D), F32), ((ROWS, D), F32),
    ]
    dma = pltpu.SemaphoreType.DMA
    return call(
        input_gradient, [SMEM] * 3 + [VMEM] + [ANY] * 11, [((LONG, D), BF), ((2 * SHORT, D), BF)],
        (scratch, dma, dma((3,))), 5 * 10**9, *scalars, vec, grads, gdp, gone, *pieces,
    )


def far(values, bit):
    return lax.ppermute(values, "narrow", [(i, i ^ bit) for i in range(4)])


def near(values, bit):
    return lax.ppermute(values, "wide", [(i, i ^ bit) for i in range(SLOTS)])


def gather_narrow(piece):
    return jnp.stack([piece] + [far(piece, k) for k in (1, 2, 3)])


def gather_chips(block):
    return [block] + [near(block, k) for k in (2, 4, 6)]


def gather_cores(blocks):
    return blocks + [near(block, 1) for block in blocks]


def total(first, others):
    result = first.astype(F32)
    for other in others:
        result = result + other.astype(F32)
    return result.astype(BF)


def reduce_cores(keep, sent):
    return [total(keep[k], [sent[k]]) for k in range(4)]


def send_chips(parts):
    return [near(parts[k], 2 * k) for k in (1, 2, 3)]


def reduce_chips(first, others):
    return [total(first[k], [other[k] for other in others]) for k in range(4)]


def send_narrow(parts):
    return [far(parts[k], k) for k in (1, 2, 3)]


def body(
    long_tokens, long_lengths, short_tokens, short_lengths,
    w_qkv, w_depth, w_point, w_kernel, w_convout, w_out, norm1_gain, norm1_bias,
    w_inner, w_outer, norm2_gain, norm2_bias, long_cotangent, short_cotangent,
):
    place = jnp.stack([lax.axis_index("wide"), lax.axis_index("narrow")]).astype(jnp.int32)
    scalars = (place, long_lengths, short_lengths)
    xl, xs = long_tokens.reshape(LONG, D), short_tokens.reshape(2 * SHORT, D)
    cl, cs = long_cotangent.reshape(LONG, D), short_cotangent.reshape(2 * SHORT, D)
    mixer, ffn = call(
        pack, [SMEM] + [VMEM] * 12, [((192, 256), BF), ((240, AH), BF)], ([],), 10**9,
        place, w_qkv, w_depth, w_point, w_kernel.T, w_convout, norm1_gain, norm1_bias,
        w_inner, w_outer, w_out, norm2_gain, norm2_bias,
    )
    mixer = gather_narrow(mixer)
    mixer, ffn = lax.optimization_barrier((mixer, ffn))
    mixer = gather_chips(mixer)
    ffn = gather_narrow(ffn)
    mixer, ffn = lax.optimization_barrier((mixer, ffn))
    mixer = gather_cores(mixer)
    ffn = gather_chips(ffn)
    xm, packed, plong, pshort, dw, kc, cq, kp, cv, ctx, vec = forward_mixer(scalars, xl, xs, mixer)
    ctx, ffn = lax.optimization_barrier((ctx, ffn))
    ffn = gather_cores(ffn)
    ol, os, keep, send, gone, gctx, gvec = feed_forward(scalars, xm, ctx, vec, cl, cs, ffn)
    ga = reduce_cores(keep, near(send, 1))
    ga_sent = send_chips(ga)
    gctx, ga = lax.optimization_barrier((gctx, ga))
    keep, s0, s1, s2, s3, grads, gdp = backward_mixer(
        place, vec, gvec, (xm, packed, plong, pshort, dw, kc, cq, kp, cv, gctx), mixer
    )
    gb = [total(keep[1], [near(s1, 1)]), total(keep[2], [near(s2, 1)])]
    keep, s0, s3, gb, ga_sent = lax.optimization_barrier((keep, s0, s3, gb, ga_sent))
    gb_sent = [near(gb[0], 2), near(gb[1], 4)]
    gb3 = total(keep[3], [near(s3, 1)])
    gb_sent.append(near(gb3, 6))
    gb = [total(keep[0], [near(s0, 1)]), gb[0], gb[1], gb3]
    ga_sent, gb = lax.optimization_barrier((ga_sent, gb))
    ga = reduce_chips(ga[0], ga_sent)
    ga_sent = [far(ga[1], 1), far(ga[2], 2)]
    grads, ga = lax.optimization_barrier((grads, ga))
    il, is_ = backward_inputs(scalars, vec, grads, gdp, gone, mixer)
    last, il = lax.optimization_barrier((ga[3], il))
    ga_sent, gb_sent, il = lax.optimization_barrier((ga_sent, gb_sent, il))
    ga_sent.append(far(last, 3))
    ga = gather_chips(lax.psum(total(ga[0], ga_sent), "hi"))
    gb = reduce_chips(gb[0], gb_sent)
    gb = gather_chips(lax.psum(total(gb[0], send_narrow(gb)), "hi"))
    inner, outer, out = call(
        unpack_ffn, [SMEM] + [VMEM] * 8,
        [((2, 96, 4 * AH), F32), ((2, AH, AH), F32), ((192, D), F32)],
        ([],), 10**9, place, *gather_cores(ga),
    )
    gb, inner = lax.optimization_barrier((gb, inner))
    outs = [
        ((192, 3 * AH), F32), ((TAPS, 192), F32), ((192, AH), F32), ((54, 96), F32), ((192, AH), F32),
    ] + [((192,), F32)] * 4
    qkv, depth, point, kernel, convout, g1, b1, g2, b2 = call(
        unpack_mixer, [SMEM] + [VMEM] * 8, outs, ([((SLOTS, 192, 256), BF)],), 10**9,
        place, *gather_cores(gb),
    )
    return (
        ol.reshape(long_tokens.shape), os.reshape(short_tokens.shape),
        il.reshape(long_tokens.shape), is_.reshape(short_tokens.shape),
        qkv, depth, point, kernel.T, convout, out, g1, b1, inner, outer, g2, b2,
    )


def solution(mesh):
    wide, narrow = mesh.shape["wide"], mesh.shape["narrow"]
    inner_mesh = Mesh(mesh.devices.reshape(wide // SLOTS, SLOTS, narrow), ("hi", "wide", "narrow"))
    every = ("hi", "wide", "narrow")
    rows = P(every, None, None)
    weights = (
        P("narrow", None), P(None, "narrow"), P("narrow", None), P("narrow", None),
        P("narrow", None), P("narrow", None), P("narrow"), P("narrow"),
        P(None, "narrow", None), P(None, "narrow", None), P("narrow"), P("narrow"),
    )
    return jax.shard_map(
        body,
        mesh=inner_mesh,
        in_specs=(rows, P(every), rows, P(every)) + weights + (rows, rows),
        out_specs=(rows, rows, rows, rows) + weights,
        check_vma=False,
    )
```

```python
import jax
import jax.numpy as jnp
from jax import lax
from jax.experimental import pallas as pl
from jax.experimental.pallas import tpu as pltpu
from jax.sharding import Mesh
from jax.sharding import PartitionSpec as P

BF = jnp.bfloat16
F32 = jnp.float32
EPS = 1e-12
D = 768
AH = 384
HEADS = 6
TAPS = 9
LONG = 512
SHORT = 128
ROWS = 768
PAD = 800
SLOTS = 8
NEG = -1000000000.0
PSTART = tuple(8 + 128 * i + 8 * max(i - 3, 0) for i in range(6))
SEGS = ((0, 512, 8), (512, 128, 528), (640, 128, 664))


def nn(a, b):
    return lax.dot_general(a, b, (((1,), (0,)), ((), ())), preferred_element_type=F32)


def nt(a, b):
    return lax.dot_general(a, b, (((1,), (1,)), ((), ())), preferred_element_type=F32)


def tn(a, b):
    return lax.dot_general(a, b, (((0,), (0,)), ((), ())), preferred_element_type=F32)


def iota(shape, axis):
    return lax.broadcasted_iota(jnp.int32, shape, axis)


def loop(count, body):
    def step(i, carry):
        body(i)
        return carry

    lax.fori_loop(0, count, step, 0)


def at(i, size):
    if isinstance(i, int):
        return pl.ds(i * size, size)
    return pl.ds(pl.multiple_of(i * size, size), size)


def padded_start(i):
    return pl.multiple_of(8 + 128 * i + 8 * jnp.maximum(i - 3, 0), 8)


def zero_gaps(ref):
    for start in (0, 520, 656, 792):
        ref[start : start + 8, :] = jnp.zeros((8, ref.shape[1]), ref.dtype)


def eye(n, dtype):
    return jnp.where(iota((n, n), 0) == iota((n, n), 1), 1.0, 0.0).astype(dtype)


def tap_permutation():
    row, col = iota((128, 128), 0), iota((128, 128), 1)
    head, tap = col & 7, col >> 3
    keep = (head < HEADS) & (tap < TAPS) & (row == 64 + head * TAPS + tap)
    return jnp.where(keep, 1.0, 0.0).astype(BF)


def head_spread():
    row, col = iota((256, AH), 0), iota((256, AH), 1)
    return jnp.where((row & 127) == (col >> 6), 1.0, 0.0).astype(BF)


def head_gather():
    row, col = iota((AH, 128), 0), iota((AH, 128), 1)
    return jnp.where((row >> 6) == col, 1.0, 0.0).astype(BF)


def split_two(values):
    high = values.astype(BF)
    low = (values - high.astype(F32)).astype(BF)
    return jnp.concatenate([high, low], axis=1)


def spread_taps(probs):
    moved = [probs] + [pltpu.roll(probs, 128 - 8 * j, 1) for j in range(1, TAPS)]
    return split_two(jnp.concatenate(moved, axis=0))


def tap_kernel(wm):
    stored = jnp.concatenate([wm[7, 192 * n : 192 * n + 96, 128:256] for n in range(4)], axis=0)
    return nn(stored, tap_permutation()).astype(BF)


def slot_of(where, core, chip):
    return 2 * ((where >> 1) ^ chip) + ((where & 1) ^ core)


def fetch_mixer(place, pieces, wm, sem):
    for at_core in range(2):
        for chip in range(4):
            piece = pieces[4 * at_core + chip]
            slot = slot_of(place[0], at_core, chip)

            def fetch(k):
                pltpu.make_async_copy(piece.at[k], wm.at[slot, at(place[1] ^ k, 192), :], sem).start()

            loop(4, fetch)


def mixer_forward(
    place, llen, slen, xl, xs, p0, p1, p2, p3, p4, p5, p6, p7,
    xm_any, packed_any, plong_any, pshort_any, dw_any, kc_any, cq_any, kp_any, cv_any, ctx_any, vec,
    wm, xpad, spread, wk, xm, packed, plong, pshort, dw, kc, cq, kp, cv, ctx, sem, sems
):
    fetch_mixer(place, (p0, p1, p2, p3, p4, p5, p6, p7), wm, sem)
    lens = (llen[0], slen[0], slen[1])
    zero_gaps(xpad)
    zero_gaps(cv)
    zero_gaps(kp)
    for i in range(6):
        seg = max(i - 3, 0)
        base = 128 * i if i < 4 else 0
        tokens = xl[128 * i : 128 * i + 128, :] if i < 4 else xs[128 * (i - 4) : 128 * (i - 3), :]
        live = base + iota((128, D), 0) < lens[seg]
        values = jnp.where(live, tokens.astype(F32), 0.0)
        xpad[PSTART[i] : PSTART[i] + 128, :] = values
        xm[128 * i : 128 * i + 128, :] = values.astype(BF)
    stores = [start_copy(xm, xm_any, sems.at[0])]
    spread[...] = head_spread()
    pltpu.make_async_copy(wm, wm, sem).wait()
    vec[...] = nt(eye(128, BF), wm[7, :, 128:256])[0:24, :]
    wk[...] = tap_kernel(wm)

    def depth(i):
        ps = padded_start(i)
        for c in range(6):
            lanes = slice(128 * c, 128 * c + 128)
            window = xpad[pl.ds(pl.multiple_of(ps - 8, 8), 144), lanes]
            total = jnp.zeros((128, 128), F32)
            for j in range(TAPS):
                total = total + vec[j : j + 1, lanes] * window[4 + j : 132 + j, :]
            dw[at(i, 128), lanes] = total.astype(BF)

    def project(b):
        packed[:, at(b, 256)] = nn(xm[...], wm[b]).astype(BF)
        depth(b)

    loop(4, project)
    depth(jnp.int32(4))
    part = nn(xm[...], wm[4])
    packed[:, 1024:1152] = part[:, 0:128].astype(BF)
    for start, rows, pstart in SEGS:
        cv[pstart : pstart + rows, 0:128] = part[start : start + rows, 128:256]
    depth(jnp.int32(5))
    part = nn(xm[...], wm[5])
    for start, rows, pstart in SEGS:
        cv[pstart : pstart + rows, 128:384] = part[start : start + rows, :]
    stores += [
        start_copy(packed, packed_any, sems.at[1]), start_copy(dw, dw_any, sems.at[2]),
        start_copy(cv, cv_any, sems.at[3]),
    ]
    kc[:, 0:256] = nn(dw[...], wm[6])
    kc[:, 256:384] = nn(dw[...], wm[7, :, 0:128])
    stores.append(start_copy(kc, kc_any, sems.at[4]))

    def tap_softmax(i):
        rows = at(i, 384)
        query = (kc[rows, :] * packed[rows, 0:AH].astype(F32)).astype(BF)
        cq[rows, :] = query
        logits = nn(query, wk[...])
        real = iota((384, 128), 1) < 8 * TAPS
        top = jnp.where(real, logits, NEG * 1e20)
        for shift in (64, 32, 16, 8):
            top = jnp.maximum(top, pltpu.roll(top, shift, 1))
        ex = jnp.where(real, jnp.exp(logits - top), 0.0)
        total = ex
        for shift in (64, 32, 16, 8):
            total = total + pltpu.roll(total, shift, 1)
        probs = ex * (1.0 / total)
        for k in range(3):
            kp[pl.ds(padded_start(3 * i + k), 128), :] = probs[128 * k : 128 * k + 128, :]

    loop(2, tap_softmax)

    def dynamic(u):
        for i in (2 * u, 2 * u + 1):
            ps = padded_start(i)
            weights = nn(spread_taps(kp[pl.ds(ps, 128), :]), spread[...])
            for c in range(3):
                lanes = slice(128 * c, 128 * c + 128)
                window = cv[pl.ds(pl.multiple_of(ps - 8, 8), 144), lanes]
                out = jnp.zeros((128, 128), F32)
                for j in range(TAPS):
                    out = out + weights[128 * j : 128 * j + 128, lanes] * window[4 + j : 132 + j, :]
                ctx[at(i, 128), AH + 128 * c : AH + 128 * c + 128] = out.astype(BF)

    loop(3, dynamic)
    stores += [start_copy(cq, cq_any, sems.at[5]), start_copy(kp, kp_any, sems.at[6])]

    def attend(row0, nq, key0, nk, limit, pair, store):
        queries = packed[pl.ds(row0, nq), at(pair, 128)].astype(F32) * 0.125
        keys = packed[pl.ds(key0, nk), at(3 + pair, 128)].astype(F32)
        vals = packed[pl.ds(key0, nk), at(6 + pair, 128)]
        lane, key_lane = iota((nq, 128), 1), iota((nk, 128), 1)
        bias = jnp.where(iota((nk, 128), 0) < limit, 0.0, NEG)
        outs = []
        for hh in range(2):
            spare = 64 * (1 - hh)
            query = jnp.where((lane >> 6) == hh, queries, jnp.where(lane == spare, 1.0, 0.0))
            scores = nt(query.astype(BF), jnp.where(key_lane == spare, bias, keys).astype(BF))
            parts = []
            for r in range(0, nq, 32):
                part = scores[r : r + 32, :]
                part = jnp.exp(part - jnp.max(part, axis=1, keepdims=True))
                part = part * (1.0 / jnp.sum(part, axis=1, keepdims=True))
                parts.append(part.astype(BF))
            probs = jnp.concatenate(parts, axis=0)
            store(hh, probs)
            outs.append(nn(probs, vals))
        both = jnp.where(lane < 64, outs[0], outs[1])
        ctx[pl.ds(row0, nq), at(pair, 128)] = both.astype(BF)

    def long_attend(i):
        pair, block = i >> 1, i & 1
        row0 = pl.multiple_of(block * 256, 256)

        def store(hh, probs):
            plong[2 * pair + hh, pl.ds(row0, 256), :] = probs

        attend(row0, 256, 0, LONG, lens[0], pair, store)

    loop(6, long_attend)
    stores.append(start_copy(plong, plong_any, sems.at[7]))
    for seg in range(2):
        for pair in range(3):

            def store(hh, probs):
                pshort[seg, 2 * pair + hh, :, :] = probs

            row0 = LONG + 128 * seg
            attend(row0, 128, row0, SHORT, lens[1 + seg], pair, store)
    stores += [start_copy(pshort, pshort_any, sems.at[8]), start_copy(ctx, ctx_any, sems.at[9])]
    for copy in stores:
        copy.wait()


def gelu_parts(hidden):
    cdf = 0.5 + 0.5 * lax.erf(hidden * 0.7071067811865476)
    return cdf, jnp.exp(hidden * hidden * -0.5) * 0.3989422804014327


def fold(values):
    return jnp.sum(values.reshape(values.shape[0] // 8, 8, values.shape[1]), axis=0)


def start_copy(source, target, sem):
    copy = pltpu.make_async_copy(source, target, sem)
    copy.start()
    return copy


def ship(keep, send, place, slot, shard, rows, source, sem):
    where = slot ^ place[0]
    chip, far_off = where >> 1, shard ^ place[1]

    @pl.when((where & 1) == 0)
    def _():
        pltpu.make_async_copy(source, keep.at[chip, far_off, rows, :], sem).start()

    @pl.when((where & 1) == 1)
    def _():
        pltpu.make_async_copy(source, send.at[chip, far_off, rows, :], sem).start()


def ffn_both(
    place, llen, slen, vec, xm_any, ctx_any, cl, cs, p0, p1, p2, p3, p4, p5, p6, p7,
    ol, os, keep, send, gone_any, gctx_any, gvec,
    wo, wi, wu, xm, ctx, cot, out, res, xhat, grouped, gffn, active, slope, ffn, rstd,
    hid_a, hid_b, ghid_a, ghid_b, gproj, gout, ginner, gouter, gone, gctx, sums, sems,
):
    loads = [start_copy(ctx_any, ctx, sems.at[3]), start_copy(xm_any, xm, sems.at[4])]

    def fetch(part):
        for core, pieces in enumerate(((p0, p1, p2, p3), (p4, p5, p6, p7))):
            for chip, piece in enumerate(pieces):
                slot = slot_of(place[0], core, chip)
                g, r = slot >> 2, slot & 3

                def one(k):
                    n = place[1] ^ k
                    if part == 0:
                        rows = pl.ds(pl.multiple_of(192 * n + 48 * r, 48), 48)
                        source, target = pl.ds(192, 48), wo.at[g, rows, :]
                    elif part == 1:
                        source, target = pl.ds(0, 96), wi.at[slot >> 1, at(n, 96), at(slot & 1, AH)]
                    else:
                        rows = at(4 * (n & 1) + r, 96)
                        source, target = pl.ds(96, 96), wu.at[2 * g + (n >> 1), rows, :]
                    pltpu.make_async_copy(piece.at[k, source, :], target, sems.at[part]).start()

                loop(4, one)

    fetch(0)
    gain_one, bias_one = vec[16:17, :], vec[17:18, :]
    gain_two, bias_two = vec[18:19, :], vec[19:20, :]
    sums[...] = jnp.zeros((32, D), F32)
    ffn[...] = jnp.zeros((2, ROWS, AH), F32)
    for copy in loads:
        copy.wait()
    pltpu.make_async_copy(wo, wo, sems.at[0]).wait()
    fetch(1)
    fetch(2)
    cots = [
        start_copy(cl, cot.at[0:LONG], sems.at[5]), start_copy(cs, cot.at[LONG:ROWS], sems.at[6])
    ]

    def mix(i):
        rows = at(i, 256)
        for c in range(2):
            lanes = slice(AH * c, AH * c + AH)
            res[rows, lanes] = nn(ctx[rows, :], wo[c]) + xm[rows, lanes].astype(F32)

    def several(i):
        return [at(4 * i + k, 32) for k in range(4)]

    def norm_one(i):
        spots = several(i)
        done = []
        for values in [res[rows, :] for rows in spots]:
            center = values - jnp.mean(values, axis=1, keepdims=True)
            scale = lax.rsqrt(jnp.mean(center * center, axis=1, keepdims=True) + EPS)
            hat = center * scale
            done.append((hat, scale, hat * gain_one + bias_one))
        for rows, (hat, scale, first) in zip(spots, done):
            xhat[rows, :] = hat
            rstd[rows, :] = jnp.broadcast_to(scale, (32, 128))
            res[rows, :] = first
            short = first.astype(BF)
            grouped[0, rows, :] = short[:, 0:AH]
            grouped[1, rows, :] = short[:, AH:D]

    mix(0)
    for tile in range(3):
        if tile < 2:
            mix(tile + 1)
        norm_one(2 * tile)
        norm_one(2 * tile + 1)
    pltpu.make_async_copy(wi, wi, sems.at[1]).wait()
    pltpu.make_async_copy(wu, wu, sems.at[2]).wait()

    def hidden(t, target):
        b = lax.div(t, 3)
        target[...] = nn(grouped[b >> 1, at(t - 3 * b, 256), :], wi[b])

    def outward(t):
        b = lax.div(t, 3)
        rows = at(t - 3 * b, 256)
        ffn[b >> 1, rows, :] += nn(active[b, rows, :], wu[b])

    def act(t, source):
        b = lax.div(t, 3)
        m = t - 3 * b
        for part in range(16):
            values = source[16 * part : 16 * part + 16, :]
            rows = pl.ds(pl.multiple_of(m * 256 + 16 * part, 16), 16)
            cdf, density = gelu_parts(values)
            active[b, rows, :] = (values * cdf).astype(BF)
            slope[b, rows, :] = cdf + values * density

    def pair(u, first=False):
        t = 2 * u
        if not first:
            outward(t - 1)
        hidden(t + 1, hid_b)
        act(t, hid_a)
        outward(t)
        hidden(jnp.minimum(t + 2, 11), hid_a)
        act(t + 1, hid_b)

    hidden(jnp.int32(0), hid_a)
    pair(jnp.int32(0), True)
    loop(5, lambda u: pair(u + 1))
    outward(jnp.int32(11))
    for copy in cots:
        copy.wait()

    def norm_two(i):
        limit = jnp.where(i < 4, llen[0], slen[jnp.clip(i - 4, 0, 1)])
        base = jnp.where(i < 4, 128 * i, 0)
        spots = several(i)
        loaded = [
            (
                jnp.concatenate([ffn[0, rows, :], ffn[1, rows, :]], axis=1) + res[rows, :],
                cot[rows, :].astype(F32),
            )
            for rows in spots
        ]
        done = []
        for k, (values, up) in enumerate(loaded):
            center = values - jnp.mean(values, axis=1, keepdims=True)
            scale = lax.rsqrt(jnp.mean(center * center, axis=1, keepdims=True) + EPS)
            hat = center * scale
            result = (hat * gain_two + bias_two).astype(BF)
            live = base + 32 * k + iota((32, D), 0) < limit
            up = jnp.where(live, up, 0.0)
            gain_part, bias_part = fold(up * hat), fold(up)
            up = up * gain_two
            grad = scale * (
                up
                - jnp.mean(up, axis=1, keepdims=True)
                - hat * jnp.mean(up * hat, axis=1, keepdims=True)
            )
            done.append((result, gain_part, bias_part, grad))
        for rows, (result, _, _, grad) in zip(spots, done):
            out[rows, :] = result
            res[rows, :] = grad
            short = grad.astype(BF)
            gffn[0, rows, :] = short[:, 0:AH]
            gffn[1, rows, :] = short[:, AH:D]
        sums[16:24, :] += done[0][1] + done[1][1] + done[2][1] + done[3][1]
        sums[24:32, :] += done[0][2] + done[1][2] + done[2][2] + done[3][2]

    loop(6, norm_two)
    stores = [
        start_copy(out.at[0:LONG], ol, sems.at[3]), start_copy(out.at[LONG:ROWS], os, sems.at[4])
    ]
    ffn[...] = jnp.zeros((2, ROWS, AH), F32)

    def slopes(b, target):
        for part in range(6):
            rows = slice(128 * part, 128 * part + 128)
            back = nt(gffn[b >> 1, rows, :], wu[b])
            target[rows, :] = (back * slope[b, rows, :]).astype(BF)

    def gradients(b, source):
        g = b >> 1
        gouter[b] = tn(active[b], gffn[g]).astype(BF)
        ginner[b] = tn(grouped[g], source[...]).astype(BF)
        ffn[g] += nt(source[...], wi[b])
        for half in range(2):
            n = 2 * (b & 1) + half
            for w in range(4):
                outer = gouter.at[b, pl.ds(AH * half + 96 * w, 96), :]
                ship(keep, send, place, 4 * g + w, n, pl.ds(96, 96), outer, sems.at[0])
                inner = ginner.at[b, pl.ds(96 * w, 96), pl.ds(AH * half, AH)]
                ship(keep, send, place, 2 * b + half, w, pl.ds(0, 96), inner, sems.at[1])

    slopes(jnp.int32(0), ghid_a)

    def contract(u):
        b = 2 * u
        slopes(b + 1, ghid_b)
        gradients(b, ghid_a)
        slopes(jnp.minimum(b + 2, 3), ghid_a)
        gradients(b + 1, ghid_b)

    loop(2, contract)

    def norm_one_back(i):
        spots = several(i)
        loaded = [
            (
                res[rows, :] + jnp.concatenate([ffn[0, rows, :], ffn[1, rows, :]], axis=1),
                xhat[rows, :], rstd[rows, 0:1],
            )
            for rows in spots
        ]
        done = []
        for up, hat, scale in loaded:
            gain_part, bias_part = fold(up * hat), fold(up)
            up = up * gain_one
            grad = scale * (
                up
                - jnp.mean(up, axis=1, keepdims=True)
                - hat * jnp.mean(up * hat, axis=1, keepdims=True)
            )
            done.append((gain_part, bias_part, grad))
        for rows, (_, _, grad) in zip(spots, done):
            gone[rows, :] = grad
            gproj[rows, :] = grad.astype(BF)
        sums[0:8, :] += done[0][0] + done[1][0] + done[2][0] + done[3][0]
        sums[8:16, :] += done[0][1] + done[1][1] + done[2][1] + done[3][1]

    def unmix(i):
        rows = at(i, 256)
        part = nt(gproj[rows, 0:AH], wo[0]) + nt(gproj[rows, AH:D], wo[1])
        gctx[rows, :] = part.astype(BF)

    loop(6, norm_one_back)
    loop(2, unmix)
    stores.append(start_copy(gone, gone_any, sems.at[5]))
    for c in range(2):
        gout[c] = tn(ctx[...], gproj[:, AH * c : AH * c + AH]).astype(BF)
        for n in range(4):
            for r in range(4):
                source = gout.at[c, pl.ds(192 * n + 48 * r, 48), :]
                ship(keep, send, place, 4 * c + r, n, pl.ds(192, 48), source, sems.at[2])
    unmix(2)
    for k in range(4):
        gvec[k : k + 1, :] = jnp.sum(sums[8 * k : 8 * k + 8, :], axis=0, keepdims=True)
    gvec[4:8, :] = jnp.zeros((4, D), F32)
    stores.append(start_copy(gctx, gctx_any, sems.at[6]))
    for copy in stores:
        copy.wait()
    pltpu.make_async_copy(gouter, gouter, sems.at[0]).wait()
    pltpu.make_async_copy(ginner, ginner, sems.at[1]).wait()
    pltpu.make_async_copy(gout, gout, sems.at[2]).wait()


def mixer_backward(
    place, vec, gvec, xm_any, packed_any, plong_any, pshort_any, dw_any, kc_any, cq_any, kp_any,
    cv_any, gctx_any, p0, p1, p2, p3, p4, p5, p6, p7,
    keep, send0, send1, send2, send3, grads_any, gdep_any,
    wm, xm, packed, plong, pshort, dw, kc, cq, kp, cv, gctx,
    xpad, gcp, gdp, grads, gqc, dkv, gkc, glog, gprob, gdep, gb, spread, gather, wk, sem, sems,
    out_sem,
):
    arrays = (
        (gctx_any, gctx), (kp_any, kp), (cv_any, cv), (packed_any, packed), (kc_any, kc),
        (xm_any, xm), (plong_any, plong), (pshort_any, pshort), (dw_any, dw), (cq_any, cq),
    )
    def begin(first, last):
        return [start_copy(*arrays[k], sems.at[k]) for k in range(first, last)]

    loads = begin(0, 3)
    zero_gaps(xpad)
    zero_gaps(gcp)
    zero_gaps(gdp)
    spread[...] = head_spread()
    gather[...] = head_gather()
    gdep[...] = jnp.zeros((8 * TAPS, D), F32)
    for copy in loads:
        copy.wait()
    loads = begin(3, 6)
    fetch_mixer(place, (p0, p1, p2, p3, p4, p5, p6, p7), wm, sem)
    late = begin(6, 10)
    for start, rows, pstart in SEGS:
        gcp[pstart : pstart + rows, :] = gctx[start : start + rows, AH:D].astype(F32)

    def dynamic(i):
        rows = at(i, 128)
        ps = padded_start(i)
        wide = pl.ds(pl.multiple_of(ps - 8, 8), 144)
        weights = nn(spread_taps(kp[wide, :]), spread[...])
        columns = []
        for c in range(3):
            lanes = slice(128 * c, 128 * c + 128)
            grad_wide = gcp[wide, lanes]
            values = cv[wide, lanes]
            grad = gcp[pl.ds(ps, 128), lanes]
            total = jnp.zeros((128, 128), F32)
            parts = []
            for j in range(TAPS):
                part = weights[144 * j : 144 * j + 144, lanes] * grad_wide
                total = total + part[12 - j : 140 - j, :]
                parts.append((grad * values[4 + j : 132 + j, :]).astype(BF))
            grads[rows, 3 * AH + 128 * c : 3 * AH + 128 * c + 128] = total.astype(BF)
            columns.append(jnp.concatenate(parts, axis=0))
        sums = nn(jnp.concatenate(columns, axis=1), gather[...])
        total = sums[0:128, :]
        for j in range(1, TAPS):
            total = total + pltpu.roll(sums[128 * j : 128 * j + 128, :], 8 * j, 1)
        gprob[rows, :] = total

    loop(6, dynamic)
    for copy in loads:
        copy.wait()
    pltpu.make_async_copy(wm, wm, sem).wait()
    wk[...] = tap_kernel(wm)

    def tap_softmax_back(i):
        rows = at(i, 384)
        probs = jnp.concatenate([kp[pl.ds(padded_start(3 * i + k), 128), :] for k in range(3)], axis=0)
        upper = gprob[rows, :]
        inner = probs * upper
        for shift in (64, 32, 16, 8):
            inner = inner + pltpu.roll(inner, shift, 1)
        glogits = (probs * (upper - inner)).astype(BF)
        glog[rows, :] = glogits
        gquery = nt(glogits, wk[...])
        gkc[rows, :] = (gquery * packed[rows, 0:AH].astype(F32)).astype(BF)
        gqc[rows, :] = gquery * kc[rows, :]

    loop(2, tap_softmax_back)
    for start, rows, pstart in SEGS:
        xpad[pstart : pstart + rows, :] = xm[start : start + rows, :].astype(F32)

    def point_back(c):
        part = nt(gkc[:, 0:256], wm[6, at(c, 256), :])
        part = part + nt(gkc[:, 256:384], wm[7, at(c, 256), 0:128])
        part = part.astype(BF).astype(F32)
        for start, rows, pstart in SEGS:
            gdp[pstart : pstart + rows, at(c, 256)] = part[start : start + rows, :]

    loop(3, point_back)
    copy_depth = start_copy(gdp, gdep_any, out_sem.at[1])

    def release(b):
        for n in range(4):
            where = b ^ place[0]
            chip, far_off = where >> 1, n ^ place[1]
            source = gb.at[b, pl.ds(192 * n, 192), :]

            @pl.when((where & 1) == 0)
            def _():
                pltpu.make_async_copy(source, keep.at[chip, far_off], out_sem.at[0]).start()

            for k, send in enumerate((send0, send1, send2, send3)):

                @pl.when(where == 2 * k + 1)
                def _():
                    pltpu.make_async_copy(source, send.at[far_off], out_sem.at[0]).start()

    def depth(i):
        ps = padded_start(i)
        wide = pl.ds(pl.multiple_of(ps - 8, 8), 144)
        for c in range(6):
            lanes = slice(128 * c, 128 * c + 128)
            tokens = xpad[pl.ds(ps, 128), lanes]
            grad_wide = gdp[wide, lanes]
            for j in range(TAPS):
                gdep[8 * j : 8 * j + 8, lanes] += fold(tokens * grad_wide[12 - j : 140 - j, :])

    loop(6, depth)
    for copy in late:
        copy.wait()
    gb[6] = tn(dw[...], gkc[:, 0:256]).astype(BF)
    gb[7, :, 0:128] = tn(dw[...], gkc[:, 256:384]).astype(BF)
    taps = [jnp.sum(gdep[8 * j : 8 * j + 8, :], axis=0, keepdims=True) for j in range(TAPS)]
    table = jnp.concatenate(
        taps + [jnp.zeros((7, D), F32), gvec[...], jnp.zeros((104, D), F32)], axis=0
    ).astype(BF)
    misc = tn(table, eye(128, BF))
    gkernel = nt(tn(cq[...], glog[...]).astype(BF), tap_permutation())
    for n in range(4):
        row = 192 * n
        part = misc[row : row + 96, :] + gkernel[96 * n : 96 * n + 96, :]
        gb[7, row : row + 96, 128:256] = part.astype(BF)
        gb[7, row + 96 : row + 192, 128:256] = misc[row + 96 : row + 192, :].astype(BF)
    release(6)
    release(7)

    def attend(row0, nq, key0, nk, pair, load, first):
        queries = packed[pl.ds(row0, nq), at(pair, 128)].astype(F32) * 0.125
        keys = packed[pl.ds(key0, nk), at(3 + pair, 128)]
        vals = packed[pl.ds(key0, nk), at(6 + pair, 128)]
        up = gctx[pl.ds(row0, nq), at(pair, 128)].astype(F32)
        lane = iota((nq, 128), 1)
        outs = []
        gkeys = jnp.zeros((nk, 128), F32)
        gvals = jnp.zeros((nk, 128), F32)
        for hh in range(2):
            mine = (lane >> 6) == hh
            query = jnp.where(mine, queries, 0.0).astype(BF)
            upper = jnp.where(mine, up, 0.0).astype(BF)
            probs_low = load(hh)
            gprobs = nt(upper, vals)
            parts = []
            for r in range(0, nq, 32):
                probs, part = probs_low[r : r + 32, :].astype(F32), gprobs[r : r + 32, :]
                inner = jnp.sum(probs * part, axis=1, keepdims=True)
                parts.append((probs * (part - inner)).astype(BF))
            gscores = jnp.concatenate(parts, axis=0)
            outs.append(nn(gscores, keys))
            gkeys = gkeys + tn(gscores, query)
            gvals = gvals + tn(probs_low, upper)
        both = jnp.where(lane < 64, outs[0], outs[1]) * 0.125
        both = both + gqc[pl.ds(row0, nq), at(pair, 128)]
        grads[pl.ds(row0, nq), at(pair, 128)] = both.astype(BF)
        span = pl.ds(key0, nk)
        if nq == nk:
            grads[span, at(3 + pair, 128)] = gkeys.astype(BF)
            grads[span, at(6 + pair, 128)] = gvals.astype(BF)
        elif first:
            dkv[0] = gkeys
            dkv[1] = gvals
        else:
            grads[span, at(3 + pair, 128)] = (dkv[0] + gkeys).astype(BF)
            grads[span, at(6 + pair, 128)] = (dkv[1] + gvals).astype(BF)

    def long_attend(pair):
        for block in range(2):
            attend(
                256 * block, 256, 0, LONG, pair,
                lambda hh: plong[2 * pair + hh, 256 * block : 256 * block + 256, :],
                block == 0,
            )

    loop(3, long_attend)
    for seg in range(2):
        for pair in range(3):
            row0 = LONG + 128 * seg
            attend(row0, 128, row0, SHORT, pair, lambda hh: pshort[seg, 2 * pair + hh, :, :], True)
    copy_grads = start_copy(grads, grads_any, out_sem.at[2])

    def weights(b):
        gb[b] = tn(xm[...], grads[:, at(b, 256)]).astype(BF)
        release(b)

    loop(6, weights)
    copy_depth.wait()
    copy_grads.wait()
    pltpu.make_async_copy(gb, gb, out_sem.at[0]).wait()


def input_gradient(
    place, llen, slen, vec, grads_any, gdp_any, gone_any, p0, p1, p2, p3, p4, p5, p6, p7,
    il, is_, wm, grads, gdp, rest, sem, sems
):
    arrays = ((gone_any, rest), (gdp_any, gdp), (grads_any, grads))
    loads = [start_copy(a, b, sems.at[k]) for k, (a, b) in enumerate(arrays)]
    fetch_mixer(place, (p0, p1, p2, p3, p4, p5, p6, p7), wm, sem)
    for copy in loads:
        copy.wait()

    def depth(i):
        ps = padded_start(i)
        for c in range(6):
            lanes = slice(128 * c, 128 * c + 128)
            window = gdp[pl.ds(pl.multiple_of(ps - 8, 8), 144), lanes]
            total = rest[at(i, 128), lanes]
            for j in range(TAPS):
                total = total + vec[j : j + 1, lanes] * window[12 - j : 140 - j, :]
            rest[at(i, 128), lanes] = total

    loop(6, depth)
    pltpu.make_async_copy(wm, wm, sem).wait()

    def inputs(i):
        rows = at(i, 256)
        total = rest[rows, :]
        for b in range(6):
            total = total + nt(grads[rows, 256 * b : 256 * b + 256], wm[b])
        return total

    def inputs_long(i):
        live = i * 256 + iota((256, D), 0) < llen[0]
        il[at(i, 256), :] = jnp.where(live, inputs(i), 0.0).astype(BF)

    loop(2, inputs_long)
    total = inputs(2)
    row = iota((128, D), 0)
    for seg in range(2):
        part = total[128 * seg : 128 * seg + 128, :]
        is_[128 * seg : 128 * seg + 128, :] = jnp.where(row < slen[seg], part, 0.0).astype(BF)


def pack(
    place, qkv, depth, point, kernel, convout, g1, b1, inner, outer, out, g2, b2, mixer, ffn
):
    for w in range(SLOTS):

        @pl.when(place[0] == w)
        def _():
            g, r = w // 4, w % 4
            ffn[0:96, :] = inner[g, :, AH * r : AH * r + AH]
            ffn[96:192, :] = outer[g, 96 * r : 96 * r + 96, :]
            ffn[192:240, :] = out[48 * r : 48 * r + 48, AH * g : AH * g + AH]
            if w < 4:
                mixer[...] = qkv[:, 256 * w : 256 * w + 256]
            elif w == 4:
                mixer[:, 0:128] = qkv[:, 1024:1152]
                mixer[:, 128:256] = convout[:, 0:128]
            elif w == 5:
                mixer[...] = convout[:, 128:384]
            elif w == 6:
                mixer[...] = point[:, 0:256]
            else:
                mixer[:, 0:128] = point[:, 256:384]
                rows = [v[...].astype(F32).reshape(1, 192) for v in (g1, b1, g2, b2)]
                table = jnp.concatenate(
                    [depth[...].astype(F32), jnp.zeros((7, 192), F32)]
                    + rows
                    + [jnp.zeros((108, 192), F32)],
                    axis=0,
                )
                left = tn(table.astype(BF), eye(128, BF))
                row, col = iota((54, 128), 0), iota((54, 128), 1)
                right = tn(kernel[...], jnp.where(col == row + 64, 1.0, 0.0).astype(BF))
                mixer[0:96, 128:256] = (left[0:96, :] + right).astype(BF)
                mixer[96:192, 128:256] = left[96:192, :].astype(BF)


def unpack_ffn(place, p0, p1, p2, p3, p4, p5, p6, p7, inner, outer, out):
    for core, pieces in enumerate(((p0, p1, p2, p3), (p4, p5, p6, p7))):
        for chip, piece in enumerate(pieces):
            slot = slot_of(place[0], core, chip)
            g, r = slot >> 2, slot & 3
            inner[g, :, at(r, AH)] = piece[0:96, :].astype(F32)
            outer[g, at(r, 96), :] = piece[96:192, :].astype(F32)
            out[at(r, 48), at(g, AH)] = piece[192:240, :].astype(F32)


def unpack_mixer(
    place, p0, p1, p2, p3, p4, p5, p6, p7,
    qkv, depth, point, kernel, convout, g1, b1, g2, b2, packed,
):
    for core, pieces in enumerate(((p0, p1, p2, p3), (p4, p5, p6, p7))):
        for chip, piece in enumerate(pieces):
            packed[slot_of(place[0], core, chip)] = piece[...]
    for w in range(4):
        qkv[:, 256 * w : 256 * w + 256] = packed[w].astype(F32)
    qkv[:, 1024:1152] = packed[4, :, 0:128].astype(F32)
    convout[:, 0:128] = packed[4, :, 128:256].astype(F32)
    convout[:, 128:384] = packed[5].astype(F32)
    point[:, 0:256] = packed[6].astype(F32)
    point[:, 256:384] = packed[7, :, 0:128].astype(F32)
    misc = packed[7, :, 128:256]
    table = nt(eye(128, BF), misc)
    depth[...] = table[0:TAPS, :]
    for k, ref in enumerate((g1, b1, g2, b2)):
        ref[...] = table[16 + k : 17 + k, :].reshape(192)
    kernel[...] = table[64:118, 0:96]


SMEM = pl.BlockSpec(memory_space=pltpu.SMEM)
VMEM = pl.BlockSpec(memory_space=pltpu.VMEM)
ANY = pl.BlockSpec(memory_space=pl.ANY)


VMEM_MIB = {'unpack_ffn': 12, 'unpack_mixer': 12}


def call(kernel, specs, outs, scratch, flops, *args, out_specs=None):
    return pl.pallas_call(
        kernel,
        out_shape=[jax.ShapeDtypeStruct(s, d) for s, d in outs],
        in_specs=specs,
        out_specs=out_specs or [VMEM] * len(outs),
        scratch_shapes=[pltpu.VMEM(s, d) for s, d in scratch[0]] + list(scratch[1:]),
        compiler_params=pltpu.CompilerParams(vmem_limit_bytes=VMEM_MIB.get(kernel.__name__, 60) << 20),
        cost_estimate=pl.CostEstimate(flops=flops, bytes_accessed=1 << 20, transcendentals=0),
        name=kernel.__name__,
    )(*args)


def forward_mixer(scalars, xl, xs, pieces):
    outs = [
        ((ROWS, D), BF), ((ROWS, 3 * AH), BF),
        ((HEADS, LONG, LONG), BF), ((2, HEADS, SHORT, SHORT), BF),
        ((ROWS, D), BF), ((ROWS, AH), F32), ((ROWS, AH), BF), ((PAD, 128), F32),
        ((PAD, AH), F32), ((ROWS, D), BF), ((24, D), F32),
    ]
    scratch = [((SLOTS, D, 256), BF), ((PAD, D), F32), ((256, AH), BF), ((AH, 128), BF)]
    return call(
        mixer_forward, [SMEM] * 3 + [VMEM] * 2 + [ANY] * 8, outs,
        (scratch + outs[:-1], pltpu.SemaphoreType.DMA, pltpu.SemaphoreType.DMA((10,))), 30 * 10**9,
        *scalars, xl, xs, *pieces, out_specs=[ANY] * 10 + [VMEM],
    )


def feed_forward(scalars, xm, ctx, vec, cl, cs, pieces):
    outs = [
        ((LONG, D), BF), ((2 * SHORT, D), BF), ((4, 4, 240, AH), BF), ((4, 4, 240, AH), BF),
        ((ROWS, D), F32), ((ROWS, D), BF), ((8, D), F32),
    ]
    scratch = [
        ((2, D, AH), BF), ((4, AH, D), BF), ((4, D, AH), BF), ((ROWS, D), BF), ((ROWS, D), BF),
        ((ROWS, D), BF), ((ROWS, D), BF), ((ROWS, D), F32), ((ROWS, D), F32),
        ((2, ROWS, AH), BF), ((2, ROWS, AH), BF), ((4, ROWS, D), BF), ((4, ROWS, D), F32),
        ((2, ROWS, AH), F32), ((ROWS, 128), F32), ((256, D), F32), ((256, D), F32),
        ((ROWS, D), BF), ((ROWS, D), BF), ((ROWS, D), BF), ((2, ROWS, AH), BF),
        ((4, AH, D), BF), ((4, D, AH), BF), ((ROWS, D), F32), ((ROWS, D), BF), ((32, D), F32),
    ]
    return call(
        ffn_both, [SMEM] * 3 + [VMEM] + [ANY] * 12, outs,
        (scratch, pltpu.SemaphoreType.DMA((7,))), 60 * 10**9,
        *scalars, vec, xm, ctx, cl, cs, *pieces, out_specs=[ANY] * 6 + [VMEM],
    )


def backward_mixer(place, vec, gvec, arrays, pieces):
    outs = [((4, 4, 192, 256), BF)] + [((4, 192, 256), BF)] * 4
    outs += [((ROWS, 4 * AH), BF), ((PAD, D), F32)]
    scratch = [((SLOTS, D, 256), BF)] + [(a.shape, a.dtype) for a in arrays] + [
        ((PAD, D), F32), ((PAD, AH), F32), ((PAD, D), F32), ((ROWS, 4 * AH), BF),
        ((ROWS, AH), F32), ((2, LONG, 128), F32), ((ROWS, AH), BF), ((ROWS, 128), BF),
        ((ROWS, 128), F32),
        ((8 * TAPS, D), F32), ((SLOTS, D, 256), BF), ((256, AH), BF), ((AH, 128), BF),
        ((AH, 128), BF),
    ]
    dma = pltpu.SemaphoreType.DMA
    return call(
        mixer_backward, [SMEM] + [VMEM] * 2 + [ANY] * 18, outs,
        (scratch, dma, dma((10,)), dma((3,))), 40 * 10**9,
        place, vec, gvec, *arrays, *pieces, out_specs=[ANY] * 7,
    )


def backward_inputs(scalars, vec, grads, gdp, gone, pieces):
    scratch = [
        ((SLOTS, D, 256), BF), ((ROWS, 4 * AH), BF), ((PAD, D), F32), ((ROWS, D), F32),
    ]
    dma = pltpu.SemaphoreType.DMA
    return call(
        input_gradient, [SMEM] * 3 + [VMEM] + [ANY] * 11, [((LONG, D), BF), ((2 * SHORT, D), BF)],
        (scratch, dma, dma((3,))), 5 * 10**9, *scalars, vec, grads, gdp, gone, *pieces,
    )


def far(values, bit):
    return lax.ppermute(values, "narrow", [(i, i ^ bit) for i in range(4)])


def near(values, bit):
    return lax.ppermute(values, "wide", [(i, i ^ bit) for i in range(SLOTS)])


def gather_narrow(piece):
    return jnp.stack([piece] + [far(piece, k) for k in (1, 2, 3)])


def gather_chips(block):
    return [block] + [near(block, k) for k in (2, 4, 6)]


def gather_cores(blocks):
    return blocks + [near(block, 1) for block in blocks]


def total(first, others):
    result = first.astype(F32)
    for other in others:
        result = result + other.astype(F32)
    return result.astype(BF)


def reduce_cores(keep, sent):
    return [total(keep[k], [sent[k]]) for k in range(4)]


def send_chips(parts):
    return [near(parts[k], 2 * k) for k in (1, 2, 3)]


def reduce_chips(first, others):
    return [total(first[k], [other[k] for other in others]) for k in range(4)]


def send_narrow(parts):
    return [far(parts[k], k) for k in (1, 2, 3)]


def body(
    long_tokens, long_lengths, short_tokens, short_lengths,
    w_qkv, w_depth, w_point, w_kernel, w_convout, w_out, norm1_gain, norm1_bias,
    w_inner, w_outer, norm2_gain, norm2_bias, long_cotangent, short_cotangent,
):
    place = jnp.stack([lax.axis_index("wide"), lax.axis_index("narrow")]).astype(jnp.int32)
    scalars = (place, long_lengths, short_lengths)
    xl, xs = long_tokens.reshape(LONG, D), short_tokens.reshape(2 * SHORT, D)
    cl, cs = long_cotangent.reshape(LONG, D), short_cotangent.reshape(2 * SHORT, D)
    mixer, ffn = call(
        pack, [SMEM] + [VMEM] * 12, [((192, 256), BF), ((240, AH), BF)], ([],), 10**9,
        place, w_qkv, w_depth, w_point, w_kernel.T, w_convout, norm1_gain, norm1_bias,
        w_inner, w_outer, w_out, norm2_gain, norm2_bias,
    )
    mixer = gather_narrow(mixer)
    mixer, ffn = lax.optimization_barrier((mixer, ffn))
    mixer = gather_chips(mixer)
    ffn = gather_narrow(ffn)
    mixer, ffn = lax.optimization_barrier((mixer, ffn))
    mixer = gather_cores(mixer)
    ffn = gather_chips(ffn)
    xm, packed, plong, pshort, dw, kc, cq, kp, cv, ctx, vec = forward_mixer(scalars, xl, xs, mixer)
    ctx, ffn = lax.optimization_barrier((ctx, ffn))
    ffn = gather_cores(ffn)
    ol, os, keep, send, gone, gctx, gvec = feed_forward(scalars, xm, ctx, vec, cl, cs, ffn)
    ga = reduce_cores(keep, near(send, 1))
    ga_sent = send_chips(ga)
    gctx, ga = lax.optimization_barrier((gctx, ga))
    keep, s0, s1, s2, s3, grads, gdp = backward_mixer(
        place, vec, gvec, (xm, packed, plong, pshort, dw, kc, cq, kp, cv, gctx), mixer
    )
    gb = [total(keep[1], [near(s1, 1)]), total(keep[2], [near(s2, 1)])]
    keep, s0, s3, gb, ga_sent = lax.optimization_barrier((keep, s0, s3, gb, ga_sent))
    gb_sent = [near(gb[0], 2), near(gb[1], 4)]
    gb3 = total(keep[3], [near(s3, 1)])
    gb_sent.append(near(gb3, 6))
    gb = [total(keep[0], [near(s0, 1)]), gb[0], gb[1], gb3]
    ga_sent, gb = lax.optimization_barrier((ga_sent, gb))
    ga = reduce_chips(ga[0], ga_sent)
    ga_sent = [far(ga[3], 3), far(ga[2], 2)]
    grads, ga = lax.optimization_barrier((grads, ga))
    il, is_ = backward_inputs(scalars, vec, grads, gdp, gone, mixer)
    last, il = lax.optimization_barrier((ga[1], il))
    ga_sent, gb_sent, il = lax.optimization_barrier((ga_sent, gb_sent, il))
    ga_sent.append(far(last, 1))
    ga = gather_chips(lax.psum(total(ga[0], ga_sent), "hi"))
    gb = reduce_chips(gb[0], gb_sent)
    gb = gather_chips(lax.psum(total(gb[0], send_narrow(gb)), "hi"))
    inner, outer, out = call(
        unpack_ffn, [SMEM] + [VMEM] * 8,
        [((2, 96, 4 * AH), F32), ((2, AH, AH), F32), ((192, D), F32)],
        ([],), 10**9, place, *gather_cores(ga),
    )
    gb, inner = lax.optimization_barrier((gb, inner))
    outs = [
        ((192, 3 * AH), F32), ((TAPS, 192), F32), ((192, AH), F32), ((54, 96), F32), ((192, AH), F32),
    ] + [((192,), F32)] * 4
    qkv, depth, point, kernel, convout, g1, b1, g2, b2 = call(
        unpack_mixer, [SMEM] + [VMEM] * 8, outs, ([((SLOTS, 192, 256), BF)],), 10**9,
        place, *gather_cores(gb),
    )
    return (
        ol.reshape(long_tokens.shape), os.reshape(short_tokens.shape),
        il.reshape(long_tokens.shape), is_.reshape(short_tokens.shape),
        qkv, depth, point, kernel.T, convout, out, g1, b1, inner, outer, g2, b2,
    )


def solution(mesh):
    wide, narrow = mesh.shape["wide"], mesh.shape["narrow"]
    inner_mesh = Mesh(mesh.devices.reshape(wide // SLOTS, SLOTS, narrow), ("hi", "wide", "narrow"))
    every = ("hi", "wide", "narrow")
    rows = P(every, None, None)
    weights = (
        P("narrow", None), P(None, "narrow"), P("narrow", None), P("narrow", None),
        P("narrow", None), P("narrow", None), P("narrow"), P("narrow"),
        P(None, "narrow", None), P(None, "narrow", None), P("narrow"), P("narrow"),
    )
    return jax.shard_map(
        body,
        mesh=inner_mesh,
        in_specs=(rows, P(every), rows, P(every)) + weights + (rows, rows),
        out_specs=(rows, rows, rows, rows) + weights,
        check_vma=False,
    )
```

```python
import jax
import jax.numpy as jnp
from jax import lax
from jax.experimental import pallas as pl
from jax.experimental.pallas import tpu as pltpu
from jax.sharding import Mesh
from jax.sharding import PartitionSpec as P

BF = jnp.bfloat16
F32 = jnp.float32
EPS = 1e-12
D = 768
AH = 384
HEADS = 6
TAPS = 9
LONG = 512
SHORT = 128
ROWS = 768
PAD = 800
SLOTS = 8
NEG = -1000000000.0
PSTART = tuple(8 + 128 * i + 8 * max(i - 3, 0) for i in range(6))
SEGS = ((0, 512, 8), (512, 128, 528), (640, 128, 664))


def nn(a, b):
    return lax.dot_general(a, b, (((1,), (0,)), ((), ())), preferred_element_type=F32)


def nt(a, b):
    return lax.dot_general(a, b, (((1,), (1,)), ((), ())), preferred_element_type=F32)


def tn(a, b):
    return lax.dot_general(a, b, (((0,), (0,)), ((), ())), preferred_element_type=F32)


def iota(shape, axis):
    return lax.broadcasted_iota(jnp.int32, shape, axis)


def loop(count, body):
    def step(i, carry):
        body(i)
        return carry

    lax.fori_loop(0, count, step, 0)


def at(i, size):
    if isinstance(i, int):
        return pl.ds(i * size, size)
    return pl.ds(pl.multiple_of(i * size, size), size)


def padded_start(i):
    return pl.multiple_of(8 + 128 * i + 8 * jnp.maximum(i - 3, 0), 8)


def zero_gaps(ref):
    for start in (0, 520, 656, 792):
        ref[start : start + 8, :] = jnp.zeros((8, ref.shape[1]), ref.dtype)


def eye(n, dtype):
    return jnp.where(iota((n, n), 0) == iota((n, n), 1), 1.0, 0.0).astype(dtype)


def tap_permutation():
    row, col = iota((128, 128), 0), iota((128, 128), 1)
    head, tap = col & 7, col >> 3
    keep = (head < HEADS) & (tap < TAPS) & (row == 64 + head * TAPS + tap)
    return jnp.where(keep, 1.0, 0.0).astype(BF)


def head_spread():
    row, col = iota((256, AH), 0), iota((256, AH), 1)
    return jnp.where((row & 127) == (col >> 6), 1.0, 0.0).astype(BF)


def head_gather():
    row, col = iota((AH, 128), 0), iota((AH, 128), 1)
    return jnp.where((row >> 6) == col, 1.0, 0.0).astype(BF)


def split_two(values):
    high = values.astype(BF)
    low = (values - high.astype(F32)).astype(BF)
    return jnp.concatenate([high, low], axis=1)


def spread_taps(probs):
    moved = [probs] + [pltpu.roll(probs, 128 - 8 * j, 1) for j in range(1, TAPS)]
    return split_two(jnp.concatenate(moved, axis=0))


def tap_kernel(wm):
    stored = jnp.concatenate([wm[7, 192 * n : 192 * n + 96, 128:256] for n in range(4)], axis=0)
    return nn(stored, tap_permutation()).astype(BF)


def slot_of(where, core, chip):
    return 2 * ((where >> 1) ^ chip) + ((where & 1) ^ core)


def fetch_mixer(place, pieces, wm, sem):
    for at_core in range(2):
        for chip in range(4):
            piece = pieces[4 * at_core + chip]
            slot = slot_of(place[0], at_core, chip)

            def fetch(k):
                pltpu.make_async_copy(piece.at[k], wm.at[slot, at(place[1] ^ k, 192), :], sem).start()

            loop(4, fetch)


def mixer_forward(
    place, llen, slen, xl, xs, p0, p1, p2, p3, p4, p5, p6, p7,
    xm_any, packed_any, plong_any, pshort_any, dw_any, kc_any, cq_any, kp_any, cv_any, ctx_any, vec,
    wm, xpad, spread, wk, xm, packed, plong, pshort, dw, kc, cq, kp, cv, ctx, sem, sems
):
    fetch_mixer(place, (p0, p1, p2, p3, p4, p5, p6, p7), wm, sem)
    lens = (llen[0], slen[0], slen[1])
    zero_gaps(xpad)
    zero_gaps(cv)
    zero_gaps(kp)
    for i in range(6):
        seg = max(i - 3, 0)
        base = 128 * i if i < 4 else 0
        tokens = xl[128 * i : 128 * i + 128, :] if i < 4 else xs[128 * (i - 4) : 128 * (i - 3), :]
        live = base + iota((128, D), 0) < lens[seg]
        values = jnp.where(live, tokens.astype(F32), 0.0)
        xpad[PSTART[i] : PSTART[i] + 128, :] = values
        xm[128 * i : 128 * i + 128, :] = values.astype(BF)
    stores = [start_copy(xm, xm_any, sems.at[0])]
    spread[...] = head_spread()
    pltpu.make_async_copy(wm, wm, sem).wait()
    vec[...] = nt(eye(128, BF), wm[7, :, 128:256])[0:24, :]
    wk[...] = tap_kernel(wm)

    def depth(i):
        ps = padded_start(i)
        for c in range(6):
            lanes = slice(128 * c, 128 * c + 128)
            window = xpad[pl.ds(pl.multiple_of(ps - 8, 8), 144), lanes]
            total = jnp.zeros((128, 128), F32)
            for j in range(TAPS):
                total = total + vec[j : j + 1, lanes] * window[4 + j : 132 + j, :]
            dw[at(i, 128), lanes] = total.astype(BF)

    def project(b):
        packed[:, at(b, 256)] = nn(xm[...], wm[b]).astype(BF)
        depth(b)

    loop(4, project)
    depth(jnp.int32(4))
    part = nn(xm[...], wm[4])
    packed[:, 1024:1152] = part[:, 0:128].astype(BF)
    for start, rows, pstart in SEGS:
        cv[pstart : pstart + rows, 0:128] = part[start : start + rows, 128:256]
    depth(jnp.int32(5))
    part = nn(xm[...], wm[5])
    for start, rows, pstart in SEGS:
        cv[pstart : pstart + rows, 128:384] = part[start : start + rows, :]
    stores += [
        start_copy(packed, packed_any, sems.at[1]), start_copy(dw, dw_any, sems.at[2]),
        start_copy(cv, cv_any, sems.at[3]),
    ]
    kc[:, 0:256] = nn(dw[...], wm[6])
    kc[:, 256:384] = nn(dw[...], wm[7, :, 0:128])
    stores.append(start_copy(kc, kc_any, sems.at[4]))

    def tap_softmax(i):
        rows = at(i, 384)
        query = (kc[rows, :] * packed[rows, 0:AH].astype(F32)).astype(BF)
        cq[rows, :] = query
        logits = nn(query, wk[...])
        real = iota((384, 128), 1) < 8 * TAPS
        top = jnp.where(real, logits, NEG * 1e20)
        for shift in (64, 32, 16, 8):
            top = jnp.maximum(top, pltpu.roll(top, shift, 1))
        ex = jnp.where(real, jnp.exp(logits - top), 0.0)
        total = ex
        for shift in (64, 32, 16, 8):
            total = total + pltpu.roll(total, shift, 1)
        probs = ex * (1.0 / total)
        for k in range(3):
            kp[pl.ds(padded_start(3 * i + k), 128), :] = probs[128 * k : 128 * k + 128, :]

    loop(2, tap_softmax)

    def dynamic(u):
        for i in (2 * u, 2 * u + 1):
            ps = padded_start(i)
            weights = nn(spread_taps(kp[pl.ds(ps, 128), :]), spread[...])
            for c in range(3):
                lanes = slice(128 * c, 128 * c + 128)
                window = cv[pl.ds(pl.multiple_of(ps - 8, 8), 144), lanes]
                out = jnp.zeros((128, 128), F32)
                for j in range(TAPS):
                    out = out + weights[128 * j : 128 * j + 128, lanes] * window[4 + j : 132 + j, :]
                ctx[at(i, 128), AH + 128 * c : AH + 128 * c + 128] = out.astype(BF)

    loop(3, dynamic)
    stores += [start_copy(cq, cq_any, sems.at[5]), start_copy(kp, kp_any, sems.at[6])]

    def attend(row0, nq, key0, nk, limit, pair, store):
        queries = packed[pl.ds(row0, nq), at(pair, 128)].astype(F32) * 0.125
        keys = packed[pl.ds(key0, nk), at(3 + pair, 128)].astype(F32)
        vals = packed[pl.ds(key0, nk), at(6 + pair, 128)]
        lane, key_lane = iota((nq, 128), 1), iota((nk, 128), 1)
        bias = jnp.where(iota((nk, 128), 0) < limit, 0.0, NEG)
        outs = []
        for hh in range(2):
            spare = 64 * (1 - hh)
            query = jnp.where((lane >> 6) == hh, queries, jnp.where(lane == spare, 1.0, 0.0))
            scores = nt(query.astype(BF), jnp.where(key_lane == spare, bias, keys).astype(BF))
            parts = []
            for r in range(0, nq, 32):
                part = scores[r : r + 32, :]
                part = jnp.exp(part - jnp.max(part, axis=1, keepdims=True))
                part = part * (1.0 / jnp.sum(part, axis=1, keepdims=True))
                parts.append(part.astype(BF))
            probs = jnp.concatenate(parts, axis=0)
            store(hh, probs)
            outs.append(nn(probs, vals))
        both = jnp.where(lane < 64, outs[0], outs[1])
        ctx[pl.ds(row0, nq), at(pair, 128)] = both.astype(BF)

    def long_attend(i):
        pair, block = i >> 1, i & 1
        row0 = pl.multiple_of(block * 256, 256)

        def store(hh, probs):
            plong[2 * pair + hh, pl.ds(row0, 256), :] = probs

        attend(row0, 256, 0, LONG, lens[0], pair, store)

    loop(6, long_attend)
    stores.append(start_copy(plong, plong_any, sems.at[7]))
    for seg in range(2):
        for pair in range(3):

            def store(hh, probs):
                pshort[seg, 2 * pair + hh, :, :] = probs

            row0 = LONG + 128 * seg
            attend(row0, 128, row0, SHORT, lens[1 + seg], pair, store)
    stores += [start_copy(pshort, pshort_any, sems.at[8]), start_copy(ctx, ctx_any, sems.at[9])]
    for copy in stores:
        copy.wait()


def gelu_parts(hidden):
    cdf = 0.5 + 0.5 * lax.erf(hidden * 0.7071067811865476)
    return cdf, jnp.exp(hidden * hidden * -0.5) * 0.3989422804014327


def fold(values):
    return jnp.sum(values.reshape(values.shape[0] // 8, 8, values.shape[1]), axis=0)


def start_copy(source, target, sem):
    copy = pltpu.make_async_copy(source, target, sem)
    copy.start()
    return copy


def ship(keep, sends, place, slot, shard, rows, source, sem):
    where = slot ^ place[0]
    chip, far_off = where >> 1, shard ^ place[1]

    @pl.when((where & 1) == 0)
    def _():
        pltpu.make_async_copy(source, keep.at[chip, far_off, rows, :], sem).start()

    for k, send in enumerate(sends):

        @pl.when(where == 2 * k + 1)
        def _():
            pltpu.make_async_copy(source, send.at[far_off, rows, :], sem).start()


def ffn_both(
    place, llen, slen, vec, xm_any, ctx_any, cl, cs, p0, p1, p2, p3, p4, p5, p6, p7,
    ol, os, keep, send0, send1, send2, send3, gone_any, gctx_any, gvec,
    wo, wi, wu, xm, ctx, cot, out, res, xhat, grouped, gffn, active, slope, ffn, rstd,
    hid_a, hid_b, ghid_a, ghid_b, gproj, gout, ginner, gouter, gone, gctx, sums, sems,
):
    sends = (send0, send1, send2, send3)
    loads = [start_copy(ctx_any, ctx, sems.at[3]), start_copy(xm_any, xm, sems.at[4])]

    def fetch(part):
        for core, pieces in enumerate(((p0, p1, p2, p3), (p4, p5, p6, p7))):
            for chip, piece in enumerate(pieces):
                slot = slot_of(place[0], core, chip)
                g, r = slot >> 2, slot & 3

                def one(k):
                    n = place[1] ^ k
                    if part == 0:
                        rows = pl.ds(pl.multiple_of(192 * n + 48 * r, 48), 48)
                        source, target = pl.ds(192, 48), wo.at[g, rows, :]
                    elif part == 1:
                        source, target = pl.ds(0, 96), wi.at[slot >> 1, at(n, 96), at(slot & 1, AH)]
                    else:
                        rows = at(4 * (n & 1) + r, 96)
                        source, target = pl.ds(96, 96), wu.at[2 * g + (n >> 1), rows, :]
                    pltpu.make_async_copy(piece.at[k, source, :], target, sems.at[part]).start()

                loop(4, one)

    fetch(0)
    gain_one, bias_one = vec[16:17, :], vec[17:18, :]
    gain_two, bias_two = vec[18:19, :], vec[19:20, :]
    sums[...] = jnp.zeros((32, D), F32)
    ffn[...] = jnp.zeros((2, ROWS, AH), F32)
    for copy in loads:
        copy.wait()
    pltpu.make_async_copy(wo, wo, sems.at[0]).wait()
    fetch(1)
    fetch(2)
    cots = [
        start_copy(cl, cot.at[0:LONG], sems.at[5]), start_copy(cs, cot.at[LONG:ROWS], sems.at[6])
    ]

    def mix(i):
        rows = at(i, 256)
        for c in range(2):
            lanes = slice(AH * c, AH * c + AH)
            res[rows, lanes] = nn(ctx[rows, :], wo[c]) + xm[rows, lanes].astype(F32)

    def several(i):
        return [at(4 * i + k, 32) for k in range(4)]

    def norm_one(i):
        spots = several(i)
        done = []
        for values in [res[rows, :] for rows in spots]:
            center = values - jnp.mean(values, axis=1, keepdims=True)
            scale = lax.rsqrt(jnp.mean(center * center, axis=1, keepdims=True) + EPS)
            hat = center * scale
            done.append((hat, scale, hat * gain_one + bias_one))
        for rows, (hat, scale, first) in zip(spots, done):
            xhat[rows, :] = hat
            rstd[rows, :] = jnp.broadcast_to(scale, (32, 128))
            res[rows, :] = first
            short = first.astype(BF)
            grouped[0, rows, :] = short[:, 0:AH]
            grouped[1, rows, :] = short[:, AH:D]

    loop(3, mix)
    loop(6, norm_one)
    pltpu.make_async_copy(wi, wi, sems.at[1]).wait()
    pltpu.make_async_copy(wu, wu, sems.at[2]).wait()

    def hidden(t, target):
        b = lax.div(t, 3)
        target[...] = nn(grouped[b >> 1, at(t - 3 * b, 256), :], wi[b])

    def outward(t):
        b = lax.div(t, 3)
        rows = at(t - 3 * b, 256)
        ffn[b >> 1, rows, :] += nn(active[b, rows, :], wu[b])

    def act(t, source):
        b = lax.div(t, 3)
        m = t - 3 * b
        for part in range(16):
            values = source[16 * part : 16 * part + 16, :]
            rows = pl.ds(pl.multiple_of(m * 256 + 16 * part, 16), 16)
            cdf, density = gelu_parts(values)
            active[b, rows, :] = (values * cdf).astype(BF)
            slope[b, rows, :] = cdf + values * density

    def pair(u, first=False):
        t = 2 * u
        if not first:
            outward(t - 1)
        hidden(t + 1, hid_b)
        act(t, hid_a)
        outward(t)
        hidden(jnp.minimum(t + 2, 11), hid_a)
        act(t + 1, hid_b)

    hidden(jnp.int32(0), hid_a)
    pair(jnp.int32(0), True)
    loop(5, lambda u: pair(u + 1))
    outward(jnp.int32(11))
    for copy in cots:
        copy.wait()

    def norm_two(i):
        limit = jnp.where(i < 4, llen[0], slen[jnp.clip(i - 4, 0, 1)])
        base = jnp.where(i < 4, 128 * i, 0)
        spots = several(i)
        loaded = [
            (
                jnp.concatenate([ffn[0, rows, :], ffn[1, rows, :]], axis=1) + res[rows, :],
                cot[rows, :].astype(F32),
            )
            for rows in spots
        ]
        done = []
        for k, (values, up) in enumerate(loaded):
            center = values - jnp.mean(values, axis=1, keepdims=True)
            scale = lax.rsqrt(jnp.mean(center * center, axis=1, keepdims=True) + EPS)
            hat = center * scale
            result = (hat * gain_two + bias_two).astype(BF)
            live = base + 32 * k + iota((32, D), 0) < limit
            up = jnp.where(live, up, 0.0)
            gain_part, bias_part = fold(up * hat), fold(up)
            up = up * gain_two
            grad = scale * (
                up
                - jnp.mean(up, axis=1, keepdims=True)
                - hat * jnp.mean(up * hat, axis=1, keepdims=True)
            )
            done.append((result, gain_part, bias_part, grad))
        for rows, (result, _, _, grad) in zip(spots, done):
            out[rows, :] = result
            res[rows, :] = grad
            short = grad.astype(BF)
            gffn[0, rows, :] = short[:, 0:AH]
            gffn[1, rows, :] = short[:, AH:D]
        sums[16:24, :] += done[0][1] + done[1][1] + done[2][1] + done[3][1]
        sums[24:32, :] += done[0][2] + done[1][2] + done[2][2] + done[3][2]

    loop(6, norm_two)
    stores = [
        start_copy(out.at[0:LONG], ol, sems.at[3]), start_copy(out.at[LONG:ROWS], os, sems.at[4])
    ]
    ffn[...] = jnp.zeros((2, ROWS, AH), F32)

    def slopes(b, target):
        for part in range(6):
            rows = slice(128 * part, 128 * part + 128)
            back = nt(gffn[b >> 1, rows, :], wu[b])
            target[rows, :] = (back * slope[b, rows, :]).astype(BF)

    def gradients(b, source):
        g = b >> 1
        gouter[b] = tn(active[b], gffn[g]).astype(BF)
        ginner[b] = tn(grouped[g], source[...]).astype(BF)
        ffn[g] += nt(source[...], wi[b])
        for half in range(2):
            n = 2 * (b & 1) + half
            for w in range(4):
                outer = gouter.at[b, pl.ds(AH * half + 96 * w, 96), :]
                ship(keep, sends, place, 4 * g + w, n, pl.ds(96, 96), outer, sems.at[0])
                inner = ginner.at[b, pl.ds(96 * w, 96), pl.ds(AH * half, AH)]
                ship(keep, sends, place, 2 * b + half, w, pl.ds(0, 96), inner, sems.at[1])

    slopes(jnp.int32(0), ghid_a)

    def contract(u):
        b = 2 * u
        slopes(b + 1, ghid_b)
        gradients(b, ghid_a)
        slopes(jnp.minimum(b + 2, 3), ghid_a)
        gradients(b + 1, ghid_b)

    loop(2, contract)

    def norm_one_back(i):
        spots = several(i)
        loaded = [
            (
                res[rows, :] + jnp.concatenate([ffn[0, rows, :], ffn[1, rows, :]], axis=1),
                xhat[rows, :], rstd[rows, 0:1],
            )
            for rows in spots
        ]
        done = []
        for up, hat, scale in loaded:
            gain_part, bias_part = fold(up * hat), fold(up)
            up = up * gain_one
            grad = scale * (
                up
                - jnp.mean(up, axis=1, keepdims=True)
                - hat * jnp.mean(up * hat, axis=1, keepdims=True)
            )
            done.append((gain_part, bias_part, grad))
        for rows, (_, _, grad) in zip(spots, done):
            gone[rows, :] = grad
            gproj[rows, :] = grad.astype(BF)
        sums[0:8, :] += done[0][0] + done[1][0] + done[2][0] + done[3][0]
        sums[8:16, :] += done[0][1] + done[1][1] + done[2][1] + done[3][1]

    def unmix(i):
        rows = at(i, 256)
        part = nt(gproj[rows, 0:AH], wo[0]) + nt(gproj[rows, AH:D], wo[1])
        gctx[rows, :] = part.astype(BF)

    loop(6, norm_one_back)
    loop(2, unmix)
    stores.append(start_copy(gone, gone_any, sems.at[5]))
    for c in range(2):
        gout[c] = tn(ctx[...], gproj[:, AH * c : AH * c + AH]).astype(BF)
        for n in range(4):
            for r in range(4):
                source = gout.at[c, pl.ds(192 * n + 48 * r, 48), :]
                ship(keep, sends, place, 4 * c + r, n, pl.ds(192, 48), source, sems.at[2])
    unmix(2)
    for k in range(4):
        gvec[k : k + 1, :] = jnp.sum(sums[8 * k : 8 * k + 8, :], axis=0, keepdims=True)
    gvec[4:8, :] = jnp.zeros((4, D), F32)
    stores.append(start_copy(gctx, gctx_any, sems.at[6]))
    for copy in stores:
        copy.wait()
    pltpu.make_async_copy(gouter, gouter, sems.at[0]).wait()
    pltpu.make_async_copy(ginner, ginner, sems.at[1]).wait()
    pltpu.make_async_copy(gout, gout, sems.at[2]).wait()


def mixer_backward(
    place, vec, gvec, xm_any, packed_any, plong_any, pshort_any, dw_any, kc_any, cq_any, kp_any,
    cv_any, gctx_any, p0, p1, p2, p3, p4, p5, p6, p7,
    keep, send0, send1, send2, send3, grads_any, gdep_any,
    wm, xm, packed, plong, pshort, dw, kc, cq, kp, cv, gctx,
    xpad, gcp, gdp, grads, gqc, dkv, gkc, glog, gprob, gdep, gb, spread, gather, wk, sem, sems,
    out_sem,
):
    arrays = (
        (gctx_any, gctx), (kp_any, kp), (cv_any, cv), (packed_any, packed), (kc_any, kc),
        (xm_any, xm), (plong_any, plong), (pshort_any, pshort), (dw_any, dw), (cq_any, cq),
    )
    def begin(first, last):
        return [start_copy(*arrays[k], sems.at[k]) for k in range(first, last)]

    loads = begin(0, 3)
    zero_gaps(xpad)
    zero_gaps(gcp)
    zero_gaps(gdp)
    spread[...] = head_spread()
    gather[...] = head_gather()
    gdep[...] = jnp.zeros((8 * TAPS, D), F32)
    for copy in loads:
        copy.wait()
    loads = begin(3, 6)
    fetch_mixer(place, (p0, p1, p2, p3, p4, p5, p6, p7), wm, sem)
    late = begin(6, 10)
    for start, rows, pstart in SEGS:
        gcp[pstart : pstart + rows, :] = gctx[start : start + rows, AH:D].astype(F32)

    def dynamic(i):
        rows = at(i, 128)
        ps = padded_start(i)
        wide = pl.ds(pl.multiple_of(ps - 8, 8), 144)
        weights = nn(spread_taps(kp[wide, :]), spread[...])
        columns = []
        for c in range(3):
            lanes = slice(128 * c, 128 * c + 128)
            grad_wide = gcp[wide, lanes]
            values = cv[wide, lanes]
            grad = gcp[pl.ds(ps, 128), lanes]
            total = jnp.zeros((128, 128), F32)
            parts = []
            for j in range(TAPS):
                part = weights[144 * j : 144 * j + 144, lanes] * grad_wide
                total = total + part[12 - j : 140 - j, :]
                parts.append((grad * values[4 + j : 132 + j, :]).astype(BF))
            grads[rows, 3 * AH + 128 * c : 3 * AH + 128 * c + 128] = total.astype(BF)
            columns.append(jnp.concatenate(parts, axis=0))
        sums = nn(jnp.concatenate(columns, axis=1), gather[...])
        total = sums[0:128, :]
        for j in range(1, TAPS):
            total = total + pltpu.roll(sums[128 * j : 128 * j + 128, :], 8 * j, 1)
        gprob[rows, :] = total

    loop(6, dynamic)
    for copy in loads:
        copy.wait()
    pltpu.make_async_copy(wm, wm, sem).wait()
    wk[...] = tap_kernel(wm)

    def tap_softmax_back(i):
        rows = at(i, 384)
        probs = jnp.concatenate([kp[pl.ds(padded_start(3 * i + k), 128), :] for k in range(3)], axis=0)
        upper = gprob[rows, :]
        inner = probs * upper
        for shift in (64, 32, 16, 8):
            inner = inner + pltpu.roll(inner, shift, 1)
        glogits = (probs * (upper - inner)).astype(BF)
        glog[rows, :] = glogits
        gquery = nt(glogits, wk[...])
        gkc[rows, :] = (gquery * packed[rows, 0:AH].astype(F32)).astype(BF)
        gqc[rows, :] = gquery * kc[rows, :]

    loop(2, tap_softmax_back)
    for start, rows, pstart in SEGS:
        xpad[pstart : pstart + rows, :] = xm[start : start + rows, :].astype(F32)

    def point_back(c):
        part = nt(gkc[:, 0:256], wm[6, at(c, 256), :])
        part = part + nt(gkc[:, 256:384], wm[7, at(c, 256), 0:128])
        part = part.astype(BF).astype(F32)
        for start, rows, pstart in SEGS:
            gdp[pstart : pstart + rows, at(c, 256)] = part[start : start + rows, :]

    loop(3, point_back)
    copy_depth = start_copy(gdp, gdep_any, out_sem.at[1])

    def release(b):
        for n in range(4):
            where = b ^ place[0]
            chip, far_off = where >> 1, n ^ place[1]
            source = gb.at[b, pl.ds(192 * n, 192), :]

            @pl.when((where & 1) == 0)
            def _():
                pltpu.make_async_copy(source, keep.at[chip, far_off], out_sem.at[0]).start()

            for k, send in enumerate((send0, send1, send2, send3)):

                @pl.when(where == 2 * k + 1)
                def _():
                    pltpu.make_async_copy(source, send.at[far_off], out_sem.at[0]).start()

    def depth(i):
        ps = padded_start(i)
        wide = pl.ds(pl.multiple_of(ps - 8, 8), 144)
        for c in range(6):
            lanes = slice(128 * c, 128 * c + 128)
            tokens = xpad[pl.ds(ps, 128), lanes]
            grad_wide = gdp[wide, lanes]
            for j in range(TAPS):
                gdep[8 * j : 8 * j + 8, lanes] += fold(tokens * grad_wide[12 - j : 140 - j, :])

    loop(6, depth)
    for copy in late:
        copy.wait()
    gb[6] = tn(dw[...], gkc[:, 0:256]).astype(BF)
    gb[7, :, 0:128] = tn(dw[...], gkc[:, 256:384]).astype(BF)
    taps = [jnp.sum(gdep[8 * j : 8 * j + 8, :], axis=0, keepdims=True) for j in range(TAPS)]
    table = jnp.concatenate(
        taps + [jnp.zeros((7, D), F32), gvec[...], jnp.zeros((104, D), F32)], axis=0
    ).astype(BF)
    misc = tn(table, eye(128, BF))
    gkernel = nt(tn(cq[...], glog[...]).astype(BF), tap_permutation())
    for n in range(4):
        row = 192 * n
        part = misc[row : row + 96, :] + gkernel[96 * n : 96 * n + 96, :]
        gb[7, row : row + 96, 128:256] = part.astype(BF)
        gb[7, row + 96 : row + 192, 128:256] = misc[row + 96 : row + 192, :].astype(BF)
    release(6)
    release(7)

    def attend(row0, nq, key0, nk, pair, load, first):
        queries = packed[pl.ds(row0, nq), at(pair, 128)].astype(F32) * 0.125
        keys = packed[pl.ds(key0, nk), at(3 + pair, 128)]
        vals = packed[pl.ds(key0, nk), at(6 + pair, 128)]
        up = gctx[pl.ds(row0, nq), at(pair, 128)].astype(F32)
        lane = iota((nq, 128), 1)
        outs = []
        gkeys = jnp.zeros((nk, 128), F32)
        gvals = jnp.zeros((nk, 128), F32)
        for hh in range(2):
            mine = (lane >> 6) == hh
            query = jnp.where(mine, queries, 0.0).astype(BF)
            upper = jnp.where(mine, up, 0.0).astype(BF)
            probs_low = load(hh)
            gprobs = nt(upper, vals)
            parts = []
            for r in range(0, nq, 32):
                probs, part = probs_low[r : r + 32, :].astype(F32), gprobs[r : r + 32, :]
                inner = jnp.sum(probs * part, axis=1, keepdims=True)
                parts.append((probs * (part - inner)).astype(BF))
            gscores = jnp.concatenate(parts, axis=0)
            outs.append(nn(gscores, keys))
            gkeys = gkeys + tn(gscores, query)
            gvals = gvals + tn(probs_low, upper)
        both = jnp.where(lane < 64, outs[0], outs[1]) * 0.125
        both = both + gqc[pl.ds(row0, nq), at(pair, 128)]
        grads[pl.ds(row0, nq), at(pair, 128)] = both.astype(BF)
        span = pl.ds(key0, nk)
        if nq == nk:
            grads[span, at(3 + pair, 128)] = gkeys.astype(BF)
            grads[span, at(6 + pair, 128)] = gvals.astype(BF)
        elif first:
            dkv[0] = gkeys
            dkv[1] = gvals
        else:
            grads[span, at(3 + pair, 128)] = (dkv[0] + gkeys).astype(BF)
            grads[span, at(6 + pair, 128)] = (dkv[1] + gvals).astype(BF)

    def long_attend(pair):
        for block in range(2):
            attend(
                256 * block, 256, 0, LONG, pair,
                lambda hh: plong[2 * pair + hh, 256 * block : 256 * block + 256, :],
                block == 0,
            )

    loop(3, long_attend)
    for seg in range(2):
        for pair in range(3):
            row0 = LONG + 128 * seg
            attend(row0, 128, row0, SHORT, pair, lambda hh: pshort[seg, 2 * pair + hh, :, :], True)
    copy_grads = start_copy(grads, grads_any, out_sem.at[2])

    def weights(b):
        gb[b] = tn(xm[...], grads[:, at(b, 256)]).astype(BF)
        release(b)

    loop(6, weights)
    copy_depth.wait()
    copy_grads.wait()
    pltpu.make_async_copy(gb, gb, out_sem.at[0]).wait()


def input_gradient(
    place, llen, slen, vec, grads_any, gdp_any, gone_any, p0, p1, p2, p3, p4, p5, p6, p7,
    il, is_, wm, grads, gdp, rest, sem, sems
):
    arrays = ((gone_any, rest), (gdp_any, gdp), (grads_any, grads))
    loads = [start_copy(a, b, sems.at[k]) for k, (a, b) in enumerate(arrays)]
    fetch_mixer(place, (p0, p1, p2, p3, p4, p5, p6, p7), wm, sem)
    for copy in loads:
        copy.wait()

    def depth(i):
        ps = padded_start(i)
        for c in range(6):
            lanes = slice(128 * c, 128 * c + 128)
            window = gdp[pl.ds(pl.multiple_of(ps - 8, 8), 144), lanes]
            total = rest[at(i, 128), lanes]
            for j in range(TAPS):
                total = total + vec[j : j + 1, lanes] * window[12 - j : 140 - j, :]
            rest[at(i, 128), lanes] = total

    loop(6, depth)
    pltpu.make_async_copy(wm, wm, sem).wait()

    def inputs(i):
        rows = at(i, 256)
        total = rest[rows, :]
        for b in range(6):
            total = total + nt(grads[rows, 256 * b : 256 * b + 256], wm[b])
        return total

    def inputs_long(i):
        live = i * 256 + iota((256, D), 0) < llen[0]
        il[at(i, 256), :] = jnp.where(live, inputs(i), 0.0).astype(BF)

    loop(2, inputs_long)
    total = inputs(2)
    row = iota((128, D), 0)
    for seg in range(2):
        part = total[128 * seg : 128 * seg + 128, :]
        is_[128 * seg : 128 * seg + 128, :] = jnp.where(row < slen[seg], part, 0.0).astype(BF)


def pack(
    place, qkv, point, convout, inner, outer, out, depth, kernel, g1, b1, g2, b2, mixer, ffn, sems
):
    for w in range(SLOTS):

        @pl.when(place[0] == w)
        def _():
            g, r = w // 4, w % 4
            if w < 4:
                parts = [(qkv.at[:, 256 * w : 256 * w + 256], mixer)]
            elif w == 4:
                parts = [
                    (qkv.at[:, 1024:1152], mixer.at[:, 0:128]),
                    (convout.at[:, 0:128], mixer.at[:, 128:256]),
                ]
            elif w == 5:
                parts = [(convout.at[:, 128:384], mixer)]
            elif w == 6:
                parts = [(point.at[:, 0:256], mixer)]
            else:
                parts = [(point.at[:, 256:384], mixer.at[:, 0:128])]
            parts += [
                (inner.at[g, :, AH * r : AH * r + AH], ffn.at[0:96]),
                (outer.at[g, 96 * r : 96 * r + 96, :], ffn.at[96:192]),
                (out.at[48 * r : 48 * r + 48, AH * g : AH * g + AH], ffn.at[192:240]),
            ]
            copies = [start_copy(a, b, sems.at[k]) for k, (a, b) in enumerate(parts)]
            if w == 7:
                rows = [v[...].astype(F32).reshape(1, 192) for v in (g1, b1, g2, b2)]
                table = jnp.concatenate(
                    [depth[...].astype(F32), jnp.zeros((7, 192), F32)]
                    + rows
                    + [jnp.zeros((108, 192), F32)],
                    axis=0,
                )
                left = tn(table.astype(BF), eye(128, BF))
                row, col = iota((54, 128), 0), iota((54, 128), 1)
                right = tn(kernel[...], jnp.where(col == row + 64, 1.0, 0.0).astype(BF))
                mixer[0:96, 128:256] = (left[0:96, :] + right).astype(BF)
                mixer[96:192, 128:256] = left[96:192, :].astype(BF)
            for copy in copies:
                copy.wait()


def unpack_ffn(place, p0, p1, p2, p3, p4, p5, p6, p7, inner, outer, out):
    for core, pieces in enumerate(((p0, p1, p2, p3), (p4, p5, p6, p7))):
        for chip, piece in enumerate(pieces):
            slot = slot_of(place[0], core, chip)
            g, r = slot >> 2, slot & 3
            inner[g, :, at(r, AH)] = piece[0:96, :].astype(F32)
            outer[g, at(r, 96), :] = piece[96:192, :].astype(F32)
            out[at(r, 48), at(g, AH)] = piece[192:240, :].astype(F32)


def unpack_mixer(
    place, p0, p1, p2, p3, p4, p5, p6, p7,
    qkv, depth, point, kernel, convout, g1, b1, g2, b2, packed,
):
    for core, pieces in enumerate(((p0, p1, p2, p3), (p4, p5, p6, p7))):
        for chip, piece in enumerate(pieces):
            packed[slot_of(place[0], core, chip)] = piece[...]
    for w in range(4):
        qkv[:, 256 * w : 256 * w + 256] = packed[w].astype(F32)
    qkv[:, 1024:1152] = packed[4, :, 0:128].astype(F32)
    convout[:, 0:128] = packed[4, :, 128:256].astype(F32)
    convout[:, 128:384] = packed[5].astype(F32)
    point[:, 0:256] = packed[6].astype(F32)
    point[:, 256:384] = packed[7, :, 0:128].astype(F32)
    misc = packed[7, :, 128:256]
    table = nt(eye(128, BF), misc)
    depth[...] = table[0:TAPS, :]
    for k, ref in enumerate((g1, b1, g2, b2)):
        ref[...] = table[16 + k : 17 + k, :].reshape(192)
    kernel[...] = table[64:118, 0:96]


SMEM = pl.BlockSpec(memory_space=pltpu.SMEM)
VMEM = pl.BlockSpec(memory_space=pltpu.VMEM)
ANY = pl.BlockSpec(memory_space=pl.ANY)


VMEM_MIB = {'unpack_ffn': 12, 'unpack_mixer': 12}


def call(kernel, specs, outs, scratch, flops, *args, out_specs=None):
    return pl.pallas_call(
        kernel,
        out_shape=[jax.ShapeDtypeStruct(s, d) for s, d in outs],
        in_specs=specs,
        out_specs=out_specs or [VMEM] * len(outs),
        scratch_shapes=[pltpu.VMEM(s, d) for s, d in scratch[0]] + list(scratch[1:]),
        compiler_params=pltpu.CompilerParams(vmem_limit_bytes=VMEM_MIB.get(kernel.__name__, 60) << 20),
        cost_estimate=pl.CostEstimate(flops=flops, bytes_accessed=1 << 20, transcendentals=0),
        name=kernel.__name__,
    )(*args)


def forward_mixer(scalars, xl, xs, pieces):
    outs = [
        ((ROWS, D), BF), ((ROWS, 3 * AH), BF),
        ((HEADS, LONG, LONG), BF), ((2, HEADS, SHORT, SHORT), BF),
        ((ROWS, D), BF), ((ROWS, AH), F32), ((ROWS, AH), BF), ((PAD, 128), F32),
        ((PAD, AH), F32), ((ROWS, D), BF), ((24, D), F32),
    ]
    scratch = [((SLOTS, D, 256), BF), ((PAD, D), F32), ((256, AH), BF), ((AH, 128), BF)]
    return call(
        mixer_forward, [SMEM] * 3 + [VMEM] * 2 + [ANY] * 8, outs,
        (scratch + outs[:-1], pltpu.SemaphoreType.DMA, pltpu.SemaphoreType.DMA((10,))), 30 * 10**9,
        *scalars, xl, xs, *pieces, out_specs=[ANY] * 10 + [VMEM],
    )


def feed_forward(scalars, xm, ctx, vec, cl, cs, pieces):
    outs = [
        ((LONG, D), BF), ((2 * SHORT, D), BF), ((4, 4, 240, AH), BF), ((4, 240, AH), BF),
        ((4, 240, AH), BF), ((4, 240, AH), BF), ((4, 240, AH), BF),
        ((ROWS, D), F32), ((ROWS, D), BF), ((8, D), F32),
    ]
    scratch = [
        ((2, D, AH), BF), ((4, AH, D), BF), ((4, D, AH), BF), ((ROWS, D), BF), ((ROWS, D), BF),
        ((ROWS, D), BF), ((ROWS, D), BF), ((ROWS, D), F32), ((ROWS, D), F32),
        ((2, ROWS, AH), BF), ((2, ROWS, AH), BF), ((4, ROWS, D), BF), ((4, ROWS, D), F32),
        ((2, ROWS, AH), F32), ((ROWS, 128), F32), ((256, D), F32), ((256, D), F32),
        ((ROWS, D), BF), ((ROWS, D), BF), ((ROWS, D), BF), ((2, ROWS, AH), BF),
        ((4, AH, D), BF), ((4, D, AH), BF), ((ROWS, D), F32), ((ROWS, D), BF), ((32, D), F32),
    ]
    return call(
        ffn_both, [SMEM] * 3 + [VMEM] + [ANY] * 12, outs,
        (scratch, pltpu.SemaphoreType.DMA((7,))), 60 * 10**9,
        *scalars, vec, xm, ctx, cl, cs, *pieces, out_specs=[ANY] * 9 + [VMEM],
    )


def backward_mixer(place, vec, gvec, arrays, pieces):
    outs = [((4, 4, 192, 256), BF)] + [((4, 192, 256), BF)] * 4
    outs += [((ROWS, 4 * AH), BF), ((PAD, D), F32)]
    scratch = [((SLOTS, D, 256), BF)] + [(a.shape, a.dtype) for a in arrays] + [
        ((PAD, D), F32), ((PAD, AH), F32), ((PAD, D), F32), ((ROWS, 4 * AH), BF),
        ((ROWS, AH), F32), ((2, LONG, 128), F32), ((ROWS, AH), BF), ((ROWS, 128), BF),
        ((ROWS, 128), F32),
        ((8 * TAPS, D), F32), ((SLOTS, D, 256), BF), ((256, AH), BF), ((AH, 128), BF),
        ((AH, 128), BF),
    ]
    dma = pltpu.SemaphoreType.DMA
    return call(
        mixer_backward, [SMEM] + [VMEM] * 2 + [ANY] * 18, outs,
        (scratch, dma, dma((10,)), dma((3,))), 40 * 10**9,
        place, vec, gvec, *arrays, *pieces, out_specs=[ANY] * 7,
    )


def backward_inputs(scalars, vec, grads, gdp, gone, pieces):
    scratch = [
        ((SLOTS, D, 256), BF), ((ROWS, 4 * AH), BF), ((PAD, D), F32), ((ROWS, D), F32),
    ]
    dma = pltpu.SemaphoreType.DMA
    return call(
        input_gradient, [SMEM] * 3 + [VMEM] + [ANY] * 11, [((LONG, D), BF), ((2 * SHORT, D), BF)],
        (scratch, dma, dma((3,))), 5 * 10**9, *scalars, vec, grads, gdp, gone, *pieces,
    )


def far(values, bit):
    return lax.ppermute(values, "narrow", [(i, i ^ bit) for i in range(4)])


def near(values, bit):
    return lax.ppermute(values, "wide", [(i, i ^ bit) for i in range(SLOTS)])


def gather_narrow(piece):
    return jnp.stack([piece] + [far(piece, k) for k in (1, 2, 3)])


def gather_chips(block):
    return [block] + [near(block, k) for k in (2, 4, 6)]


def gather_cores(blocks):
    return blocks + [near(block, 1) for block in blocks]


def total(first, others):
    result = first.astype(F32)
    for other in others:
        result = result + other.astype(F32)
    return result.astype(BF)


def reduce_cores(keep, sent):
    return [total(keep[k], [sent[k]]) for k in range(4)]


def send_chips(parts):
    return [near(parts[k], 2 * k) for k in (1, 2, 3)]


def reduce_chips(first, others):
    return [total(first[k], [other[k] for other in others]) for k in range(4)]


def send_narrow(parts):
    return [far(parts[k], k) for k in (1, 2, 3)]


def body(
    long_tokens, long_lengths, short_tokens, short_lengths,
    w_qkv, w_depth, w_point, w_kernel, w_convout, w_out, norm1_gain, norm1_bias,
    w_inner, w_outer, norm2_gain, norm2_bias, long_cotangent, short_cotangent,
):
    place = jnp.stack([lax.axis_index("wide"), lax.axis_index("narrow")]).astype(jnp.int32)
    scalars = (place, long_lengths, short_lengths)
    xl, xs = long_tokens.reshape(LONG, D), short_tokens.reshape(2 * SHORT, D)
    cl, cs = long_cotangent.reshape(LONG, D), short_cotangent.reshape(2 * SHORT, D)
    mixer, ffn = call(
        pack, [SMEM] + [ANY] * 6 + [VMEM] * 6, [((192, 256), BF), ((240, AH), BF)],
        ([], pltpu.SemaphoreType.DMA((5,))), 10**9,
        place, w_qkv, w_point, w_convout, w_inner, w_outer, w_out,
        w_depth, w_kernel.T, norm1_gain, norm1_bias, norm2_gain, norm2_bias,
    )
    mixer = gather_narrow(mixer)
    mixer, ffn = lax.optimization_barrier((mixer, ffn))
    mixer = gather_chips(mixer)
    ffn = gather_narrow(ffn)
    mixer, ffn = lax.optimization_barrier((mixer, ffn))
    mixer = gather_cores(mixer)
    ffn = gather_chips(ffn)
    xm, packed, plong, pshort, dw, kc, cq, kp, cv, ctx, vec = forward_mixer(scalars, xl, xs, mixer)
    ctx, ffn = lax.optimization_barrier((ctx, ffn))
    ffn = gather_cores(ffn)
    ol, os, keep, s0, s1, s2, s3, gone, gctx, gvec = feed_forward(
        scalars, xm, ctx, vec, cl, cs, ffn
    )
    swapped = [near(s3, 1), near(s1, 1), near(s2, 1), near(s0, 1)]
    ga = [total(keep[3], swapped[0:1]), total(keep[1], swapped[1:2])]
    rest, _ = lax.optimization_barrier((swapped[2:4], ga))
    ga = [total(keep[0], rest[1:2]), ga[1], total(keep[2], rest[0:1]), ga[0]]
    ga_sent = send_chips(ga)
    gctx, ga = lax.optimization_barrier((gctx, ga))
    keep, s0, s1, s2, s3, grads, gdp = backward_mixer(
        place, vec, gvec, (xm, packed, plong, pshort, dw, kc, cq, kp, cv, gctx), mixer
    )
    gb = [total(keep[1], [near(s1, 1)]), total(keep[2], [near(s2, 1)])]
    keep, s0, s3, gb, ga_sent = lax.optimization_barrier((keep, s0, s3, gb, ga_sent))
    gb_sent = [near(gb[0], 2), near(gb[1], 4)]
    gb3 = total(keep[3], [near(s3, 1)])
    gb_sent.append(near(gb3, 6))
    gb = [total(keep[0], [near(s0, 1)]), gb[0], gb[1], gb3]
    ga_sent, gb = lax.optimization_barrier((ga_sent, gb))
    ga = reduce_chips(ga[0], ga_sent)
    ga_sent = [far(ga[1], 1), far(ga[2], 2)]
    grads, ga = lax.optimization_barrier((grads, ga))
    il, is_ = backward_inputs(scalars, vec, grads, gdp, gone, mixer)
    last, il = lax.optimization_barrier((ga[3], il))
    ga_sent, gb_sent, il = lax.optimization_barrier((ga_sent, gb_sent, il))
    ga_sent.append(far(last, 3))
    ga = gather_chips(lax.psum(total(ga[0], ga_sent), "hi"))
    gb = reduce_chips(gb[0], gb_sent)
    gb = gather_chips(lax.psum(total(gb[0], send_narrow(gb)), "hi"))
    inner, outer, out = call(
        unpack_ffn, [SMEM] + [VMEM] * 8,
        [((2, 96, 4 * AH), F32), ((2, AH, AH), F32), ((192, D), F32)],
        ([],), 10**9, place, *gather_cores(ga),
    )
    gb, inner = lax.optimization_barrier((gb, inner))
    outs = [
        ((192, 3 * AH), F32), ((TAPS, 192), F32), ((192, AH), F32), ((54, 96), F32), ((192, AH), F32),
    ] + [((192,), F32)] * 4
    qkv, depth, point, kernel, convout, g1, b1, g2, b2 = call(
        unpack_mixer, [SMEM] + [VMEM] * 8, outs, ([((SLOTS, 192, 256), BF)],), 10**9,
        place, *gather_cores(gb),
    )
    return (
        ol.reshape(long_tokens.shape), os.reshape(short_tokens.shape),
        il.reshape(long_tokens.shape), is_.reshape(short_tokens.shape),
        qkv, depth, point, kernel.T, convout, out, g1, b1, inner, outer, g2, b2,
    )


def solution(mesh):
    wide, narrow = mesh.shape["wide"], mesh.shape["narrow"]
    inner_mesh = Mesh(mesh.devices.reshape(wide // SLOTS, SLOTS, narrow), ("hi", "wide", "narrow"))
    every = ("hi", "wide", "narrow")
    rows = P(every, None, None)
    weights = (
        P("narrow", None), P(None, "narrow"), P("narrow", None), P("narrow", None),
        P("narrow", None), P("narrow", None), P("narrow"), P("narrow"),
        P(None, "narrow", None), P(None, "narrow", None), P("narrow"), P("narrow"),
    )
    return jax.shard_map(
        body,
        mesh=inner_mesh,
        in_specs=(rows, P(every), rows, P(every)) + weights + (rows, rows),
        out_specs=(rows, rows, rows, rows) + weights,
        check_vma=False,
    )
```
